128 devices in a mesh: slab: 16 (over z, y), lat: 8 (over x, core).
Axes of the slice: x: 4, y: 4, z: 4, core: 2. Of those that a mesh axis runs over, the one named last changes fastest.
Arguments:
- residual_blocks: float32 [4096, 2, 64, 128], P(('slab', 'lat')), may hold values from -1.5 to 1.5
- residual_slab: int32 [4096, 1], P(('slab', 'lat')), may hold values from 0 to 15; in each aligned block of 32 rows (0 to 31, 32 to 63, ...) at most 4 rows name the same one
- residual_pos: int32 [4096], P(('slab', 'lat')), may hold values from 0 to 3
- shot_ids: int32 [64], replicated, may hold values from 0 to 63, each once
- wavelet: float32 [64, 2], replicated, may hold values from -4 to 4
- down_panel: float32 [16, 8, 2, 512, 512], P('slab', 'lat'), may hold values from -1 to 1
- up_panel: float32 [16, 8, 2, 512, 512], P('slab', 'lat'), may hold values from -1 to 1
- recovery: float32 [16, 8, 2, 768, 1024], P('slab', 'lat'), may hold values from -0.109375 to 0.109375
- forward_field: float32 [16, 8, 2, 64, 1024], P('slab', 'lat'), may hold values from -3 to 3
- element_owner: int32 [1024, 1], P(('slab', 'lat')), may hold values from 0 to 15; in each aligned block of 8 rows (0 to 7, 8 to 15, ...) at most 2 rows name the same one
- element_slot: int32 [1024], P(('slab', 'lat')), may hold values from 0 to 7
Outputs:
- adjoint_trace: float32 [16, 8, 2, 64, 512], P('slab', 'lat')
- velocity_gradient: float32 [16, 8, 8, 128], P('slab', 'lat')
The draws below stay inside these ranges and needn't reach their ends.
Inputs may be any that keep to these rules, and one draw needn't show every extreme that they name: `residual_slab`: in the 32 rows of one device no slab is named more than 4 times, a bound that some block reaches. `shot_ids`: each shot number appears once. `element_owner`: in the 8 rows of one device no slab is named more than 2 times, a bound that some block reaches.
All inputs are finite; a program needn't handle non-finite values.
Results may differ from the reference program's by a relative error of at most 0.00014.
Values sent between devices are 32-bit elements; how exact they have to be, the bound alone decides.
A program may use at most 128 MiB of HBM per device.

```python
import math
import jax
import jax.numpy as jnp
import numpy as np
from jax import lax

SH = 64
NR = 32
CAP = 4
TR = 512
LB = 128
P_SIZE = 4
RECOV = 768
NEB = 8
NEL = 1024
MBLK = 8
GCAP = 2
SLABS = 16
LATS = 8
RBLOCKS = 4096
EBLOCKS = 1024
N_SLAB = 16


def panel_common(key):
    keys = jax.random.split(key, 3)
    magnitude = jax.random.uniform(keys[0], (SLABS, LATS, TR), jnp.float32, 0.75, 0.9)
    phase = jax.random.uniform(keys[1], (SLABS, LATS, TR), jnp.float32, -math.pi, math.pi)
    noise = jax.random.normal(keys[2], (SLABS, LATS, 2, TR, TR), jnp.float32) * (0.3 / math.sqrt(2.0 * TR))
    noise = jnp.clip(noise, -0.1, 0.1)
    diagonal = jnp.stack([magnitude * jnp.cos(phase), magnitude * jnp.sin(phase)], axis=2)
    identity = jnp.eye(TR, dtype=jnp.float32)
    return noise + identity * diagonal[..., :, None]


def draw_down_panel(key, part):
    return panel_common(jax.random.fold_in(key, 11))


def draw_up_panel(key, part):
    return panel_common(jax.random.fold_in(key, 12))


def touch_ends(result, rng, least, high):
    longest = result.shape.index(max(result.shape))
    spots = []
    for shift in (0, 1):
        where = [jax.random.randint(jax.random.fold_in(rng, axis), (), 0, length) for axis, length in enumerate(result.shape)]
        where[longest] = (where[longest] + shift) % result.shape[longest]
        spots.append(tuple(where))
    return result.at[spots[0]].set(least).at[spots[1]].set(high)


def shard_levels(key, extent, shards, least, high):
    gain, own = 1.0, jax.random.fold_in(key, 6)
    for position, blocks in shards:
        draws = jnp.exp(jax.random.uniform(jax.random.fold_in(own, position), (blocks,), jnp.float32, least / len(shards), high / len(shards)))
        gain = gain * jnp.repeat(draws, extent[position] // blocks).reshape([-1 if axis == position else 1 for axis in range(len(extent))])
    return gain


def routed_block(rng, own, number, rows, count, top, bound, skew):
    ranking = jax.random.permutation(rng, count)
    crowded, common = portions_of(count, rows * top, bound, skew, True), portions_of(count, rows * top, bound, skew, False)
    places = jnp.arange(count)

    def named(sizes, turn):
        used = int((sizes > 0).sum())
        fixed = max(1, used // 4)
        shifted = fixed + (places - fixed + turn * (used - fixed)) % max(1, count - fixed)
        return jnp.zeros((count,), jnp.int32).at[ranking[jnp.where(places < fixed, places, shifted)]].set(jnp.asarray(sizes, jnp.int32))

    sizes = jnp.where(number % 4 == 0, named(crowded, number // 4), named(common, number - number // 4 - 1))
    mixed = jax.random.permutation(jax.random.fold_in(own, 3), count)
    giver, receiver = mixed[0:count // 2 * 2:2], mixed[1:count // 2 * 2:2]
    slack = jnp.minimum(sizes[giver] - 1, bound - sizes[receiver]) // 2
    slack = jnp.where((giver == ranking[0]) | (receiver == ranking[0]) | (sizes[receiver] == 0), 0, jnp.maximum(slack, 0))
    shifted = jax.random.randint(jax.random.fold_in(own, 4), (count // 2,), 0, 1 << 20) % (slack + 1)
    sizes = sizes.at[giver].add(-shifted).at[receiver].add(shifted)
    items = jnp.searchsorted(jnp.cumsum(sizes), jnp.arange(rows * top), side="right").astype(jnp.int32)
    listing = items.reshape(top, rows).T
    listing = listing[jax.random.permutation(jax.random.fold_in(own, 1), rows)]
    turn = jax.random.randint(jax.random.fold_in(own, 2), (rows, 1), 0, top)
    return jnp.take_along_axis(listing, (jnp.arange(top)[None, :] + turn) % top, axis=1)


def portions_of(number_of, total, reach, slope, full):
    portions = [(1 << 20) // math.isqrt(standing ** slope) + 1 for standing in range(1, number_of + 1)]
    largest = reach if full else min(reach, max(-(-total // number_of), total * portions[0] // sum(portions)))
    least = 1 if total - largest >= number_of - 1 else 0
    given, rest = [largest] + [least] * (number_of - 1), total - largest - least * (number_of - 1)
    while rest > 0:
        free = [i for i in range(1, number_of) if given[i] < largest] or [i for i in range(1, number_of) if given[i] < reach]
        mass, left = sum([portions[i] for i in free]), rest
        for i in free:
            addition = min(reach - given[i], max(1, left * portions[i] // mass), rest)
            given[i] = given[i] + addition
            rest = rest - addition
    return np.array(given)


def scatter_about(stream_key, dims, spread, bound, shards=(), kind=jnp.bfloat16):
    array = spread * jax.random.normal(stream_key, dims, jnp.float32)
    if shards:
        array = array * shard_levels(stream_key, dims, shards, -0.22, 0.18)
    return jnp.clip(array, -bound, bound).astype(kind)


def setup_inputs(seed: int = 0) -> dict:
    splits = jax.random.split(jax.random.key(seed), 12)
    residual_blocks = scatter_about(splits[0], (RBLOCKS, 2, SH, LB), 0.25, 1.5, ((0, 128),), jnp.float32)
    residual_slab_keys = jax.random.split(jax.random.fold_in(splits[1], 1), RBLOCKS // NR)
    residual_slab_turns = jax.random.permutation(jax.random.fold_in(splits[1], 3), RBLOCKS // NR)
    residual_slab = jax.vmap(lambda own, number: routed_block(jax.random.fold_in(splits[1], 2), own, number, NR, N_SLAB, 1, CAP, 2))(residual_slab_keys, residual_slab_turns).reshape((RBLOCKS, 1))
    residual_pos = touch_ends(jax.random.randint(splits[2], (RBLOCKS,), 0, P_SIZE), jax.random.fold_in(splits[2], 1), 0, P_SIZE - 1).astype(jnp.int32)
    shot_ids = jax.random.permutation(splits[3], SH).astype(jnp.int32)
    wavelet = scatter_about(splits[4], (SH, 2), 1.0, 4.0, (), jnp.float32)
    down_panel = draw_down_panel(jax.random.fold_in(splits[11], 71), 0)
    up_panel = draw_up_panel(jax.random.fold_in(splits[11], 71), 0)
    recovery = scatter_about(splits[7], (SLABS, LATS, 2, RECOV, NEL), (4 * RECOV) ** -0.5, 0.109375, ((0, 16), (1, 8)), jnp.float32)
    forward_field = scatter_about(splits[8], (SLABS, LATS, 2, SH, NEL), 0.5, 3.0, ((0, 16), (1, 8)), jnp.float32)
    element_owner_keys = jax.random.split(jax.random.fold_in(splits[9], 1), EBLOCKS // NEB)
    element_owner_turns = jax.random.permutation(jax.random.fold_in(splits[9], 3), EBLOCKS // NEB)
    element_owner = jax.vmap(lambda own, number: routed_block(jax.random.fold_in(splits[9], 2), own, number, NEB, N_SLAB, 1, GCAP, 2))(element_owner_keys, element_owner_turns).reshape((EBLOCKS, 1))
    element_slot = touch_ends(jax.random.randint(splits[10], (EBLOCKS,), 0, MBLK), jax.random.fold_in(splits[10], 1), 0, MBLK - 1).astype(jnp.int32)
    return {"residual_blocks": residual_blocks, "residual_slab": residual_slab, "residual_pos": residual_pos, "shot_ids": shot_ids, "wavelet": wavelet, "down_panel": down_panel, "up_panel": up_panel, "recovery": recovery, "forward_field": forward_field, "element_owner": element_owner, "element_slot": element_slot}


def complex_product(vector, panel):
    value_re = vector[..., 0, :, :]
    value_im = vector[..., 1, :, :]
    panel_re = panel[..., 0, :, :]
    panel_im = panel[..., 1, :, :]
    first = jnp.matmul(value_re, panel_re, precision=lax.Precision.HIGHEST) - jnp.matmul(value_im, panel_im, precision=lax.Precision.HIGHEST)
    second = jnp.matmul(value_re, panel_im, precision=lax.Precision.HIGHEST) + jnp.matmul(value_im, panel_re, precision=lax.Precision.HIGHEST)
    return jnp.stack([first, second], axis=-3)


def reference(residual_blocks, residual_slab, residual_pos, shot_ids, wavelet, down_panel, up_panel, recovery, forward_field, element_owner, element_slot):
    block_rows = jnp.arange(RBLOCKS, dtype=jnp.int32)
    lateral = (block_rows // NR) % LATS
    target = ((residual_slab[:, 0] * LATS + lateral) * P_SIZE + residual_pos).astype(jnp.int32)
    summed = jax.ops.segment_sum(residual_blocks, target, num_segments=SLABS * LATS * P_SIZE)
    summed = summed.reshape(SLABS, LATS, P_SIZE, 2, SH, LB).transpose(0, 1, 3, 4, 2, 5).reshape(SLABS, LATS, 2, SH, TR)
    weights = wavelet[shot_ids]
    weight_re = weights[:, 0][:, None]
    weight_im = weights[:, 1][:, None]
    summed_re = summed[:, :, 0]
    summed_im = summed[:, :, 1]
    sources = jnp.stack([weight_re * summed_re - weight_im * summed_im, weight_re * summed_im + weight_im * summed_re], axis=2)

    def down_turn(carry, inputs):
        panel, source = inputs
        value = complex_product(carry, panel) + source
        return value, value

    start = jnp.zeros((LATS, 2, SH, TR), jnp.float32)
    unused, downs = lax.scan(down_turn, start, (down_panel, sources))

    def up_turn(carry, inputs):
        panel, source = inputs
        value = complex_product(carry, panel) + source
        return value, value

    unused, ups = lax.scan(up_turn, start, (up_panel, downs), reverse=True)
    left_rim = jnp.pad(ups[:, :-1, :, :, TR - LB:], ((0, 0), (1, 0), (0, 0), (0, 0), (0, 0)))
    right_rim = jnp.pad(ups[:, 1:, :, :, :LB], ((0, 0), (0, 1), (0, 0), (0, 0), (0, 0)))
    extended = jnp.concatenate([left_rim, ups, right_rim], axis=-1)
    interior = complex_product(extended, recovery)
    gradient = jnp.sum(forward_field * interior, axis=(2, 3)) * (SH ** -0.5)
    element_blocks = gradient.reshape(EBLOCKS, LB)
    element_rows = jnp.arange(EBLOCKS, dtype=jnp.int32)
    element_lat = (element_rows // NEB) % LATS
    element_target = ((element_owner[:, 0] * LATS + element_lat) * MBLK + element_slot).astype(jnp.int32)
    model = jax.ops.segment_sum(element_blocks, element_target, num_segments=SLABS * LATS * MBLK)
    return ups, model.reshape(SLABS, LATS, MBLK, LB)
```

```python
import functools

import jax
import jax.numpy as jnp
from jax import lax
from jax.experimental import pallas as pl
from jax.experimental.pallas import tpu as pltpu
from jax.sharding import PartitionSpec as P

MESH = pl.DeviceIdType.MESH
F32 = jnp.float32
BF16 = jnp.bfloat16
LB = 128
RY = 4
CH = 8


def split(value):
    high = value.astype(BF16)
    low = (value - high.astype(F32)).astype(BF16)
    return high, low


def remote(src, dst, send, recv, axis, where):
    return pltpu.make_async_remote_copy(
        src_ref=src,
        dst_ref=dst,
        send_sem=send,
        recv_sem=recv,
        device_id={axis: where},
        device_id_type=MESH,
    )


def kernel(
    slab_sm,
    pos_sm,
    own_sm,
    slot_sm,
    shot_v,
    wav_v,
    res_hbm,
    down_hbm,
    up_hbm,
    rec_hbm,
    ff_hbm,
    u_out,
    model_out,
    res,
    pan,
    rec,
    ff,
    wd,
    wu,
    wr,
    part,
    h1,
    f1,
    h2,
    f2,
    src,
    dbuf,
    drecv,
    urecv,
    lext,
    rext,
    xr,
    gbuf,
    gsend,
    grecv,
    load_sem,
    h1s,
    h1r,
    f1s,
    f1r,
    h2s,
    h2r,
    f2s,
    f2r,
    ds_,
    dr_,
    us_,
    ur_,
    ls_,
    lr_,
    rs_,
    rr_,
    gs_,
    gr_,
):
    slabs = 16
    lats = 8
    shots, trace = src.shape[1], src.shape[2]
    half = shots // 2
    places = trace // LB
    nres = res.shape[0]
    nch = shots // CH
    me = lax.axis_index("slab")
    lat = lax.axis_index("lat")
    y = lax.rem(me, RY)
    z = lax.div(me, RY)

    loads = [
        pltpu.make_async_copy(res_hbm, res, load_sem.at[0]),
        pltpu.make_async_copy(down_hbm, pan.at[0], load_sem.at[1]),
        pltpu.make_async_copy(up_hbm, pan.at[1], load_sem.at[2]),
        pltpu.make_async_copy(rec_hbm, rec, load_sem.at[3]),
        pltpu.make_async_copy(ff_hbm, ff, load_sem.at[4]),
    ]
    for load in loads:
        load.start()

    barrier = pltpu.get_barrier_semaphore()

    def greet(k, carry):
        other = lax.rem(me + k, slabs)
        pl.semaphore_signal(barrier, inc=1, device_id={"slab": other}, device_id_type=MESH)
        return carry

    lax.fori_loop(1, slabs, greet, 0)

    @pl.when(lat > 0)
    def _():
        pl.semaphore_signal(barrier, inc=1, device_id={"lat": lat - 1}, device_id_type=MESH)

    @pl.when(lat < lats - 1)
    def _():
        pl.semaphore_signal(barrier, inc=1, device_id={"lat": lat + 1}, device_id_type=MESH)

    def ring(col):
        return y if col == 0 else z

    def cross(col):
        return z if col == 0 else y

    def slab_at(col, t, i):
        return i * RY + t if col == 0 else t * RY + i

    def build(col, s):
        rows = pl.ds(half * col, half)

        def add(r, accs):
            block = res[r, :, rows, :]
            tag = slab_sm[r] * places + pos_sm[r]
            return tuple(
                acc + block * jnp.where(tag == s * places + p, 1.0, 0.0).astype(F32)
                for p, acc in enumerate(accs)
            )

        zero = jnp.zeros((2, half, LB), F32)
        accs = lax.fori_loop(0, nres, add, (zero,) * places, unroll=4)
        for p in range(places):
            part[s, :, rows, p * LB : (p + 1) * LB] = accs[p]

    def half_copy(stage, col, i, way, s):
        rows = pl.ds(half * col, half)
        a, b = ring(col), cross(col)
        if stage == 1:
            to = lax.rem(a + (RY - 1 if way == 0 else 1), RY)
            where = slab_at(col, to, b)
            return remote(
                part.at[s, way, rows, :], h1.at[col, i, way], h1s.at[col, i, way], h1r.at[col, i, way], "slab", where
            )
        to = lax.rem(b + (RY - 1 if way == 0 else 1), RY)
        where = slab_at(col, a, to)
        return remote(part.at[s, way, rows, :], h2.at[col, way], h2s.at[col, way], h2r.at[col, way], "slab", where)

    def full_copy(stage, col, i, way, s):
        rows = pl.ds(half * col, half)
        a, b = ring(col), cross(col)
        if stage == 1:
            to = lax.rem(a + (RY - 1 if way == 0 else 1), RY)
            where = slab_at(col, to, b)
            return remote(
                part.at[s, :, rows, :], f1.at[col, i, way], f1s.at[col, i, way], f1r.at[col, i, way], "slab", where
            )
        to = lax.rem(b + (RY - 1 if way == 0 else 1), RY)
        where = slab_at(col, a, to)
        return remote(part.at[s, :, rows, :], f2.at[col, way], f2s.at[col, way], f2r.at[col, way], "slab", where)

    loads[0].wait()

    def first(i, carry):
        for col in (0, 1):
            s = slab_at(col, lax.rem(ring(col) + 2, RY), i)
            build(col, s)
        return carry

    lax.fori_loop(0, RY, first, 0)
    peers = slabs - 1 + (lat > 0).astype(jnp.int32) + (lat < lats - 1).astype(jnp.int32)
    pl.semaphore_wait(barrier, peers)

    def first_send(i, carry):
        for col in (0, 1):
            s = slab_at(col, lax.rem(ring(col) + 2, RY), i)
            for way in (0, 1):
                half_copy(1, col, i, way, s).start()
        return carry

    lax.fori_loop(0, RY, first_send, 0)

    def second(i, carry):
        for col in (0, 1):
            for way in (0, 1):
                t = lax.rem(ring(col) + (RY - 1 if way == 0 else 1), RY)
                s = slab_at(col, t, i)
                rows = pl.ds(half * col, half)
                build(col, s)
                half_copy(1, col, i, way, s).wait_recv()
                part[s, way, rows, :] = part[s, way, rows, :] + h1[col, i, way]
                full_copy(1, col, i, way, s).start()
        return carry

    lax.fori_loop(0, RY, second, 0)

    def own(i, carry):
        for col in (0, 1):
            build(col, slab_at(col, ring(col), i))
        return carry

    lax.fori_loop(0, RY, own, 0)

    def pack(source, which, target, count):
        def col_block(j, carry):
            cols = pl.ds(pl.multiple_of(j * LB, LB), LB)
            for part_no in (0, 1):
                ref = source.at[which] if which is not None else source
                high, low = split(ref[part_no, :, cols])
                target[j, :, part_no * LB : (part_no + 1) * LB] = high
                target[j, :, (2 + part_no) * LB : (3 + part_no) * LB] = low
            return carry

        lax.fori_loop(0, count, col_block, 0)

    loads[1].wait()
    pack(pan, 0, wd, trace // LB)

    def gather(i, carry):
        for col in (0, 1):
            s = slab_at(col, ring(col), i)
            rows = pl.ds(half * col, half)
            for way in (0, 1):
                full_copy(1, col, i, way, s).wait_recv()
            part[s, :, rows, :] = part[s, :, rows, :] + (f1[col, i, 0] + f1[col, i, 1])
        return carry

    lax.fori_loop(0, RY, gather, 0)
    for col in (0, 1):
        i = lax.rem(cross(col) + 2, RY)
        s = slab_at(col, ring(col), i)
        for way in (0, 1):
            half_copy(2, col, i, way, s).start()
    loads[2].wait()
    pack(pan, 1, wu, trace // LB)
    for col in (0, 1):
        rows = pl.ds(half * col, half)
        for way in (0, 1):
            i = lax.rem(cross(col) + (RY - 1 if way == 0 else 1), RY)
            s = slab_at(col, ring(col), i)
            half_copy(2, col, i, way, s).wait_recv()
            part[s, way, rows, :] = part[s, way, rows, :] + h2[col, way]
            full_copy(2, col, i, way, s).start()

    picker = (shot_v[...] == lax.broadcasted_iota(jnp.int32, (shots, shots), 1)).astype(F32)
    weights = jnp.dot(picker, wav_v[...], precision=lax.Precision.HIGHEST, preferred_element_type=F32)

    @pl.when(lat == 0)
    def _():
        lext[...] = jnp.zeros_like(lext)

    @pl.when(lat == lats - 1)
    def _():
        rext[...] = jnp.zeros_like(rext)

    for col in (0, 1):
        rows = pl.ds(half * col, half)
        for way in (0, 1):
            full_copy(2, col, 0, way, me).wait_recv()
        total = part[me, :, rows, :] + (f2[col, 0] + f2[col, 1])
        w_re = weights[half * col : half * (col + 1), 0:1]
        w_im = weights[half * col : half * (col + 1), 1:2]
        src[0, rows, :] = w_re * total[0] - w_im * total[1]
        src[1, rows, :] = w_re * total[1] + w_im * total[0]

    def turn(arrived, target, rows, weight, extra):
        x = jnp.concatenate([arrived[0, rows, :], arrived[1, rows, :]], axis=0)
        high, low = split(x)
        x = jnp.concatenate([high, low], axis=0)
        for j in range(trace // LB):
            cols = slice(j * LB, (j + 1) * LB)
            prod = jnp.dot(x, weight[j], preferred_element_type=F32)
            prod = prod[: 2 * CH] + prod[2 * CH :]
            prod = prod[:, : 2 * LB] + prod[:, 2 * LB :]
            target[0, rows, cols] = prod[:CH, :LB] - prod[CH:, LB:] + extra[0, rows, cols]
            target[1, rows, cols] = prod[:CH, LB:] + prod[CH:, :LB] + extra[1, rows, cols]

    def rows_of(c):
        return pl.ds(pl.multiple_of(c * CH, CH), CH)

    def down_copy(c):
        rows = rows_of(c)
        return remote(
            dbuf.at[:, rows, :], drecv.at[:, rows, :], ds_.at[c], dr_.at[c], "slab", lax.rem(me + 1, slabs)
        )

    def up_copy(c):
        rows = rows_of(c)
        return remote(
            u_out.at[:, rows, :],
            urecv.at[:, rows, :],
            us_.at[c],
            ur_.at[c],
            "slab",
            lax.rem(me + slabs - 1, slabs),
        )

    def right_copy(c):
        rows = rows_of(c)
        return remote(
            u_out.at[:, rows, pl.ds(trace - LB, LB)],
            lext.at[:, rows, :],
            ls_.at[c],
            lr_.at[c],
            "lat",
            lax.rem(lat + 1, lats),
        )

    def left_copy(c):
        rows = rows_of(c)
        return remote(
            u_out.at[:, rows, pl.ds(0, LB)],
            rext.at[:, rows, :],
            rs_.at[c],
            rr_.at[c],
            "lat",
            lax.rem(lat + lats - 1, lats),
        )

    def finish(c):
        @pl.when(me > 0)
        def _():
            up_copy(c).start()

        @pl.when(lat < lats - 1)
        def _():
            right_copy(c).start()

        @pl.when(lat > 0)
        def _():
            left_copy(c).start()

    def down(c, carry):
        rows = rows_of(c)

        @pl.when(me == 0)
        def _():
            dbuf[:, rows, :] = src[:, rows, :]

        @pl.when(me > 0)
        def _():
            down_copy(c).wait_recv()
            turn(drecv, dbuf, rows, wd, src)

        @pl.when(me < slabs - 1)
        def _():
            down_copy(c).start()

        @pl.when(me == slabs - 1)
        def _():
            u_out[:, rows, :] = dbuf[:, rows, :]
            finish(c)

        return carry

    lax.fori_loop(0, nch, down, 0)
    loads[3].wait()
    pack(rec, None, wr, rec.shape[2] // LB)
    loads[4].wait()

    def up(c, carry):
        rows = rows_of(c)
        up_copy(c).wait_recv()
        turn(urecv, u_out, rows, wu, dbuf)
        finish(c)
        return carry

    @pl.when(me < slabs - 1)
    def _():
        lax.fori_loop(0, nch, up, 0)

    def edges(c, carry):
        @pl.when(lat > 0)
        def _():
            right_copy(c).wait_recv()

        @pl.when(lat < lats - 1)
        def _():
            left_copy(c).wait_recv()

        return carry

    def place(value, first_col):
        width = value.shape[-1]
        for part_no in (0, 1):
            high, low = split(value[part_no])
            xr[part_no * shots : (part_no + 1) * shots, first_col : first_col + width] = high
            xr[(2 + part_no) * shots : (3 + part_no) * shots, first_col : first_col + width] = low

    place(u_out[...], LB)
    lax.fori_loop(0, nch, edges, 0)
    place(lext[...], 0)
    place(rext[...], LB + trace)

    def recover(j, carry):
        cols = pl.ds(pl.multiple_of(j * LB, LB), LB)
        prod = jnp.dot(xr[...], wr[j, :, : 2 * LB], preferred_element_type=F32)
        prod = prod[: 2 * shots] + prod[2 * shots :]
        prod = prod + jnp.dot(xr[: 2 * shots, :], wr[j, :, 2 * LB :], preferred_element_type=F32)
        re = prod[:shots, :LB] - prod[shots:, LB:]
        im = prod[:shots, LB:] + prod[shots:, :LB]
        row = jnp.sum(ff[0, :, cols] * re + ff[1, :, cols] * im, axis=0, keepdims=True)
        gbuf[pl.ds(j, 1), :] = row * (shots ** (-0.5))
        return carry

    neb = gbuf.shape[0]
    lax.fori_loop(0, neb, recover, 0)

    grads = gbuf[...]
    lanes = lax.broadcasted_iota(jnp.int32, gsend.shape[1:], 0)
    placed = []
    for b in range(neb):
        row = jnp.broadcast_to(grads[b : b + 1, :], gsend.shape[1:])
        placed.append(jnp.where(lanes == slot_sm[b], row, 0.0))
    for s in range(slabs):
        total = jnp.zeros(gsend.shape[1:], F32)
        for b in range(neb):
            total = total + placed[b] * jnp.where(own_sm[b] == s, 1.0, 0.0).astype(F32)
        gsend[s] = total

    def grad_copy(to, sender):
        return remote(gsend.at[to], grecv.at[sender], gs_.at[to], gr_.at[sender], "slab", to)

    def grad_send(k, carry):
        grad_copy(lax.rem(me + k, slabs), me).start()
        return carry

    lax.fori_loop(1, slabs, grad_send, 0)
    grecv[me] = gsend[me]

    def drain1(i, carry):
        for col in (0, 1):
            s = slab_at(col, lax.rem(ring(col) + 2, RY), i)
            for way in (0, 1):
                half_copy(1, col, i, way, s).wait_send()
                full_copy(1, col, i, way, s).wait_send()
        return carry

    lax.fori_loop(0, RY, drain1, 0)
    for col in (0, 1):
        for way in (0, 1):
            half_copy(2, col, 0, way, me).wait_send()
            full_copy(2, col, 0, way, me).wait_send()

    def drain2(c, carry):
        @pl.when(me < slabs - 1)
        def _():
            down_copy(c).wait_send()

        @pl.when(me > 0)
        def _():
            up_copy(c).wait_send()

        @pl.when(lat < lats - 1)
        def _():
            right_copy(c).wait_send()

        @pl.when(lat > 0)
        def _():
            left_copy(c).wait_send()

        return carry

    lax.fori_loop(0, nch, drain2, 0)

    def grad_wait(k, total):
        other = lax.rem(me + k, slabs)
        grad_copy(other, other).wait_recv()
        return total + grecv[other]

    model_out[...] = lax.fori_loop(1, slabs, grad_wait, grecv[me])

    def grad_drain(k, carry):
        grad_copy(lax.rem(me + k, slabs), me).wait_send()
        return carry

    lax.fori_loop(1, slabs, grad_drain, 0)


def body(
    residual_blocks,
    residual_slab,
    residual_pos,
    shot_ids,
    wavelet,
    down_panel,
    up_panel,
    recovery,
    forward_field,
    element_owner,
    element_slot,
):
    slabs = 16
    nres, _, shots, width = residual_blocks.shape
    trace = down_panel.shape[-1]
    depth, nel = recovery.shape[-2:]
    neb = element_slot.shape[0]
    half = shots // 2
    nch = shots // CH
    smem = pl.BlockSpec(memory_space=pltpu.SMEM)
    vmem = pl.BlockSpec(memory_space=pltpu.VMEM)
    hbm = pl.BlockSpec(memory_space=pl.ANY)
    dma = pltpu.SemaphoreType.DMA
    ups, model = pl.pallas_call(
        kernel,
        out_shape=(
            jax.ShapeDtypeStruct((2, shots, trace), F32),
            jax.ShapeDtypeStruct((neb, width), F32),
        ),
        in_specs=[smem] * 4 + [vmem] * 2 + [hbm] * 5,
        out_specs=(vmem, vmem),
        scratch_shapes=[
            pltpu.VMEM((nres, 2, shots, width), F32),
            pltpu.VMEM((2, 2, trace, trace), F32),
            pltpu.VMEM((2, depth, nel), F32),
            pltpu.VMEM((2, shots, nel), F32),
            pltpu.VMEM((trace // width, trace, 4 * width), BF16),
            pltpu.VMEM((trace // width, trace, 4 * width), BF16),
            pltpu.VMEM((nel // width, depth, 4 * width), BF16),
            pltpu.VMEM((slabs, 2, shots, trace), F32),
            pltpu.VMEM((2, RY, 2, half, trace), F32),
            pltpu.VMEM((2, RY, 2, 2, half, trace), F32),
            pltpu.VMEM((2, 2, half, trace), F32),
            pltpu.VMEM((2, 2, 2, half, trace), F32),
            pltpu.VMEM((2, shots, trace), F32),
            pltpu.VMEM((2, shots, trace), F32),
            pltpu.VMEM((2, shots, trace), F32),
            pltpu.VMEM((2, shots, trace), F32),
            pltpu.VMEM((2, shots, width), F32),
            pltpu.VMEM((2, shots, width), F32),
            pltpu.VMEM((4 * shots, depth), BF16),
            pltpu.VMEM((neb, width), F32),
            pltpu.VMEM((slabs, neb, width), F32),
            pltpu.VMEM((slabs, neb, width), F32),
            dma((5,)),
            dma((2, RY, 2)),
            dma((2, RY, 2)),
            dma((2, RY, 2)),
            dma((2, RY, 2)),
            dma((2, 2)),
            dma((2, 2)),
            dma((2, 2)),
            dma((2, 2)),
            dma((nch,)),
            dma((nch,)),
            dma((nch,)),
            dma((nch,)),
            dma((nch,)),
            dma((nch,)),
            dma((nch,)),
            dma((nch,)),
            dma((slabs,)),
            dma((slabs,)),
        ],
        compiler_params=pltpu.CompilerParams(
            collective_id=0, has_side_effects=True, vmem_limit_bytes=60 * 1024 * 1024
        ),
    )(
        residual_slab.reshape(-1),
        residual_pos,
        element_owner.reshape(-1),
        element_slot,
        shot_ids.reshape(-1, 1),
        wavelet,
        residual_blocks,
        down_panel[0, 0],
        up_panel[0, 0],
        recovery[0, 0],
        forward_field[0, 0],
    )
    return (ups[None, None], model[None, None])


def solution(mesh):
    placed = (
        P(("slab", "lat"), None, None, None),
        P(("slab", "lat"), None),
        P(("slab", "lat")),
        P(),
        P(),
        P("slab", "lat", None, None, None),
        P("slab", "lat", None, None, None),
        P("slab", "lat", None, None, None),
        P("slab", "lat", None, None, None),
        P(("slab", "lat"), None),
        P(("slab", "lat")),
    )
    return jax.shard_map(
        body,
        mesh=mesh,
        in_specs=placed,
        out_specs=(P("slab", "lat", None, None, None), P("slab", "lat", None, None)),
        check_vma=False,
    )
```

```python
import functools

import jax
import jax.numpy as jnp
from jax import lax
from jax.experimental import pallas as pl
from jax.experimental.pallas import tpu as pltpu
from jax.sharding import PartitionSpec as P

MESH = pl.DeviceIdType.MESH
F32 = jnp.float32
BF16 = jnp.bfloat16
LB = 128
RY = 4
CH = 8


def split(value):
    high = value.astype(BF16)
    low = (value - high.astype(F32)).astype(BF16)
    return high, low


def remote(src, dst, send, recv, axis, where):
    return pltpu.make_async_remote_copy(
        src_ref=src,
        dst_ref=dst,
        send_sem=send,
        recv_sem=recv,
        device_id={axis: where},
        device_id_type=MESH,
    )


def kernel(
    slab_sm,
    pos_sm,
    own_sm,
    slot_sm,
    shot_v,
    wav_v,
    res_hbm,
    down_hbm,
    up_hbm,
    rec_hbm,
    ff_hbm,
    u_out,
    model_out,
    res,
    pan,
    rec,
    ff,
    wd,
    wu,
    wr,
    part,
    h1,
    f1,
    h2,
    f2,
    src,
    dbuf,
    ubuf,
    drecv,
    urecv,
    lext,
    rext,
    xr,
    gbuf,
    gsend,
    grecv,
    load_sem,
    h1s,
    h1r,
    f1s,
    f1r,
    h2s,
    h2r,
    f2s,
    f2r,
    ds_,
    dr_,
    us_,
    ur_,
    ls_,
    lr_,
    rs_,
    r2s_,
    rr_,
    as_,
    ar_,
    gs_,
    gr_,
    ps_,
    pr_,
    ss_,
    sr_,
):
    slabs = 16
    lats = 8
    shots, trace = src.shape[2], src.shape[3]
    half = shots // 2
    places = trace // LB
    nres = res.shape[0]
    nch = shots // CH
    me = lax.axis_index("slab")
    lat = lax.axis_index("lat")
    y = lax.rem(me, RY)
    z = lax.div(me, RY)

    core = lax.rem(lat, 2)
    mate = lat + 1 - 2 * core
    load_res = pltpu.make_async_copy(res_hbm, res, load_sem.at[0])
    load_down = pltpu.make_async_copy(down_hbm, pan.at[0], load_sem.at[1])
    load_up = pltpu.make_async_copy(up_hbm, pan.at[1], load_sem.at[2])
    load_rec = pltpu.make_async_copy(rec_hbm, rec, load_sem.at[3])
    load_ff = pltpu.make_async_copy(ff_hbm, ff, load_sem.at[4])
    load_res.start()

    @pl.when(core == 1)
    def _():
        load_down.start()
        load_up.start()

    load_rec.start()
    load_ff.start()

    barrier = pltpu.get_barrier_semaphore()

    def greet(k, carry):
        other = lax.rem(me + k, slabs)
        pl.semaphore_signal(barrier, inc=1, device_id={"slab": other}, device_id_type=MESH)
        return carry

    lax.fori_loop(1, slabs, greet, 0)

    def meet(step, present):
        @pl.when(present)
        def _():
            pl.semaphore_signal(barrier, inc=1, device_id={"lat": lat + step}, device_id_type=MESH)

    meet(-1, lat > 0)
    meet(1, lat < lats - 1)
    meet(-2, jnp.logical_and(core == 1, lat > 1))
    meet(2, jnp.logical_and(core == 1, lat < lats - 1))

    def ring(col):
        return y if col == 0 else z

    def cross(col):
        return z if col == 0 else y

    def slab_at(col, t, i):
        return i * RY + t if col == 0 else t * RY + i

    def order(col, k):
        off = jnp.where(k < 2, 2 - k, 3 * (3 - k))
        return lax.rem(cross(col) + off, RY)

    def build(col, s):
        rows = pl.ds(half * col, half)

        def add(r, accs):
            block = res[r, :, rows, :]
            tag = slab_sm[r] * places + pos_sm[r]
            return tuple(
                acc + block * jnp.where(tag == s * places + p, 1.0, 0.0).astype(F32)
                for p, acc in enumerate(accs)
            )

        zero = jnp.zeros((2, half, LB), F32)
        accs = lax.fori_loop(0, nres, add, (zero,) * places, unroll=4)
        for p in range(places):
            part[s, :, rows, p * LB : (p + 1) * LB] = accs[p]

    def half_copy(stage, col, i, way, s):
        rows = pl.ds(half * col, half)
        a, b = ring(col), cross(col)
        if stage == 1:
            to = lax.rem(a + (RY - 1 if way == 0 else 1), RY)
            where = slab_at(col, to, b)
            return remote(
                part.at[s, way, rows, :], h1.at[col, i, way], h1s.at[col, i, way], h1r.at[col, i, way], "slab", where
            )
        to = lax.rem(b + (RY - 1 if way == 0 else 1), RY)
        where = slab_at(col, a, to)
        return remote(part.at[s, way, rows, :], h2.at[col, way], h2s.at[col, way], h2r.at[col, way], "slab", where)

    def full_copy(stage, col, i, way, s):
        rows = pl.ds(half * col, half)
        a, b = ring(col), cross(col)
        if stage == 1:
            to = lax.rem(a + (RY - 1 if way == 0 else 1), RY)
            where = slab_at(col, to, b)
            return remote(
                part.at[s, :, rows, :], f1.at[col, i, way], f1s.at[col, i, way], f1r.at[col, i, way], "slab", where
            )
        to = lax.rem(b + (RY - 1 if way == 0 else 1), RY)
        where = slab_at(col, a, to)
        return remote(part.at[s, :, rows, :], f2.at[col, way], f2s.at[col, way], f2r.at[col, way], "slab", where)

    load_res.wait()

    def first(k, carry):
        for col in (0, 1):
            i = order(col, k)
            s = slab_at(col, lax.rem(ring(col) + 2, RY), i)
            build(col, s)
        return carry

    lax.fori_loop(0, RY, first, 0)
    peers = slabs - 1 + (lat > 0).astype(jnp.int32) + (lat < lats - 1).astype(jnp.int32)
    peers = peers + core * ((lat > 1).astype(jnp.int32) + (lat < lats - 1).astype(jnp.int32))
    pl.semaphore_wait(barrier, peers)

    def panel_copy(which):
        ref = down_hbm if which == 0 else up_hbm
        return remote(ref, pan.at[2 + which], ps_.at[which], pr_.at[which], "lat", mate)

    @pl.when(core == 0)
    def _():
        panel_copy(0).start()

    def first_send(k, carry):
        for col in (0, 1):
            i = order(col, k)
            s = slab_at(col, lax.rem(ring(col) + 2, RY), i)
            for way in (0, 1):
                half_copy(1, col, i, way, s).start()
        return carry

    lax.fori_loop(0, RY, first_send, 0)

    def second(k, carry):
        for col in (0, 1):
            i = order(col, k)
            for way in (0, 1):
                t = lax.rem(ring(col) + (RY - 1 if way == 0 else 1), RY)
                s = slab_at(col, t, i)
                rows = pl.ds(half * col, half)
                build(col, s)
                half_copy(1, col, i, way, s).wait_recv()
                part[s, way, rows, :] = part[s, way, rows, :] + h1[col, i, way]
                full_copy(1, col, i, way, s).start()
        return carry

    lax.fori_loop(0, RY, second, 0)

    def own(i, carry):
        for col in (0, 1):
            build(col, slab_at(col, ring(col), i))
        return carry

    lax.fori_loop(0, RY, own, 0)

    def pack(source, which, target, count):
        def col_block(j, carry):
            cols = pl.ds(pl.multiple_of(j * LB, LB), LB)
            for part_no in (0, 1):
                ref = source.at[which] if which is not None else source
                high, low = split(ref[part_no, :, cols])
                target[j, :, part_no * LB : (part_no + 1) * LB] = high
                target[j, :, (2 + part_no) * LB : (3 + part_no) * LB] = low
            return carry

        lax.fori_loop(0, count, col_block, 0)

    @pl.when(core == 1)
    def _():
        load_down.wait()
        pack(pan, 0, wd.at[1], trace // LB)

    @pl.when(core == 0)
    def _():
        panel_copy(1).start()


    def gather(k, carry):
        for col in (0, 1):
            i = order(col, k)
            s = slab_at(col, ring(col), i)
            rows = pl.ds(half * col, half)
            for way in (0, 1):
                full_copy(1, col, i, way, s).wait_recv()
            part[s, :, rows, :] = part[s, :, rows, :] + (f1[col, i, 0] + f1[col, i, 1])
        return carry

    lax.fori_loop(0, 1, gather, 0)
    for col in (0, 1):
        i = lax.rem(cross(col) + 2, RY)
        s = slab_at(col, ring(col), i)
        for way in (0, 1):
            half_copy(2, col, i, way, s).start()
    lax.fori_loop(1, RY, gather, 0)
    for col in (0, 1):
        rows = pl.ds(half * col, half)
        for way in (0, 1):
            i = lax.rem(cross(col) + (RY - 1 if way == 0 else 1), RY)
            s = slab_at(col, ring(col), i)
            half_copy(2, col, i, way, s).wait_recv()
            part[s, way, rows, :] = part[s, way, rows, :] + h2[col, way]
            full_copy(2, col, i, way, s).start()

    @pl.when(core == 1)
    def _():
        panel_copy(0).wait_recv()
        pack(pan, 2, wd.at[0], trace // LB)
        load_up.wait()
        pack(pan, 1, wu.at[1], trace // LB)

    @pl.when(core == 0)
    def _():
        load_rec.wait()
        pack(rec, None, wr, rec.shape[2] // LB)

    picker = (shot_v[...] == lax.broadcasted_iota(jnp.int32, (shots, shots), 1)).astype(F32)
    weights = jnp.dot(picker, wav_v[...], precision=lax.Precision.HIGHEST, preferred_element_type=F32)

    @pl.when(lat == 0)
    def _():
        lext[...] = jnp.zeros_like(lext)

    @pl.when(lat == lats - 1)
    def _():
        rext[...] = jnp.zeros_like(rext)

    def source_copy(col):
        rows = pl.ds(half * col, half)
        return remote(src.at[0, :, rows, :], src.at[0, :, rows, :], ss_.at[col], sr_.at[col], "lat", mate)

    for col in (0, 1):
        rows = pl.ds(half * col, half)
        for way in (0, 1):
            full_copy(2, col, 0, way, me).wait_recv()
        total = part[me, :, rows, :] + (f2[col, 0] + f2[col, 1])
        w_re = weights[half * col : half * (col + 1), 0:1]
        w_im = weights[half * col : half * (col + 1), 1:2]
        src[core, 0, rows, :] = w_re * total[0] - w_im * total[1]
        src[core, 1, rows, :] = w_re * total[1] + w_im * total[0]

        @pl.when(core == 0)
        def _():
            source_copy(col).start()

    def turn(arrived, target, rows, weight, extra):
        x = jnp.concatenate([arrived[0, rows, :], arrived[1, rows, :]], axis=0)
        high, low = split(x)
        x = jnp.concatenate([high, low], axis=0)
        for j in range(trace // LB):
            cols = slice(j * LB, (j + 1) * LB)
            prod = jnp.dot(x, weight[j], preferred_element_type=F32)
            prod = prod[: 2 * CH] + prod[2 * CH :]
            prod = prod[:, : 2 * LB] + prod[:, 2 * LB :]
            target[0, rows, cols] = prod[:CH, :LB] - prod[CH:, LB:] + extra[0, rows, cols]
            target[1, rows, cols] = prod[:CH, LB:] + prod[CH:, :LB] + extra[1, rows, cols]

    def rows_of(c):
        return pl.ds(pl.multiple_of(c * CH, CH), CH)

    def down_copy(c, w):
        rows = rows_of(c)
        return remote(
            dbuf.at[w, :, rows, :],
            drecv.at[w, :, rows, :],
            ds_.at[w, c],
            dr_.at[w, c],
            "slab",
            lax.rem(me + 1, slabs),
        )

    def up_copy(c, w):
        rows = rows_of(c)
        return remote(
            ubuf.at[w, :, rows, :],
            urecv.at[w, :, rows, :],
            us_.at[w, c],
            ur_.at[w, c],
            "slab",
            lax.rem(me + slabs - 1, slabs),
        )

    def last_cells(c, w, to):
        rows = rows_of(c)
        return remote(
            ubuf.at[w, :, rows, pl.ds(trace - LB, LB)], lext.at[:, rows, :], ls_.at[c], lr_.at[c], "lat", to
        )

    def first_cells(c, w, to):
        rows = rows_of(c)
        send = rs_ if w == 1 else r2s_
        return remote(ubuf.at[w, :, rows, pl.ds(0, LB)], rext.at[:, rows, :], send.at[c], rr_.at[c], "lat", to)

    def back_copy(c):
        rows = rows_of(c)
        return remote(ubuf.at[0, :, rows, :], u_out.at[:, rows, :], as_.at[c], ar_.at[c], "lat", mate)

    after = lax.rem(lat + 1, lats)
    before2 = lax.rem(lat + lats - 2, lats)

    def finish(c, w):
        rows = rows_of(c)

        @pl.when(me > 0)
        def _():
            up_copy(c, w).start()

        if w == 0:
            back_copy(c).start()

            @pl.when(lat > 1)
            def _():
                first_cells(c, 0, before2).start()

            lext[:, rows, :] = ubuf[0, :, rows, trace - LB :]
        else:
            first_cells(c, 1, mate).start()

            @pl.when(lat < lats - 1)
            def _():
                last_cells(c, 1, after).start()

            u_out[:, rows, :] = ubuf[1, :, rows, :]

    def down(c, carry):
        rows = rows_of(c)
        for w in (1, 0):

            @pl.when(me == 0)
            def _():
                dbuf[w, :, rows, :] = src[w, :, rows, :]

            @pl.when(me > 0)
            def _():
                down_copy(c, w).wait_recv()
                turn(drecv.at[w], dbuf.at[w], rows, wd.at[w], src.at[w])

            @pl.when(me < slabs - 1)
            def _():
                down_copy(c, w).start()

            @pl.when(me == slabs - 1)
            def _():
                ubuf[w, :, rows, :] = dbuf[w, :, rows, :]
                finish(c, w)

        return carry

    def up(c, carry):
        rows = rows_of(c)
        for w in (1, 0):
            up_copy(c, w).wait_recv()
            turn(urecv.at[w], ubuf.at[w], rows, wu.at[w], dbuf.at[w])
            finish(c, w)
        return carry

    def late_packs():
        panel_copy(1).wait_recv()
        pack(pan, 3, wu.at[0], trace // LB)
        load_rec.wait()
        pack(rec, None, wr, rec.shape[2] // LB)

    @pl.when(core == 1)
    def _():
        @pl.when(me >= slabs // 2)
        def _():
            late_packs()

        for col in (0, 1):
            source_copy(col).wait_recv()
        lax.fori_loop(0, nch, down, 0)

        @pl.when(me < slabs // 2)
        def _():
            late_packs()

        @pl.when(me < slabs - 1)
        def _():
            lax.fori_loop(0, nch, up, 0)

    load_ff.wait()

    def edges(c, carry):
        @pl.when(core == 0)
        def _():
            back_copy(c).wait_recv()
            first_cells(c, 1, mate).wait_recv()

        @pl.when(jnp.logical_and(core == 0, lat > 0))
        def _():
            last_cells(c, 1, after).wait_recv()

        @pl.when(jnp.logical_and(core == 1, lat < lats - 1))
        def _():
            first_cells(c, 0, before2).wait_recv()

        return carry

    def place(value, first_col):
        width = value.shape[-1]
        for part_no in (0, 1):
            high, low = split(value[part_no])
            xr[part_no * shots : (part_no + 1) * shots, first_col : first_col + width] = high
            xr[(2 + part_no) * shots : (3 + part_no) * shots, first_col : first_col + width] = low

    lax.fori_loop(0, nch, edges, 0)
    place(u_out[...], LB)
    place(lext[...], 0)
    place(rext[...], LB + trace)

    def recover(j, carry):
        cols = pl.ds(pl.multiple_of(j * LB, LB), LB)
        prod = jnp.dot(xr[...], wr[j, :, : 2 * LB], preferred_element_type=F32)
        prod = prod[: 2 * shots] + prod[2 * shots :]
        prod = prod + jnp.dot(xr[: 2 * shots, :], wr[j, :, 2 * LB :], preferred_element_type=F32)
        re = prod[:shots, :LB] - prod[shots:, LB:]
        im = prod[:shots, LB:] + prod[shots:, :LB]
        row = jnp.sum(ff[0, :, cols] * re + ff[1, :, cols] * im, axis=0, keepdims=True)
        gbuf[pl.ds(j, 1), :] = row * (shots ** (-0.5))
        return carry

    neb = gbuf.shape[0]
    lax.fori_loop(0, neb, recover, 0)

    grads = gbuf[...]
    lanes = lax.broadcasted_iota(jnp.int32, gsend.shape[1:], 0)
    placed = []
    for b in range(neb):
        row = jnp.broadcast_to(grads[b : b + 1, :], gsend.shape[1:])
        placed.append(jnp.where(lanes == slot_sm[b], row, 0.0))
    for s in range(slabs):
        total = jnp.zeros(gsend.shape[1:], F32)
        for b in range(neb):
            total = total + placed[b] * jnp.where(own_sm[b] == s, 1.0, 0.0).astype(F32)
        gsend[s] = total

    def grad_copy(to, sender):
        return remote(gsend.at[to], grecv.at[sender], gs_.at[to], gr_.at[sender], "slab", to)

    def grad_send(k, carry):
        grad_copy(lax.rem(me + k, slabs), me).start()
        return carry

    lax.fori_loop(1, slabs, grad_send, 0)
    grecv[me] = gsend[me]

    def drain1(i, carry):
        for col in (0, 1):
            s = slab_at(col, lax.rem(ring(col) + 2, RY), i)
            for way in (0, 1):
                half_copy(1, col, i, way, s).wait_send()
                full_copy(1, col, i, way, s).wait_send()
        return carry

    lax.fori_loop(0, RY, drain1, 0)
    for col in (0, 1):
        for way in (0, 1):
            half_copy(2, col, 0, way, me).wait_send()
            full_copy(2, col, 0, way, me).wait_send()

    def drain2(c, carry):
        for w in (0, 1):

            @pl.when(me < slabs - 1)
            def _():
                down_copy(c, w).wait_send()

            @pl.when(me > 0)
            def _():
                up_copy(c, w).wait_send()

        back_copy(c).wait_send()
        first_cells(c, 1, mate).wait_send()

        @pl.when(lat > 1)
        def _():
            first_cells(c, 0, before2).wait_send()

        @pl.when(lat < lats - 1)
        def _():
            last_cells(c, 1, after).wait_send()

        return carry

    @pl.when(core == 1)
    def _():
        lax.fori_loop(0, nch, drain2, 0)

    @pl.when(core == 0)
    def _():
        for k in (0, 1):
            panel_copy(k).wait_send()
            source_copy(k).wait_send()

    def grad_wait(k, total):
        other = lax.rem(me + k, slabs)
        grad_copy(other, other).wait_recv()
        return total + grecv[other]

    model_out[...] = lax.fori_loop(1, slabs, grad_wait, grecv[me])

    def grad_drain(k, carry):
        grad_copy(lax.rem(me + k, slabs), me).wait_send()
        return carry

    lax.fori_loop(1, slabs, grad_drain, 0)


def body(
    residual_blocks,
    residual_slab,
    residual_pos,
    shot_ids,
    wavelet,
    down_panel,
    up_panel,
    recovery,
    forward_field,
    element_owner,
    element_slot,
):
    slabs = 16
    nres, _, shots, width = residual_blocks.shape
    trace = down_panel.shape[-1]
    depth, nel = recovery.shape[-2:]
    neb = element_slot.shape[0]
    half = shots // 2
    nch = shots // CH
    smem = pl.BlockSpec(memory_space=pltpu.SMEM)
    vmem = pl.BlockSpec(memory_space=pltpu.VMEM)
    hbm = pl.BlockSpec(memory_space=pl.ANY)
    dma = pltpu.SemaphoreType.DMA
    ups, model = pl.pallas_call(
        kernel,
        out_shape=(
            jax.ShapeDtypeStruct((2, shots, trace), F32),
            jax.ShapeDtypeStruct((neb, width), F32),
        ),
        in_specs=[smem] * 4 + [vmem] * 2 + [hbm] * 5,
        out_specs=(vmem, vmem),
        scratch_shapes=[
            pltpu.VMEM((nres, 2, shots, width), F32),
            pltpu.VMEM((4, 2, trace, trace), F32),
            pltpu.VMEM((2, depth, nel), F32),
            pltpu.VMEM((2, shots, nel), F32),
            pltpu.VMEM((2, trace // width, trace, 4 * width), BF16),
            pltpu.VMEM((2, trace // width, trace, 4 * width), BF16),
            pltpu.VMEM((nel // width, depth, 4 * width), BF16),
            pltpu.VMEM((slabs, 2, shots, trace), F32),
            pltpu.VMEM((2, RY, 2, half, trace), F32),
            pltpu.VMEM((2, RY, 2, 2, half, trace), F32),
            pltpu.VMEM((2, 2, half, trace), F32),
            pltpu.VMEM((2, 2, 2, half, trace), F32),
            pltpu.VMEM((2, 2, shots, trace), F32),
            pltpu.VMEM((2, 2, shots, trace), F32),
            pltpu.VMEM((2, 2, shots, trace), F32),
            pltpu.VMEM((2, 2, shots, trace), F32),
            pltpu.VMEM((2, 2, shots, trace), F32),
            pltpu.VMEM((2, shots, width), F32),
            pltpu.VMEM((2, shots, width), F32),
            pltpu.VMEM((4 * shots, depth), BF16),
            pltpu.VMEM((neb, width), F32),
            pltpu.VMEM((slabs, neb, width), F32),
            pltpu.VMEM((slabs, neb, width), F32),
            dma((5,)),
            dma((2, RY, 2)),
            dma((2, RY, 2)),
            dma((2, RY, 2)),
            dma((2, RY, 2)),
            dma((2, 2)),
            dma((2, 2)),
            dma((2, 2)),
            dma((2, 2)),
            dma((2, nch)),
            dma((2, nch)),
            dma((2, nch)),
            dma((2, nch)),
            dma((nch,)),
            dma((nch,)),
            dma((nch,)),
            dma((nch,)),
            dma((nch,)),
            dma((nch,)),
            dma((nch,)),
            dma((slabs,)),
            dma((slabs,)),
            dma((2,)),
            dma((2,)),
            dma((2,)),
            dma((2,)),
        ],
        compiler_params=pltpu.CompilerParams(
            collective_id=0, has_side_effects=True, vmem_limit_bytes=60 * 1024 * 1024
        ),
    )(
        residual_slab.reshape(-1),
        residual_pos,
        element_owner.reshape(-1),
        element_slot,
        shot_ids.reshape(-1, 1),
        wavelet,
        residual_blocks,
        down_panel[0, 0],
        up_panel[0, 0],
        recovery[0, 0],
        forward_field[0, 0],
    )
    return (ups[None, None], model[None, None])


def solution(mesh):
    placed = (
        P(("slab", "lat"), None, None, None),
        P(("slab", "lat"), None),
        P(("slab", "lat")),
        P(),
        P(),
        P("slab", "lat", None, None, None),
        P("slab", "lat", None, None, None),
        P("slab", "lat", None, None, None),
        P("slab", "lat", None, None, None),
        P(("slab", "lat"), None),
        P(("slab", "lat")),
    )
    return jax.shard_map(
        body,
        mesh=mesh,
        in_specs=placed,
        out_specs=(P("slab", "lat", None, None, None), P("slab", "lat", None, None)),
        check_vma=False,
    )
```

```python
import functools

import jax
import jax.numpy as jnp
from jax import lax
from jax.experimental import pallas as pl
from jax.experimental.pallas import tpu as pltpu
from jax.sharding import PartitionSpec as P

MESH = pl.DeviceIdType.MESH
F32 = jnp.float32
BF16 = jnp.bfloat16
LB = 128
RY = 4
CAP = 4
CH = 8
NS = 1


def split(value):
    high = value.astype(BF16)
    low = (value - high.astype(F32)).astype(BF16)
    return high, low


def remote(src, dst, send, recv, axis, where):
    return pltpu.make_async_remote_copy(
        src_ref=src,
        dst_ref=dst,
        send_sem=send,
        recv_sem=recv,
        device_id={axis: where},
        device_id_type=MESH,
    )


def kernel(
    slab_v,
    pos_v,
    own_sm,
    slot_sm,
    shot_sm,
    wav_sm,
    res_hbm,
    down_hbm,
    up_hbm,
    rec_hbm,
    ff_hbm,
    u_hbm,
    model_out,
    res,
    pan,
    rec,
    ff,
    wd,
    wu,
    wr,
    part,
    h1,
    f1,
    h2,
    f2,
    src,
    dbuf,
    ubuf,
    drecv,
    urecv,
    lext,
    rext,
    xr,
    gbuf,
    gsend,
    grecv,
    tab_v,
    tab_sm,
    wbuf,
    load_sem,
    h1s,
    h1r,
    f1s,
    f1r,
    h2s,
    h2r,
    f2s,
    f2r,
    ds_,
    dr_,
    us_,
    ur_,
    ls_,
    lr_,
    rs_,
    r2s_,
    rr_,
    as_,
    ar_,
    gs_,
    gr_,
    ps_,
    pr_,
    ss_,
    sr_,
):
    slabs = 16
    lats = 8
    shots, trace = src.shape[2], src.shape[3]
    half = shots // 2
    places = trace // LB
    nres = res.shape[0]
    nch = shots // CH
    me = lax.axis_index("slab")
    lat = lax.axis_index("lat")
    y = lax.rem(me, RY)
    z = lax.div(me, RY)

    core = lax.rem(lat, 2)
    mate = lat + 1 - 2 * core
    load_res = pltpu.make_async_copy(res_hbm, res, load_sem.at[0])
    load_down = pltpu.make_async_copy(down_hbm, pan.at[0], load_sem.at[1])
    load_up = pltpu.make_async_copy(up_hbm, pan.at[1], load_sem.at[2])
    load_rec = pltpu.make_async_copy(rec_hbm, rec, load_sem.at[3])
    load_ff = pltpu.make_async_copy(ff_hbm, ff, load_sem.at[4])
    load_res.start()

    @pl.when(core == 1)
    def _():
        load_down.start()
        load_up.start()

    load_rec.start()
    load_ff.start()

    barrier = pltpu.get_barrier_semaphore()

    for step in (1, RY - 1):
        for other in (z * RY + lax.rem(y + step, RY), lax.rem(z + step, RY) * RY + y):
            pl.semaphore_signal(barrier, inc=1, device_id={"slab": other}, device_id_type=MESH)

    def meet(step, present):
        @pl.when(present)
        def _():
            pl.semaphore_signal(barrier, inc=1, device_id={"lat": lat + step}, device_id_type=MESH)

    meet(-1, lat > 0)
    meet(1, lat < lats - 1)
    meet(-2, jnp.logical_and(core == 1, lat > 1))
    meet(2, jnp.logical_and(core == 1, lat < lats - 1))

    rows_no = lax.broadcasted_iota(jnp.int32, (1, nres), 1)
    match = slab_v[...] == lax.broadcasted_iota(jnp.int32, (slabs, nres), 0)
    hits = jnp.where(match, 1.0, 0.0).astype(F32)
    before = lax.broadcasted_iota(jnp.int32, (nres, nres), 0) < lax.broadcasted_iota(jnp.int32, (nres, nres), 1)
    rank = jnp.dot(hits.astype(BF16), jnp.where(before, 1.0, 0.0).astype(BF16), preferred_element_type=F32)
    code = (rows_no * 8 + pos_v[...]).astype(F32)
    found = jnp.sum(hits, axis=1, keepdims=True)
    lane = lax.broadcasted_iota(jnp.int32, tab_v.shape, 1)
    table = jnp.zeros(tab_v.shape, F32)
    for c in range(CAP):
        value = jnp.sum(jnp.where(rank == c, hits * code, 0.0), axis=1, keepdims=True)
        value = jnp.where(found > c, value, 7.0)
        table = table + jnp.where(lane == c, value, 0.0)
    tab_v[...] = table.astype(jnp.int32)
    load_tab = pltpu.make_async_copy(tab_v, tab_sm, load_sem.at[5])
    load_tab.start()

    def weight_row(j, carry):
        for part_no in (0, 1):
            wbuf[part_no, pl.ds(j, 1), :] = jnp.full((1, LB), wav_sm[part_no, shot_sm[j]], F32)
        return carry

    lax.fori_loop(0, shots, weight_row, 0, unroll=8)
    load_tab.wait()

    def ring(col):
        return y if col == 0 else z

    def cross(col):
        return z if col == 0 else y

    def slab_at(col, t, i):
        return i * RY + t if col == 0 else t * RY + i

    def order(col, k):
        off = jnp.where(k < 2, 2 - k, 3 * (3 - k))
        return lax.rem(cross(col) + off, RY)

    def build(col, s):
        rows = pl.ds(half * col, half)
        codes = [tab_sm[s, c] for c in range(CAP)]
        blocks = [res[lax.bitwise_and(lax.shift_right_logical(code, 3), nres - 1), :, rows, :] for code in codes]
        spots = [lax.bitwise_and(code, 7) for code in codes]
        for p in range(places):
            total = blocks[0] * jnp.where(spots[0] == p, 1.0, 0.0).astype(F32)
            for c in range(1, CAP):
                total = total + blocks[c] * jnp.where(spots[c] == p, 1.0, 0.0).astype(F32)
            part[s, :, rows, p * LB : (p + 1) * LB] = total

    def half_copy(stage, col, i, way, s):
        rows = pl.ds(half * col, half)
        a, b = ring(col), cross(col)
        if stage == 1:
            to = lax.rem(a + (RY - 1 if way == 0 else 1), RY)
            where = slab_at(col, to, b)
            return remote(
                part.at[s, way, rows, :], h1.at[col, i, way], h1s, h1r.at[col, i, way], "slab", where
            )
        to = lax.rem(b + (RY - 1 if way == 0 else 1), RY)
        where = slab_at(col, a, to)
        return remote(part.at[s, way, rows, :], h2.at[col, way], h2s, h2r.at[col, way], "slab", where)

    def full_copy(stage, col, i, way, s):
        rows = pl.ds(half * col, half)
        a, b = ring(col), cross(col)
        if stage == 1:
            to = lax.rem(a + (RY - 1 if way == 0 else 1), RY)
            where = slab_at(col, to, b)
            return remote(
                part.at[s, :, rows, :], f1.at[col, i, way], f1s, f1r.at[col, i, way], "slab", where
            )
        to = lax.rem(b + (RY - 1 if way == 0 else 1), RY)
        where = slab_at(col, a, to)
        return remote(part.at[s, :, rows, :], f2.at[col, way], f2s, f2r.at[col, way], "slab", where)

    load_res.wait()

    def first(k, carry):
        for col in (0, 1):
            i = order(col, k)
            s = slab_at(col, lax.rem(ring(col) + 2, RY), i)
            build(col, s)
        return carry

    lax.fori_loop(0, RY, first, 0)
    peers = 4 + (lat > 0).astype(jnp.int32) + (lat < lats - 1).astype(jnp.int32)
    peers = peers + core * ((lat > 1).astype(jnp.int32) + (lat < lats - 1).astype(jnp.int32))
    pl.semaphore_wait(barrier, peers)

    def panel_copy(which):
        ref = down_hbm if which == 0 else up_hbm
        return remote(ref, pan.at[2 + which], ps_.at[which], pr_.at[which], "lat", mate)

    @pl.when(core == 0)
    def _():
        panel_copy(0).start()

    def first_send(k, carry):
        for col in (0, 1):
            i = order(col, k)
            s = slab_at(col, lax.rem(ring(col) + 2, RY), i)
            for way in (0, 1):
                half_copy(1, col, i, way, s).start()
        return carry

    lax.fori_loop(0, RY, first_send, 0)

    def second(k, carry):
        for col in (0, 1):
            i = order(col, k)
            for way in (0, 1):
                t = lax.rem(ring(col) + (RY - 1 if way == 0 else 1), RY)
                s = slab_at(col, t, i)
                rows = pl.ds(half * col, half)
                build(col, s)
                half_copy(1, col, i, way, s).wait_recv()
                part[s, way, rows, :] = part[s, way, rows, :] + h1[col, i, way]
                full_copy(1, col, i, way, s).start()
        return carry

    lax.fori_loop(0, RY, second, 0)

    def own(i, carry):
        for col in (0, 1):
            build(col, slab_at(col, ring(col), i))
        return carry

    lax.fori_loop(0, RY, own, 0)

    def pack(source, which, target, count):
        def col_block(j, carry):
            cols = pl.ds(pl.multiple_of(j * LB, LB), LB)
            for part_no in (0, 1):
                ref = source.at[which] if which is not None else source
                high, low = split(ref[part_no, :, cols])
                target[j, :, part_no * LB : (part_no + 1) * LB] = high
                target[j, :, (2 + part_no) * LB : (3 + part_no) * LB] = low
            return carry

        lax.fori_loop(0, count, col_block, 0)

    @pl.when(core == 1)
    def _():
        load_down.wait()
        pack(pan, 0, wd.at[1], trace // LB)

    @pl.when(core == 0)
    def _():
        panel_copy(1).start()


    def gather(k, carry):
        for col in (0, 1):
            i = order(col, k)
            s = slab_at(col, ring(col), i)
            rows = pl.ds(half * col, half)
            for way in (0, 1):
                full_copy(1, col, i, way, s).wait_recv()
            part[s, :, rows, :] = part[s, :, rows, :] + (f1[col, i, 0] + f1[col, i, 1])
        return carry

    lax.fori_loop(0, 1, gather, 0)
    for col in (0, 1):
        i = lax.rem(cross(col) + 2, RY)
        s = slab_at(col, ring(col), i)
        for way in (0, 1):
            half_copy(2, col, i, way, s).start()
    lax.fori_loop(1, RY, gather, 0)
    for col in (0, 1):
        rows = pl.ds(half * col, half)
        for way in (0, 1):
            i = lax.rem(cross(col) + (RY - 1 if way == 0 else 1), RY)
            s = slab_at(col, ring(col), i)
            half_copy(2, col, i, way, s).wait_recv()
            part[s, way, rows, :] = part[s, way, rows, :] + h2[col, way]
            full_copy(2, col, i, way, s).start()

    @pl.when(core == 1)
    def _():
        panel_copy(0).wait_recv()
        pack(pan, 2, wd.at[0], trace // LB)
        load_up.wait()
        pack(pan, 1, wu.at[1], trace // LB)

    @pl.when(core == 0)
    def _():
        load_rec.wait()
        pack(rec, None, wr, rec.shape[2] // LB)

    @pl.when(lat == 0)
    def _():
        lext[...] = jnp.zeros_like(lext)

    @pl.when(lat == lats - 1)
    def _():
        rext[...] = jnp.zeros_like(rext)

    def source_copy(col):
        rows = pl.ds(half * col, half)
        return remote(src.at[0, :, rows, :], src.at[0, :, rows, :], ss_.at[col], sr_.at[col], "lat", mate)

    for col in (0, 1):
        rows = pl.ds(half * col, half)
        for way in (0, 1):
            full_copy(2, col, 0, way, me).wait_recv()
        total = part[me, :, rows, :] + (f2[col, 0] + f2[col, 1])
        w_re = jnp.tile(wbuf[0, rows, :], (1, places))
        w_im = jnp.tile(wbuf[1, rows, :], (1, places))
        src[core, 0, rows, :] = w_re * total[0] - w_im * total[1]
        src[core, 1, rows, :] = w_re * total[1] + w_im * total[0]

        @pl.when(core == 0)
        def _():
            source_copy(col).start()

    def turn(arrived, target, rows, weight, extra, piece):
        x = jnp.concatenate([arrived[0, rows, :], arrived[1, rows, :]], axis=0)
        high, low = split(x)
        x = jnp.concatenate([high, low], axis=0)
        count = trace // LB
        group = count // NS
        prods = [jnp.dot(x, weight[j], preferred_element_type=F32) for j in range(min(group + 1, count))]
        for k in range(NS):
            for j in range(k * group, (k + 1) * group):
                cols = slice(j * LB, (j + 1) * LB)
                prod = prods[j][: 2 * CH] + prods[j][2 * CH :]
                prod = prod[:, : 2 * LB] + prod[:, 2 * LB :]
                target[0, rows, cols] = prod[:CH, :LB] - prod[CH:, LB:] + extra[0, rows, cols]
                target[1, rows, cols] = prod[:CH, LB:] + prod[CH:, :LB] + extra[1, rows, cols]
            piece(k).start()
            for j in range(len(prods), min(len(prods) + group, count)):
                prods.append(jnp.dot(x, weight[j], preferred_element_type=F32))

    def rows_of(c):
        return pl.ds(pl.multiple_of(c * CH, CH), CH)

    def cols_of(k):
        return pl.ds(0, trace) if k is None else pl.ds(k * (trace // NS), trace // NS)

    def down_copy(c, w, k=None):
        rows, cols = rows_of(c), cols_of(k)
        return remote(
            dbuf.at[w, :, rows, cols],
            drecv.at[w, :, rows, cols],
            ds_,
            dr_.at[w, c],
            "slab",
            lax.rem(me + 1, slabs),
        )

    def up_copy(c, w, k=None):
        rows, cols = rows_of(c), cols_of(k)
        return remote(
            ubuf.at[w, :, rows, cols],
            urecv.at[w, :, rows, cols],
            us_,
            ur_.at[w, c],
            "slab",
            lax.rem(me + slabs - 1, slabs),
        )

    def last_cells(rows, w, h, to):
        return remote(
            ubuf.at[w, :, rows, pl.ds(trace - LB, LB)], lext.at[:, rows, :], ls_, lr_.at[h], "lat", to
        )

    def first_cells(rows, w, h, to):
        send = rs_ if w == 1 else r2s_
        return remote(ubuf.at[w, :, rows, pl.ds(0, LB)], rext.at[:, rows, :], send, rr_.at[h], "lat", to)

    def back_copy(rows, h):
        return remote(ubuf.at[0, :, rows, :], ubuf.at[0, :, rows, :], as_, ar_.at[h], "lat", mate)

    after = lax.rem(lat + 1, lats)
    before2 = lax.rem(lat + lats - 2, lats)

    def finish(c, w):
        rows = rows_of(c)
        h = lax.div(c, nch // 2)

        if w == 0:
            back_copy(rows, h).start()

            @pl.when(lat > 1)
            def _():
                first_cells(rows, 0, h, before2).start()

            lext[:, rows, :] = ubuf[0, :, rows, trace - LB :]
        else:
            first_cells(rows, 1, h, mate).start()

            @pl.when(lat < lats - 1)
            def _():
                last_cells(rows, 1, h, after).start()

    def down(c, carry):
        rows = rows_of(c)
        for w in (1, 0):

            @pl.when(me == 0)
            def _():
                dbuf[w, :, rows, :] = src[w, :, rows, :]
                down_copy(c, w).start()

            @pl.when(me > 0)
            def _():
                down_copy(c, w).wait_recv()
                turn(drecv.at[w], dbuf.at[w], rows, wd.at[w], src.at[w], lambda k: down_copy(c, w, k))

            @pl.when(me == slabs - 1)
            def _():
                ubuf[w, :, rows, :] = dbuf[w, :, rows, :]
                up_copy(c, w).start()
                finish(c, w)

        return carry

    def up(c, carry):
        rows = rows_of(c)
        for w in (1, 0):
            up_copy(c, w).wait_recv()
            turn(urecv.at[w], ubuf.at[w], rows, wu.at[w], dbuf.at[w], lambda k: up_copy(c, w, k))
            finish(c, w)
        return carry

    def late_packs():
        panel_copy(1).wait_recv()
        pack(pan, 3, wu.at[0], trace // LB)
        load_rec.wait()
        pack(rec, None, wr, rec.shape[2] // LB)

    @pl.when(core == 1)
    def _():
        @pl.when(me >= slabs // 2)
        def _():
            late_packs()

        for col in (0, 1):
            source_copy(col).wait_recv()
        lax.fori_loop(0, nch, down, 0)

        @pl.when(me < slabs // 2)
        def _():
            late_packs()

        @pl.when(me < slabs - 1)
        def _():
            lax.fori_loop(0, nch, up, 0)

    load_ff.wait()

    def arrive(h):
        rows = pl.ds(half * h, half)

        @pl.when(core == 0)
        def _():
            back_copy(rows, h).wait_recv()
            first_cells(rows, 1, h, mate).wait_recv()

        @pl.when(jnp.logical_and(core == 0, lat > 0))
        def _():
            last_cells(rows, 1, h, after).wait_recv()

        @pl.when(jnp.logical_and(core == 1, lat < lats - 1))
        def _():
            first_cells(rows, 0, h, before2).wait_recv()

    def place(h, value, first_col):
        width = value.shape[-1]
        for part_no in (0, 1):
            high, low = split(value[part_no])
            xr[h, part_no * half : (part_no + 1) * half, first_col : first_col + width] = high
            xr[h, (2 + part_no) * half : (3 + part_no) * half, first_col : first_col + width] = low

    neb = gbuf.shape[0]

    def recover(h):
        rows = pl.ds(half * h, half)
        place(h, ubuf[core, :, rows, :], LB)
        place(h, lext[:, rows, :], 0)
        place(h, rext[:, rows, :], LB + trace)

        def block(j, carry):
            cols = pl.ds(pl.multiple_of(j * LB, LB), LB)
            prod = jnp.dot(xr[h], wr[j, :, : 2 * LB], preferred_element_type=F32)
            prod = prod[: 2 * half] + prod[2 * half :]
            prod = prod + jnp.dot(xr[h, : 2 * half, :], wr[j, :, 2 * LB :], preferred_element_type=F32)
            re = prod[:half, :LB] - prod[half:, LB:]
            im = prod[:half, LB:] + prod[half:, :LB]
            row = jnp.sum(ff[0, rows, cols] * re + ff[1, rows, cols] * im, axis=0, keepdims=True)
            if h == 0:
                gbuf[pl.ds(j, 1), :] = row
            else:
                gbuf[pl.ds(j, 1), :] = gbuf[pl.ds(j, 1), :] + row
            return carry

        lax.fori_loop(0, neb, block, 0)

    arrive(0)
    recover(0)
    arrive(1)
    leave = pltpu.make_async_copy(ubuf.at[core], u_hbm, load_sem.at[6])
    leave.start()
    recover(1)

    grads = gbuf[...] * (shots ** (-0.5))
    lanes = lax.broadcasted_iota(jnp.int32, gsend.shape[1:], 0)
    placed = []
    for b in range(neb):
        row = jnp.broadcast_to(grads[b : b + 1, :], gsend.shape[1:])
        placed.append(jnp.where(lanes == slot_sm[b], row, 0.0))
    for s in range(slabs):
        total = jnp.zeros(gsend.shape[1:], F32)
        for b in range(neb):
            total = total + placed[b] * jnp.where(own_sm[b] == s, 1.0, 0.0).astype(F32)
        gsend[s] = total

    def grad_copy(to, sender):
        return remote(gsend.at[to], grecv.at[sender], gs_, gr_, "slab", to)

    def grad_send(k, carry):
        grad_copy(lax.rem(me + k, slabs), me).start()
        return carry

    lax.fori_loop(1, slabs, grad_send, 0)
    grecv[me] = gsend[me]

    def sent(ref, sem, axis="slab", where=me):
        remote(ref, ref, sem, sem, axis, where).wait_send()

    sent(h1, h1s)
    sent(f1, f1s)
    sent(h2, h2s)
    sent(f2, f2s)

    @pl.when(core == 1)
    def _():
        sent(dbuf, ds_)
        sent(ubuf, us_)

        @pl.when(me == 0)
        def _():
            for w in (0, 1):
                for c in range(nch):
                    down_copy(c, w).wait_recv()

        @pl.when(me == slabs - 1)
        def _():
            for w in (0, 1):
                for c in range(nch):
                    up_copy(c, w).wait_recv()

        sent(ubuf.at[0], as_)
        sent(rext, rs_)

        @pl.when(lat > 1)
        def _():
            sent(rext, r2s_)

        @pl.when(lat < lats - 1)
        def _():
            sent(lext, ls_)

    @pl.when(core == 0)
    def _():
        for k in (0, 1):
            panel_copy(k).wait_send()
            source_copy(k).wait_send()

    leave.wait()
    all_others = pl.ds(0, slabs - 1)
    remote(gsend.at[all_others], grecv.at[all_others], gs_, gr_, "slab", me).wait_recv()
    total = grecv[0]
    for k in range(1, slabs):
        total = total + grecv[k]
    model_out[...] = total
    sent(gsend.at[all_others], gs_)


def body(
    residual_blocks,
    residual_slab,
    residual_pos,
    shot_ids,
    wavelet,
    down_panel,
    up_panel,
    recovery,
    forward_field,
    element_owner,
    element_slot,
):
    slabs = 16
    nres, _, shots, width = residual_blocks.shape
    trace = down_panel.shape[-1]
    depth, nel = recovery.shape[-2:]
    neb = element_slot.shape[0]
    half = shots // 2
    nch = shots // CH
    smem = pl.BlockSpec(memory_space=pltpu.SMEM)
    vmem = pl.BlockSpec(memory_space=pltpu.VMEM)
    hbm = pl.BlockSpec(memory_space=pl.ANY)
    dma = pltpu.SemaphoreType.DMA
    ups, model = pl.pallas_call(
        kernel,
        out_shape=(
            jax.ShapeDtypeStruct((2, shots, trace), F32),
            jax.ShapeDtypeStruct((neb, width), F32),
        ),
        in_specs=[vmem] * 2 + [smem] * 4 + [hbm] * 5,
        out_specs=(hbm, vmem),
        scratch_shapes=[
            pltpu.VMEM((nres, 2, shots, width), F32),
            pltpu.VMEM((4, 2, trace, trace), F32),
            pltpu.VMEM((2, depth, nel), F32),
            pltpu.VMEM((2, shots, nel), F32),
            pltpu.VMEM((2, trace // width, trace, 4 * width), BF16),
            pltpu.VMEM((2, trace // width, trace, 4 * width), BF16),
            pltpu.VMEM((nel // width, depth, 4 * width), BF16),
            pltpu.VMEM((slabs, 2, shots, trace), F32),
            pltpu.VMEM((2, RY, 2, half, trace), F32),
            pltpu.VMEM((2, RY, 2, 2, half, trace), F32),
            pltpu.VMEM((2, 2, half, trace), F32),
            pltpu.VMEM((2, 2, 2, half, trace), F32),
            pltpu.VMEM((2, 2, shots, trace), F32),
            pltpu.VMEM((2, 2, shots, trace), F32),
            pltpu.VMEM((2, 2, shots, trace), F32),
            pltpu.VMEM((2, 2, shots, trace), F32),
            pltpu.VMEM((2, 2, shots, trace), F32),
            pltpu.VMEM((2, shots, width), F32),
            pltpu.VMEM((2, shots, width), F32),
            pltpu.VMEM((2, 2 * shots, depth), BF16),
            pltpu.VMEM((neb, width), F32),
            pltpu.VMEM((slabs, neb, width), F32),
            pltpu.VMEM((slabs, neb, width), F32),
            pltpu.VMEM((slabs, width), jnp.int32),
            pltpu.SMEM((slabs, width), jnp.int32),
            pltpu.VMEM((2, shots, width), F32),
            dma((7,)),
            dma,
            dma((2, RY, 2)),
            dma,
            dma((2, RY, 2)),
            dma,
            dma((2, 2)),
            dma,
            dma((2, 2)),
            dma,
            dma((2, nch)),
            dma,
            dma((2, nch)),
            dma,
            dma((2,)),
            dma,
            dma,
            dma((2,)),
            dma,
            dma((2,)),
            dma,
            dma,
            dma((2,)),
            dma((2,)),
            dma((2,)),
            dma((2,)),
        ],
        compiler_params=pltpu.CompilerParams(
            collective_id=0, has_side_effects=True, vmem_limit_bytes=60 * 1024 * 1024
        ),
    )(
        residual_slab.reshape(1, -1),
        residual_pos.reshape(1, -1),
        element_owner.reshape(-1),
        element_slot,
        shot_ids,
        wavelet.T,
        residual_blocks,
        down_panel[0, 0],
        up_panel[0, 0],
        recovery[0, 0],
        forward_field[0, 0],
    )
    return (ups[None, None], model[None, None])


def solution(mesh):
    placed = (
        P(("slab", "lat"), None, None, None),
        P(("slab", "lat"), None),
        P(("slab", "lat")),
        P(),
        P(),
        P("slab", "lat", None, None, None),
        P("slab", "lat", None, None, None),
        P("slab", "lat", None, None, None),
        P("slab", "lat", None, None, None),
        P(("slab", "lat"), None),
        P(("slab", "lat")),
    )
    return jax.shard_map(
        body,
        mesh=mesh,
        in_specs=placed,
        out_specs=(P("slab", "lat", None, None, None), P("slab", "lat", None, None)),
        check_vma=False,
    )
```

```python
import functools

import jax
import jax.numpy as jnp
from jax import lax
from jax.experimental import pallas as pl
from jax.experimental.pallas import tpu as pltpu
from jax.sharding import PartitionSpec as P

MESH = pl.DeviceIdType.MESH
F32 = jnp.float32
BF16 = jnp.bfloat16
LB = 128
RY = 4
CAP = 4
CH = 8
VR = 32
VP = 64


def split(value):
    high = value.astype(BF16)
    low = (value - high.astype(F32)).astype(BF16)
    return high, low


def remote(src, dst, send, recv, axis, where):
    return pltpu.make_async_remote_copy(
        src_ref=src,
        dst_ref=dst,
        send_sem=send,
        recv_sem=recv,
        device_id={axis: where},
        device_id_type=MESH,
    )


def kernel(
    slab_v,
    pos_v,
    own_sm,
    slot_sm,
    shot_sm,
    wav_sm,
    res_hbm,
    down_hbm,
    up_hbm,
    rec_hbm,
    ff_hbm,
    u_hbm,
    model_out,
    res,
    pan,
    rec,
    ff,
    wd,
    wz,
    wr,
    part,
    h1,
    f1,
    h2,
    f2,
    src,
    de,
    ubuf,
    drecv,
    urecv,
    lext,
    rext,
    xr,
    gbuf,
    gsend,
    grecv,
    tab_v,
    tab_sm,
    wbuf,
    upan,
    vland,
    erecv,
    load_sem,
    h1s,
    h1r,
    f1s,
    f1r,
    h2s,
    h2r,
    f2s,
    f2r,
    ds_,
    dr_,
    us_,
    ur_,
    ls_,
    lr_,
    rs_,
    r2s_,
    rr_,
    as_,
    ar_,
    gs_,
    gr_,
    ps_,
    pr_,
    ss_,
    sr_,
    ul_,
    vs_,
    vr_,
    xs_,
    xr_,
    es_,
    er_,
):
    slabs = 16
    lats = 8
    shots, trace = src.shape[2], src.shape[3]
    half = shots // 2
    places = trace // LB
    nres = res.shape[0]
    nch = shots // CH
    me = lax.axis_index("slab")
    lat = lax.axis_index("lat")
    y = lax.rem(me, RY)
    z = lax.div(me, RY)

    core = lax.rem(lat, 2)
    mate = lat + 1 - 2 * core
    top = slabs - RY
    even = lax.rem(me, 2) == 0
    pair = jnp.logical_and(even, me < top)
    leaf = jnp.logical_and(lax.rem(me, 2) == 1, me < top)
    which = jnp.where(pair, 1, 0)
    below = lax.rem(me + slabs - 1, slabs)
    load_res = pltpu.make_async_copy(res_hbm, res, load_sem.at[0])
    load_down = pltpu.make_async_copy(down_hbm, pan.at[0], load_sem.at[1])
    load_up = pltpu.make_async_copy(up_hbm, pan.at[1], load_sem.at[2])
    load_rec = pltpu.make_async_copy(rec_hbm, rec, load_sem.at[3])
    load_ff = pltpu.make_async_copy(ff_hbm, ff, load_sem.at[4])
    load_res.start()

    @pl.when(core == 1)
    def _():
        load_down.start()

    @pl.when(jnp.logical_or(core == 1, pair))
    def _():
        load_up.start()

    load_rec.start()
    load_ff.start()

    barrier = pltpu.get_barrier_semaphore()

    for step in (1, RY - 1):
        for other in (z * RY + lax.rem(y + step, RY), lax.rem(z + step, RY) * RY + y):
            pl.semaphore_signal(barrier, inc=1, device_id={"slab": other}, device_id_type=MESH)

    def meet(step, present):
        @pl.when(present)
        def _():
            pl.semaphore_signal(barrier, inc=1, device_id={"lat": lat + step}, device_id_type=MESH)

    meet(-1, lat > 0)
    meet(1, lat < lats - 1)
    meet(-2, jnp.logical_and(core == 1, lat > 1))
    meet(2, jnp.logical_and(core == 1, lat < lats - 1))

    rows_no = lax.broadcasted_iota(jnp.int32, (1, nres), 1)
    match = slab_v[...] == lax.broadcasted_iota(jnp.int32, (slabs, nres), 0)
    hits = jnp.where(match, 1.0, 0.0).astype(F32)
    before = lax.broadcasted_iota(jnp.int32, (nres, nres), 0) < lax.broadcasted_iota(jnp.int32, (nres, nres), 1)
    rank = jnp.dot(hits.astype(BF16), jnp.where(before, 1.0, 0.0).astype(BF16), preferred_element_type=F32)
    code = (rows_no * 8 + pos_v[...]).astype(F32)
    found = jnp.sum(hits, axis=1, keepdims=True)
    lane = lax.broadcasted_iota(jnp.int32, tab_v.shape, 1)
    table = jnp.zeros(tab_v.shape, F32)
    for c in range(CAP):
        value = jnp.sum(jnp.where(rank == c, hits * code, 0.0), axis=1, keepdims=True)
        value = jnp.where(found > c, value, 7.0)
        table = table + jnp.where(lane == c, value, 0.0)
    tab_v[...] = table.astype(jnp.int32)
    load_tab = pltpu.make_async_copy(tab_v, tab_sm, load_sem.at[5])
    load_tab.start()

    def weight_row(j, carry):
        for part_no in (0, 1):
            wbuf[part_no, pl.ds(j, 1), :] = jnp.full((1, LB), wav_sm[part_no, shot_sm[j]], F32)
        return carry

    lax.fori_loop(0, shots, weight_row, 0, unroll=8)
    load_tab.wait()

    def ring(col):
        return y if col == 0 else z

    def cross(col):
        return z if col == 0 else y

    def slab_at(col, t, i):
        return i * RY + t if col == 0 else t * RY + i

    def order(col, k):
        off = jnp.where(k < 2, 2 - k, 3 * (3 - k))
        return lax.rem(cross(col) + off, RY)

    def build(col, s):
        rows = pl.ds(half * col, half)
        codes = [tab_sm[s, c] for c in range(CAP)]
        blocks = [res[lax.bitwise_and(lax.shift_right_logical(code, 3), nres - 1), :, rows, :] for code in codes]
        spots = [lax.bitwise_and(code, 7) for code in codes]
        for p in range(places):
            total = blocks[0] * jnp.where(spots[0] == p, 1.0, 0.0).astype(F32)
            for c in range(1, CAP):
                total = total + blocks[c] * jnp.where(spots[c] == p, 1.0, 0.0).astype(F32)
            part[s, :, rows, p * LB : (p + 1) * LB] = total

    def half_copy(stage, col, i, way, s):
        rows = pl.ds(half * col, half)
        a, b = ring(col), cross(col)
        if stage == 1:
            to = lax.rem(a + (RY - 1 if way == 0 else 1), RY)
            where = slab_at(col, to, b)
            return remote(
                part.at[s, way, rows, :], h1.at[col, i, way], h1s, h1r.at[col, i, way], "slab", where
            )
        to = lax.rem(b + (RY - 1 if way == 0 else 1), RY)
        where = slab_at(col, a, to)
        return remote(part.at[s, way, rows, :], h2.at[col, way], h2s, h2r.at[col, way], "slab", where)

    def full_copy(stage, col, i, way, s):
        rows = pl.ds(half * col, half)
        a, b = ring(col), cross(col)
        if stage == 1:
            to = lax.rem(a + (RY - 1 if way == 0 else 1), RY)
            where = slab_at(col, to, b)
            return remote(
                part.at[s, :, rows, :], f1.at[col, i, way], f1s, f1r.at[col, i, way], "slab", where
            )
        to = lax.rem(b + (RY - 1 if way == 0 else 1), RY)
        where = slab_at(col, a, to)
        return remote(part.at[s, :, rows, :], f2.at[col, way], f2s, f2r.at[col, way], "slab", where)

    load_res.wait()

    def first(k, carry):
        for col in (0, 1):
            i = order(col, k)
            s = slab_at(col, lax.rem(ring(col) + 2, RY), i)
            build(col, s)
        return carry

    lax.fori_loop(0, RY, first, 0)
    peers = 4 + (lat > 0).astype(jnp.int32) + (lat < lats - 1).astype(jnp.int32)
    peers = peers + core * ((lat > 1).astype(jnp.int32) + (lat < lats - 1).astype(jnp.int32))
    pl.semaphore_wait(barrier, peers)

    def panel_copy(which):
        ref = down_hbm if which == 0 else up_hbm
        return remote(ref, pan.at[2 + which], ps_.at[which], pr_.at[which], "lat", mate)

    @pl.when(core == 0)
    def _():
        panel_copy(0).start()

    def first_send(k, carry):
        for col in (0, 1):
            i = order(col, k)
            s = slab_at(col, lax.rem(ring(col) + 2, RY), i)
            for way in (0, 1):
                half_copy(1, col, i, way, s).start()
        return carry

    lax.fori_loop(0, RY, first_send, 0)

    def second(k, carry):
        for col in (0, 1):
            i = order(col, k)
            for way in (0, 1):
                t = lax.rem(ring(col) + (RY - 1 if way == 0 else 1), RY)
                s = slab_at(col, t, i)
                rows = pl.ds(half * col, half)
                build(col, s)
                half_copy(1, col, i, way, s).wait_recv()
                part[s, way, rows, :] = part[s, way, rows, :] + h1[col, i, way]
                full_copy(1, col, i, way, s).start()
        return carry

    lax.fori_loop(0, RY, second, 0)

    def own(i, carry):
        for col in (0, 1):
            build(col, slab_at(col, ring(col), i))
        return carry

    lax.fori_loop(0, RY, own, 0)

    def pack(source, which, target, count):
        def col_block(j, carry):
            cols = pl.ds(pl.multiple_of(j * LB, LB), LB)
            for part_no in (0, 1):
                ref = source.at[which] if which is not None else source
                high, low = split(ref[part_no, :, cols])
                target[j, :, part_no * LB : (part_no + 1) * LB] = high
                target[j, :, (2 + part_no) * LB : (3 + part_no) * LB] = low
            return carry

        lax.fori_loop(0, count, col_block, 0)

    @pl.when(core == 1)
    def _():
        load_down.wait()
        pack(pan, 0, wd.at[1], trace // LB)

    @pl.when(core == 0)
    def _():
        panel_copy(1).start()


    def gather(k, carry):
        for col in (0, 1):
            i = order(col, k)
            s = slab_at(col, ring(col), i)
            rows = pl.ds(half * col, half)
            for way in (0, 1):
                full_copy(1, col, i, way, s).wait_recv()
            part[s, :, rows, :] = part[s, :, rows, :] + (f1[col, i, 0] + f1[col, i, 1])
        return carry

    lax.fori_loop(0, 1, gather, 0)
    for col in (0, 1):
        i = lax.rem(cross(col) + 2, RY)
        s = slab_at(col, ring(col), i)
        for way in (0, 1):
            half_copy(2, col, i, way, s).start()
    lax.fori_loop(1, RY, gather, 0)
    for col in (0, 1):
        rows = pl.ds(half * col, half)
        for way in (0, 1):
            i = lax.rem(cross(col) + (RY - 1 if way == 0 else 1), RY)
            s = slab_at(col, ring(col), i)
            half_copy(2, col, i, way, s).wait_recv()
            part[s, way, rows, :] = part[s, way, rows, :] + h2[col, way]
            full_copy(2, col, i, way, s).start()

    def piece_copy(b):
        rows = pl.ds(pl.multiple_of(b * VP, VP), VP)
        return remote(up_hbm.at[:, rows, :], upan.at[:, rows, :], vs_, vr_.at[b], "slab", below)

    @pl.when(leaf)
    def _():
        for b in range(trace // VP):
            piece_copy(b).start()

    @pl.when(core == 1)
    def _():
        panel_copy(0).wait_recv()
        pack(pan, 2, wd.at[0], trace // LB)
        load_up.wait()
        pack(pan, 1, wz.at[0, 1], trace // LB)

    @pl.when(core == 0)
    def _():
        load_rec.wait()
        pack(rec, None, wr, rec.shape[2] // LB)

        @pl.when(pair)
        def _():
            load_up.wait()
            pack(pan, 1, wz.at[0, 0], trace // LB)

    @pl.when(lat == 0)
    def _():
        lext[...] = jnp.zeros_like(lext)

    @pl.when(lat == lats - 1)
    def _():
        rext[...] = jnp.zeros_like(rext)

    def source_copy(col):
        rows = pl.ds(half * col, half)
        return remote(src.at[0, :, rows, :], src.at[0, :, rows, :], ss_.at[col], sr_.at[col], "lat", mate)

    for col in (0, 1):
        rows = pl.ds(half * col, half)
        for way in (0, 1):
            full_copy(2, col, 0, way, me).wait_recv()
        total = part[me, :, rows, :] + (f2[col, 0] + f2[col, 1])
        w_re = jnp.tile(wbuf[0, rows, :], (1, places))
        w_im = jnp.tile(wbuf[1, rows, :], (1, places))
        src[core, 0, rows, :] = w_re * total[0] - w_im * total[1]
        src[core, 1, rows, :] = w_re * total[1] + w_im * total[0]

        @pl.when(core == 0)
        def _():
            source_copy(col).start()

    def product(first, second, weight, j):
        count = first.shape[0]
        high, low = split(jnp.concatenate([first, second], axis=0))
        x = jnp.concatenate([high, low], axis=0)
        prod = jnp.dot(x, weight[j], preferred_element_type=F32)
        prod = prod[: 2 * count] + prod[2 * count :]
        prod = prod[:, : 2 * LB] + prod[:, 2 * LB :]
        return prod[:count, :LB] - prod[count:, LB:], prod[:count, LB:] + prod[count:, :LB]

    def turn(arrived, target, rows, weight, extra):
        first, second = arrived[0, rows, :], arrived[1, rows, :]
        for j in range(trace // LB):
            cols = slice(j * LB, (j + 1) * LB)
            re, im = product(first, second, weight, j)
            target[0, rows, cols] = re + extra[0, rows, cols]
            target[1, rows, cols] = im + extra[1, rows, cols]

    def rows_of(c):
        return pl.ds(pl.multiple_of(c * CH, CH), CH)

    def down_copy(c, w):
        rows = rows_of(c)
        return remote(
            de.at[0, w, :, rows, :], drecv.at[w, :, rows, :], ds_, dr_.at[w, c], "slab", lax.rem(me + 1, slabs)
        )

    has_chain = jnp.logical_or(me > top, jnp.logical_and(even, me > 0))
    has_leaf = jnp.logical_and(even, jnp.logical_and(me > 0, me <= top))

    def up_copy(c, w, to_leaf=False):
        rows = rows_of(c)
        step = jnp.where(me > top, 1, 2)
        to = below if to_leaf else lax.rem(me + slabs - step, slabs)
        send = ul_ if to_leaf else us_
        return remote(ubuf.at[w, :, rows, :], urecv.at[w, :, rows, :], send, ur_.at[w, c], "slab", to)

    def last_cells(rows, w, h, to):
        return remote(
            ubuf.at[w, :, rows, pl.ds(trace - LB, LB)], lext.at[:, rows, :], ls_, lr_.at[h], "lat", to
        )

    def first_cells(rows, w, h, to):
        send = rs_ if w == 1 else r2s_
        return remote(ubuf.at[w, :, rows, pl.ds(0, LB)], rext.at[:, rows, :], send, rr_.at[h], "lat", to)

    def back_copy(rows, h):
        return remote(ubuf.at[0, :, rows, :], ubuf.at[0, :, rows, :], as_, ar_.at[h], "lat", mate)

    after = lax.rem(lat + 1, lats)
    before2 = lax.rem(lat + lats - 2, lats)

    def finish(c, w):
        rows = rows_of(c)
        h = lax.div(c, nch // 2)

        @pl.when(has_chain)
        def _():
            up_copy(c, w).start()

        @pl.when(has_leaf)
        def _():
            up_copy(c, w, True).start()

        if w == 0:
            back_copy(rows, h).start()

            @pl.when(lat > 1)
            def _():
                first_cells(rows, 0, h, before2).start()

            lext[:, rows, :] = ubuf[0, :, rows, trace - LB :]
        else:
            first_cells(rows, 1, h, mate).start()

            @pl.when(lat < lats - 1)
            def _():
                last_cells(rows, 1, h, after).start()

    def down(c, carry):
        rows = rows_of(c)
        for w in (1, 0):

            @pl.when(me == 0)
            def _():
                de[0, w, :, rows, :] = src[w, :, rows, :]

            @pl.when(me > 0)
            def _():
                down_copy(c, w).wait_recv()
                turn(drecv.at[w], de.at[0, w], rows, wd.at[w], src.at[w])

            @pl.when(me < slabs - 1)
            def _():
                down_copy(c, w).start()

            @pl.when(me == slabs - 1)
            def _():
                ubuf[w, :, rows, :] = de[0, w, :, rows, :]
                finish(c, w)

        return carry

    def up(c, carry):
        rows = rows_of(c)
        for w in (1, 0):
            up_copy(c, w).wait_recv()
            turn(urecv.at[w], ubuf.at[w], rows, wz.at[which, w], de.at[which, w])
            finish(c, w)
        return carry

    def give_copy(b):
        rows = pl.ds(pl.multiple_of(b * VP, VP), VP)
        return remote(vland.at[:, rows, :], vland.at[:, rows, :], xs_, xr_, "lat", mate)

    def form(store, done):
        def piece(b, carry):
            piece_copy(b).wait_recv()

            def block(k, carry):
                rows = pl.ds(pl.multiple_of(b * VP + k * VR, VR), VR)
                first, second = upan[0, rows, :], upan[1, rows, :]
                for j in range(trace // LB):
                    re, im = product(first, second, wz.at[0, core], j)
                    store(j, rows, re, im)
                return carry

            lax.fori_loop(0, VP // VR, block, 0)
            done(b)
            return carry

        lax.fori_loop(0, trace // VP, piece, 0)

    def store_packed(j, rows, re, im):
        for part_no, value in enumerate((re, im)):
            high, low = split(value)
            wz[1, 1, j, rows, part_no * LB : (part_no + 1) * LB] = high
            wz[1, 1, j, rows, (2 + part_no) * LB : (3 + part_no) * LB] = low

    def store_plain(j, rows, re, im):
        vland[0, rows, j * LB : (j + 1) * LB] = re
        vland[1, rows, j * LB : (j + 1) * LB] = im

    def odd_copy(w):
        return remote(de.at[0, w], erecv.at[w], es_, er_.at[w], "slab", below)

    @pl.when(jnp.logical_and(core == 0, pair))
    def _():
        form(store_plain, lambda b: give_copy(b).start())

    def late_packs():
        panel_copy(1).wait_recv()
        pack(pan, 3, wz.at[0, 0], trace // LB)
        load_rec.wait()
        pack(rec, None, wr, rec.shape[2] // LB)

    @pl.when(core == 1)
    def _():
        @pl.when(me >= slabs // 2)
        def _():
            late_packs()

        for col in (0, 1):
            source_copy(col).wait_recv()
        lax.fori_loop(0, nch, down, 0)

        @pl.when(leaf)
        def _():
            for w in (1, 0):
                odd_copy(w).start()

        @pl.when(me < slabs // 2)
        def _():
            late_packs()

        @pl.when(pair)
        def _():
            form(store_packed, lambda b: None)
            remote(vland, vland, xs_, xr_, "lat", mate).wait_recv()
            pack(vland, None, wz.at[1, 0], trace // LB)
            for w in (1, 0):
                odd_copy(w).wait_recv()

                def two(k, carry):
                    rows = pl.ds(pl.multiple_of(k * VR, VR), VR)
                    turn(erecv.at[w], de.at[1, w], rows, wz.at[0, w], de.at[0, w])
                    return carry

                lax.fori_loop(0, shots // VR, two, 0)

        @pl.when(me < slabs - 1)
        def _():
            lax.fori_loop(0, nch, up, 0)

    load_ff.wait()

    def arrive(h):
        rows = pl.ds(half * h, half)

        @pl.when(core == 0)
        def _():
            back_copy(rows, h).wait_recv()
            first_cells(rows, 1, h, mate).wait_recv()

        @pl.when(jnp.logical_and(core == 0, lat > 0))
        def _():
            last_cells(rows, 1, h, after).wait_recv()

        @pl.when(jnp.logical_and(core == 1, lat < lats - 1))
        def _():
            first_cells(rows, 0, h, before2).wait_recv()

    def place(h, value, first_col):
        width = value.shape[-1]
        for part_no in (0, 1):
            high, low = split(value[part_no])
            xr[h, part_no * half : (part_no + 1) * half, first_col : first_col + width] = high
            xr[h, (2 + part_no) * half : (3 + part_no) * half, first_col : first_col + width] = low

    neb = gbuf.shape[0]

    def recover(h):
        rows = pl.ds(half * h, half)
        place(h, ubuf[core, :, rows, :], LB)
        place(h, lext[:, rows, :], 0)
        place(h, rext[:, rows, :], LB + trace)

        def block(j, carry):
            cols = pl.ds(pl.multiple_of(j * LB, LB), LB)
            prod = jnp.dot(xr[h], wr[j, :, : 2 * LB], preferred_element_type=F32)
            prod = prod[: 2 * half] + prod[2 * half :]
            prod = prod + jnp.dot(xr[h, : 2 * half, :], wr[j, :, 2 * LB :], preferred_element_type=F32)
            re = prod[:half, :LB] - prod[half:, LB:]
            im = prod[:half, LB:] + prod[half:, :LB]
            row = jnp.sum(ff[0, rows, cols] * re + ff[1, rows, cols] * im, axis=0, keepdims=True)
            if h == 0:
                gbuf[pl.ds(j, 1), :] = row
            else:
                gbuf[pl.ds(j, 1), :] = gbuf[pl.ds(j, 1), :] + row
            return carry

        lax.fori_loop(0, neb, block, 0)

    arrive(0)
    recover(0)
    arrive(1)
    leave = pltpu.make_async_copy(ubuf.at[core], u_hbm, load_sem.at[6])
    leave.start()
    recover(1)

    grads = gbuf[...] * (shots ** (-0.5))
    lanes = lax.broadcasted_iota(jnp.int32, gsend.shape[1:], 0)
    placed = []
    for b in range(neb):
        row = jnp.broadcast_to(grads[b : b + 1, :], gsend.shape[1:])
        placed.append(jnp.where(lanes == slot_sm[b], row, 0.0))
    for s in range(slabs):
        total = jnp.zeros(gsend.shape[1:], F32)
        for b in range(neb):
            total = total + placed[b] * jnp.where(own_sm[b] == s, 1.0, 0.0).astype(F32)
        gsend[s] = total

    def grad_copy(to, sender):
        return remote(gsend.at[to], grecv.at[sender], gs_, gr_, "slab", to)

    def grad_send(k, carry):
        grad_copy(lax.rem(me + k, slabs), me).start()
        return carry

    lax.fori_loop(1, slabs, grad_send, 0)
    grecv[me] = gsend[me]

    def sent(ref, sem, axis="slab", where=me):
        remote(ref, ref, sem, sem, axis, where).wait_send()

    @pl.when(leaf)
    def _():
        sent(upan, vs_)

    @pl.when(jnp.logical_and(core == 0, pair))
    def _():
        sent(vland, xs_)

    sent(h1, h1s)
    sent(f1, f1s)
    sent(h2, h2s)
    sent(f2, f2s)

    @pl.when(core == 1)
    def _():
        @pl.when(me < slabs - 1)
        def _():
            sent(de.at[0], ds_)

        @pl.when(has_chain)
        def _():
            sent(ubuf, us_)

        @pl.when(has_leaf)
        def _():
            sent(ubuf, ul_)

        @pl.when(leaf)
        def _():
            sent(de.at[0], es_)

        sent(ubuf.at[0], as_)
        sent(rext, rs_)

        @pl.when(lat > 1)
        def _():
            sent(rext, r2s_)

        @pl.when(lat < lats - 1)
        def _():
            sent(lext, ls_)

    @pl.when(core == 0)
    def _():
        for k in (0, 1):
            panel_copy(k).wait_send()
            source_copy(k).wait_send()

    leave.wait()
    all_others = pl.ds(0, slabs - 1)
    remote(gsend.at[all_others], grecv.at[all_others], gs_, gr_, "slab", me).wait_recv()
    total = grecv[0]
    for k in range(1, slabs):
        total = total + grecv[k]
    model_out[...] = total
    sent(gsend.at[all_others], gs_)


def body(
    residual_blocks,
    residual_slab,
    residual_pos,
    shot_ids,
    wavelet,
    down_panel,
    up_panel,
    recovery,
    forward_field,
    element_owner,
    element_slot,
):
    slabs = 16
    nres, _, shots, width = residual_blocks.shape
    trace = down_panel.shape[-1]
    depth, nel = recovery.shape[-2:]
    neb = element_slot.shape[0]
    half = shots // 2
    nch = shots // CH
    smem = pl.BlockSpec(memory_space=pltpu.SMEM)
    vmem = pl.BlockSpec(memory_space=pltpu.VMEM)
    hbm = pl.BlockSpec(memory_space=pl.ANY)
    dma = pltpu.SemaphoreType.DMA
    ups, model = pl.pallas_call(
        kernel,
        out_shape=(
            jax.ShapeDtypeStruct((2, shots, trace), F32),
            jax.ShapeDtypeStruct((neb, width), F32),
        ),
        in_specs=[vmem] * 2 + [smem] * 4 + [hbm] * 5,
        out_specs=(hbm, vmem),
        scratch_shapes=[
            pltpu.VMEM((nres, 2, shots, width), F32),
            pltpu.VMEM((4, 2, trace, trace), F32),
            pltpu.VMEM((2, depth, nel), F32),
            pltpu.VMEM((2, shots, nel), F32),
            pltpu.VMEM((2, trace // width, trace, 4 * width), BF16),
            pltpu.VMEM((2, 2, trace // width, trace, 4 * width), BF16),
            pltpu.VMEM((nel // width, depth, 4 * width), BF16),
            pltpu.VMEM((slabs, 2, shots, trace), F32),
            pltpu.VMEM((2, RY, 2, half, trace), F32),
            pltpu.VMEM((2, RY, 2, 2, half, trace), F32),
            pltpu.VMEM((2, 2, half, trace), F32),
            pltpu.VMEM((2, 2, 2, half, trace), F32),
            pltpu.VMEM((2, 2, shots, trace), F32),
            pltpu.VMEM((2, 2, 2, shots, trace), F32),
            pltpu.VMEM((2, 2, shots, trace), F32),
            pltpu.VMEM((2, 2, shots, trace), F32),
            pltpu.VMEM((2, 2, shots, trace), F32),
            pltpu.VMEM((2, shots, width), F32),
            pltpu.VMEM((2, shots, width), F32),
            pltpu.VMEM((2, 2 * shots, depth), BF16),
            pltpu.VMEM((neb, width), F32),
            pltpu.VMEM((slabs, neb, width), F32),
            pltpu.VMEM((slabs, neb, width), F32),
            pltpu.VMEM((slabs, width), jnp.int32),
            pltpu.SMEM((slabs, width), jnp.int32),
            pltpu.VMEM((2, shots, width), F32),
            pltpu.VMEM((2, trace, trace), F32),
            pltpu.VMEM((2, trace, trace), F32),
            pltpu.VMEM((2, 2, shots, trace), F32),
            dma((7,)),
            dma,
            dma((2, RY, 2)),
            dma,
            dma((2, RY, 2)),
            dma,
            dma((2, 2)),
            dma,
            dma((2, 2)),
            dma,
            dma((2, nch)),
            dma,
            dma((2, nch)),
            dma,
            dma((2,)),
            dma,
            dma,
            dma((2,)),
            dma,
            dma((2,)),
            dma,
            dma,
            dma((2,)),
            dma((2,)),
            dma((2,)),
            dma((2,)),
            dma,
            dma,
            dma((trace // VP,)),
            dma,
            dma,
            dma,
            dma((2,)),
        ],
        compiler_params=pltpu.CompilerParams(
            collective_id=0, has_side_effects=True, vmem_limit_bytes=60 * 1024 * 1024
        ),
    )(
        residual_slab.reshape(1, -1),
        residual_pos.reshape(1, -1),
        element_owner.reshape(-1),
        element_slot,
        shot_ids,
        wavelet.T,
        residual_blocks,
        down_panel[0, 0],
        up_panel[0, 0],
        recovery[0, 0],
        forward_field[0, 0],
    )
    return (ups[None, None], model[None, None])


def solution(mesh):
    placed = (
        P(("slab", "lat"), None, None, None),
        P(("slab", "lat"), None),
        P(("slab", "lat")),
        P(),
        P(),
        P("slab", "lat", None, None, None),
        P("slab", "lat", None, None, None),
        P("slab", "lat", None, None, None),
        P("slab", "lat", None, None, None),
        P(("slab", "lat"), None),
        P(("slab", "lat")),
    )
    return jax.shard_map(
        body,
        mesh=mesh,
        in_specs=placed,
        out_specs=(P("slab", "lat", None, None, None), P("slab", "lat", None, None)),
        check_vma=False,
    )
```

```python
import functools

import jax
import jax.numpy as jnp
from jax import lax
from jax.experimental import pallas as pl
from jax.experimental.pallas import tpu as pltpu
from jax.sharding import PartitionSpec as P

MESH = pl.DeviceIdType.MESH
F32 = jnp.float32
BF16 = jnp.bfloat16
LB = 128
RY = 4
CAP = 4
CH = 8
VR = 32
VP = 64


def split(value):
    high = value.astype(BF16)
    low = (value - high.astype(F32)).astype(BF16)
    return high, low


def remote(src, dst, send, recv, axis, where):
    return pltpu.make_async_remote_copy(
        src_ref=src,
        dst_ref=dst,
        send_sem=send,
        recv_sem=recv,
        device_id={axis: where},
        device_id_type=MESH,
    )


def kernel(
    slab_v,
    pos_v,
    own_sm,
    slot_sm,
    shot_sm,
    wav_sm,
    res_hbm,
    down_hbm,
    up_hbm,
    rec_hbm,
    ff_hbm,
    u_hbm,
    model_out,
    res,
    pan,
    rec,
    ff,
    wd,
    wz,
    wr,
    part,
    h1,
    f1,
    h2,
    f2,
    src,
    de,
    ubuf,
    drecv,
    urecv,
    lext,
    rext,
    xr,
    gbuf,
    gsend,
    grecv,
    tab_v,
    tab_sm,
    wbuf,
    upan,
    vland,
    erecv,
    load_sem,
    h1s,
    h1r,
    f1s,
    f1r,
    h2s,
    h2r,
    f2s,
    f2r,
    ds_,
    dr_,
    us_,
    ur_,
    ls_,
    lr_,
    rs_,
    r2s_,
    rr_,
    as_,
    ar_,
    gs_,
    gr_,
    ps_,
    pr_,
    ss_,
    sr_,
    ul_,
    vs_,
    vr_,
    xs_,
    xr_,
    es_,
    er_,
):
    slabs = 16
    lats = 8
    shots, trace = src.shape[2], src.shape[3]
    half = shots // 2
    places = trace // LB
    nres = res.shape[0]
    nch = shots // CH
    me = lax.axis_index("slab")
    lat = lax.axis_index("lat")
    y = lax.rem(me, RY)
    z = lax.div(me, RY)

    core = lax.rem(lat, 2)
    mate = lat + 1 - 2 * core
    top = slabs - RY
    even = lax.rem(me, 2) == 0
    pair = jnp.logical_and(even, me < top)
    leaf = jnp.logical_and(lax.rem(me, 2) == 1, me < top)
    which = jnp.where(pair, 1, 0)
    below = lax.rem(me + slabs - 1, slabs)
    load_res = pltpu.make_async_copy(res_hbm, res, load_sem.at[0])
    load_down = pltpu.make_async_copy(down_hbm, pan.at[0], load_sem.at[1])
    load_up = pltpu.make_async_copy(up_hbm, pan.at[1], load_sem.at[2])
    load_rec = pltpu.make_async_copy(rec_hbm, rec, load_sem.at[3])
    load_ff = pltpu.make_async_copy(ff_hbm, ff, load_sem.at[4])
    load_res.start()

    @pl.when(core == 1)
    def _():
        load_down.start()

    @pl.when(jnp.logical_or(core == 1, pair))
    def _():
        load_up.start()

    load_rec.start()
    load_ff.start()

    barrier = pltpu.get_barrier_semaphore()

    for step in (1, RY - 1):
        for other in (z * RY + lax.rem(y + step, RY), lax.rem(z + step, RY) * RY + y):
            pl.semaphore_signal(barrier, inc=1, device_id={"slab": other}, device_id_type=MESH)

    def meet(step, present):
        @pl.when(present)
        def _():
            pl.semaphore_signal(barrier, inc=1, device_id={"lat": lat + step}, device_id_type=MESH)

    meet(-1, lat > 0)
    meet(1, lat < lats - 1)
    meet(-2, jnp.logical_and(core == 1, lat > 1))
    meet(2, jnp.logical_and(core == 1, lat < lats - 1))

    rows_no = lax.broadcasted_iota(jnp.int32, (1, nres), 1)
    match = slab_v[...] == lax.broadcasted_iota(jnp.int32, (slabs, nres), 0)
    hits = jnp.where(match, 1.0, 0.0).astype(F32)
    before = lax.broadcasted_iota(jnp.int32, (nres, nres), 0) < lax.broadcasted_iota(jnp.int32, (nres, nres), 1)
    rank = jnp.dot(hits.astype(BF16), jnp.where(before, 1.0, 0.0).astype(BF16), preferred_element_type=F32)
    code = (rows_no * 8 + pos_v[...]).astype(F32)
    found = jnp.sum(hits, axis=1, keepdims=True)
    lane = lax.broadcasted_iota(jnp.int32, tab_v.shape, 1)
    table = jnp.zeros(tab_v.shape, F32)
    for c in range(CAP):
        value = jnp.sum(jnp.where(rank == c, hits * code, 0.0), axis=1, keepdims=True)
        value = jnp.where(found > c, value, 7.0)
        table = table + jnp.where(lane == c, value, 0.0)
    tab_v[...] = table.astype(jnp.int32)
    load_tab = pltpu.make_async_copy(tab_v, tab_sm, load_sem.at[5])
    load_tab.start()

    def weight_row(j, carry):
        for part_no in (0, 1):
            wbuf[part_no, pl.ds(j, 1), :] = jnp.full((1, LB), wav_sm[part_no, shot_sm[j]], F32)
        return carry

    lax.fori_loop(0, shots, weight_row, 0, unroll=8)
    load_tab.wait()

    def ring(col):
        return y if col == 0 else z

    def cross(col):
        return z if col == 0 else y

    def slab_at(col, t, i):
        return i * RY + t if col == 0 else t * RY + i

    def order(col, k):
        off = jnp.where(k < 2, 2 - k, 3 * (3 - k))
        return lax.rem(cross(col) + off, RY)

    def build(col, s):
        rows = pl.ds(half * col, half)
        codes = [tab_sm[s, c] for c in range(CAP)]
        blocks = [res[lax.bitwise_and(lax.shift_right_logical(code, 3), nres - 1), :, rows, :] for code in codes]
        spots = [lax.bitwise_and(code, 7) for code in codes]
        for p in range(places):
            total = blocks[0] * jnp.where(spots[0] == p, 1.0, 0.0).astype(F32)
            for c in range(1, CAP):
                total = total + blocks[c] * jnp.where(spots[c] == p, 1.0, 0.0).astype(F32)
            part[s, :, rows, p * LB : (p + 1) * LB] = total

    def half_copy(stage, col, i, way, s):
        rows = pl.ds(half * col, half)
        a, b = ring(col), cross(col)
        if stage == 1:
            to = lax.rem(a + (RY - 1 if way == 0 else 1), RY)
            where = slab_at(col, to, b)
            return remote(
                part.at[s, way, rows, :], h1.at[col, i, way], h1s, h1r.at[col, i, way], "slab", where
            )
        to = lax.rem(b + (RY - 1 if way == 0 else 1), RY)
        where = slab_at(col, a, to)
        return remote(part.at[s, way, rows, :], h2.at[col, way], h2s, h2r.at[col, way], "slab", where)

    def full_copy(stage, col, i, way, s):
        rows = pl.ds(half * col, half)
        a, b = ring(col), cross(col)
        if stage == 1:
            to = lax.rem(a + (RY - 1 if way == 0 else 1), RY)
            where = slab_at(col, to, b)
            return remote(
                part.at[s, :, rows, :], f1.at[col, i, way], f1s, f1r.at[col, i, way], "slab", where
            )
        to = lax.rem(b + (RY - 1 if way == 0 else 1), RY)
        where = slab_at(col, a, to)
        return remote(part.at[s, :, rows, :], f2.at[col, way], f2s, f2r.at[col, way], "slab", where)

    load_res.wait()

    def first(k, carry):
        for col in (0, 1):
            i = order(col, k)
            s = slab_at(col, lax.rem(ring(col) + 2, RY), i)
            build(col, s)
        return carry

    first(0, 0)
    peers = 4 + (lat > 0).astype(jnp.int32) + (lat < lats - 1).astype(jnp.int32)
    peers = peers + core * ((lat > 1).astype(jnp.int32) + (lat < lats - 1).astype(jnp.int32))
    pl.semaphore_wait(barrier, peers)

    def panel_copy(which):
        ref = down_hbm if which == 0 else up_hbm
        return remote(ref, pan.at[2 + which], ps_.at[which], pr_.at[which], "lat", mate)

    @pl.when(core == 0)
    def _():
        panel_copy(0).start()

    def first_send(k, carry):
        for col in (0, 1):
            i = order(col, k)
            s = slab_at(col, lax.rem(ring(col) + 2, RY), i)
            for way in (0, 1):
                half_copy(1, col, i, way, s).start()
        return carry

    first_send(0, 0)

    def first_rest(k, carry):
        first(k, carry)
        return first_send(k, carry)

    lax.fori_loop(1, RY, first_rest, 0)

    def middle(k, carry):
        for col in (0, 1):
            i = order(col, k)
            for step in (RY - 1, 1, 0):
                build(col, slab_at(col, lax.rem(ring(col) + step, RY), i))
        return carry

    lax.fori_loop(0, RY, middle, 0)

    def second(k, carry):
        for col in (0, 1):
            i = order(col, k)
            for way in (0, 1):
                t = lax.rem(ring(col) + (RY - 1 if way == 0 else 1), RY)
                s = slab_at(col, t, i)
                rows = pl.ds(half * col, half)
                half_copy(1, col, i, way, s).wait_recv()
                part[s, way, rows, :] = part[s, way, rows, :] + h1[col, i, way]
                full_copy(1, col, i, way, s).start()
        return carry

    def gather(k, carry):
        for col in (0, 1):
            i = order(col, k)
            s = slab_at(col, ring(col), i)
            rows = pl.ds(half * col, half)
            for way in (0, 1):
                full_copy(1, col, i, way, s).wait_recv()
            part[s, :, rows, :] = part[s, :, rows, :] + (f1[col, i, 0] + f1[col, i, 1])
        return carry

    lax.fori_loop(0, 2, second, 0)
    gather(0, 0)
    for col in (0, 1):
        i = lax.rem(cross(col) + 2, RY)
        s = slab_at(col, ring(col), i)
        for way in (0, 1):
            half_copy(2, col, i, way, s).start()
    lax.fori_loop(2, RY, second, 0)

    def pack(source, which, target, count):
        def col_block(j, carry):
            cols = pl.ds(pl.multiple_of(j * LB, LB), LB)
            for part_no in (0, 1):
                ref = source.at[which] if which is not None else source
                high, low = split(ref[part_no, :, cols])
                target[j, :, part_no * LB : (part_no + 1) * LB] = high
                target[j, :, (2 + part_no) * LB : (3 + part_no) * LB] = low
            return carry

        lax.fori_loop(0, count, col_block, 0)

    @pl.when(core == 1)
    def _():
        load_down.wait()
        pack(pan, 0, wd.at[1], trace // LB)

    @pl.when(core == 0)
    def _():
        panel_copy(1).start()


    lax.fori_loop(1, RY - 1, gather, 0)
    for col in (0, 1):
        rows = pl.ds(half * col, half)
        for way in (0, 1):
            i = lax.rem(cross(col) + (RY - 1 if way == 0 else 1), RY)
            s = slab_at(col, ring(col), i)
            half_copy(2, col, i, way, s).wait_recv()
            part[s, way, rows, :] = part[s, way, rows, :] + h2[col, way]
            full_copy(2, col, i, way, s).start()
    gather(RY - 1, 0)

    def piece_copy(b):
        rows = pl.ds(pl.multiple_of(b * VP, VP), VP)
        return remote(up_hbm.at[:, rows, :], upan.at[:, rows, :], vs_, vr_.at[b], "slab", below)

    @pl.when(leaf)
    def _():
        for b in range(trace // VP):
            piece_copy(b).start()

    @pl.when(core == 1)
    def _():
        panel_copy(0).wait_recv()
        pack(pan, 2, wd.at[0], trace // LB)
        load_up.wait()
        pack(pan, 1, wz.at[0, 1], trace // LB)

    @pl.when(core == 0)
    def _():
        load_rec.wait()
        pack(rec, None, wr, rec.shape[2] // LB)

        @pl.when(pair)
        def _():
            load_up.wait()
            pack(pan, 1, wz.at[0, 0], trace // LB)

    @pl.when(lat == 0)
    def _():
        lext[...] = jnp.zeros_like(lext)

    @pl.when(lat == lats - 1)
    def _():
        rext[...] = jnp.zeros_like(rext)

    def source_copy(col):
        rows = pl.ds(half * col, half)
        return remote(src.at[0, :, rows, :], src.at[0, :, rows, :], ss_.at[col], sr_.at[col], "lat", mate)

    for col in (0, 1):
        rows = pl.ds(half * col, half)
        for way in (0, 1):
            full_copy(2, col, 0, way, me).wait_recv()
        total = part[me, :, rows, :] + (f2[col, 0] + f2[col, 1])
        w_re = jnp.tile(wbuf[0, rows, :], (1, places))
        w_im = jnp.tile(wbuf[1, rows, :], (1, places))
        src[core, 0, rows, :] = w_re * total[0] - w_im * total[1]
        src[core, 1, rows, :] = w_re * total[1] + w_im * total[0]

        @pl.when(core == 0)
        def _():
            source_copy(col).start()

    def product(first, second, weight, j):
        count = first.shape[0]
        high, low = split(jnp.concatenate([first, second], axis=0))
        x = jnp.concatenate([high, low], axis=0)
        prod = jnp.dot(x, weight[j], preferred_element_type=F32)
        prod = prod[: 2 * count] + prod[2 * count :]
        prod = prod[:, : 2 * LB] + prod[:, 2 * LB :]
        return prod[:count, :LB] - prod[count:, LB:], prod[:count, LB:] + prod[count:, :LB]

    def turn(arrived, target, rows, weight, extra):
        first, second = arrived[0, rows, :], arrived[1, rows, :]
        for j in range(trace // LB):
            cols = slice(j * LB, (j + 1) * LB)
            re, im = product(first, second, weight, j)
            target[0, rows, cols] = re + extra[0, rows, cols]
            target[1, rows, cols] = im + extra[1, rows, cols]

    def rows_of(c):
        return pl.ds(pl.multiple_of(c * CH, CH), CH)

    def down_copy(c, w):
        rows = rows_of(c)
        return remote(
            de.at[0, w, :, rows, :], drecv.at[w, :, rows, :], ds_, dr_.at[w, c], "slab", lax.rem(me + 1, slabs)
        )

    has_chain = jnp.logical_or(me > top, jnp.logical_and(even, me > 0))
    has_leaf = jnp.logical_and(even, jnp.logical_and(me > 0, me <= top))

    def up_copy(c, w, to_leaf=False):
        rows = rows_of(c)
        step = jnp.where(me > top, 1, 2)
        to = below if to_leaf else lax.rem(me + slabs - step, slabs)
        send = ul_ if to_leaf else us_
        return remote(ubuf.at[w, :, rows, :], urecv.at[w, :, rows, :], send, ur_.at[w, c], "slab", to)

    def last_cells(rows, w, h, to):
        return remote(
            ubuf.at[w, :, rows, pl.ds(trace - LB, LB)], lext.at[:, rows, :], ls_, lr_.at[h], "lat", to
        )

    def first_cells(rows, w, h, to):
        send = rs_ if w == 1 else r2s_
        return remote(ubuf.at[w, :, rows, pl.ds(0, LB)], rext.at[:, rows, :], send, rr_.at[h], "lat", to)

    def back_copy(rows, h):
        return remote(ubuf.at[0, :, rows, :], ubuf.at[0, :, rows, :], as_, ar_.at[h], "lat", mate)

    after = lax.rem(lat + 1, lats)
    before2 = lax.rem(lat + lats - 2, lats)

    def finish(c, w):
        rows = rows_of(c)
        h = lax.div(c, nch // 2)

        @pl.when(has_chain)
        def _():
            up_copy(c, w).start()

        @pl.when(has_leaf)
        def _():
            up_copy(c, w, True).start()

        if w == 0:
            back_copy(rows, h).start()

            @pl.when(lat > 1)
            def _():
                first_cells(rows, 0, h, before2).start()

            lext[:, rows, :] = ubuf[0, :, rows, trace - LB :]
        else:
            first_cells(rows, 1, h, mate).start()

            @pl.when(lat < lats - 1)
            def _():
                last_cells(rows, 1, h, after).start()

    def down(c, carry):
        rows = rows_of(c)
        for w in (1, 0):

            @pl.when(me == 0)
            def _():
                de[0, w, :, rows, :] = src[w, :, rows, :]

            @pl.when(me > 0)
            def _():
                down_copy(c, w).wait_recv()
                turn(drecv.at[w], de.at[0, w], rows, wd.at[w], src.at[w])

            @pl.when(me < slabs - 1)
            def _():
                down_copy(c, w).start()

            @pl.when(me == slabs - 1)
            def _():
                ubuf[w, :, rows, :] = de[0, w, :, rows, :]
                finish(c, w)

        return carry

    def up(c, carry):
        rows = rows_of(c)
        for w in (1, 0):
            up_copy(c, w).wait_recv()
            turn(urecv.at[w], ubuf.at[w], rows, wz.at[which, w], de.at[which, w])
            finish(c, w)
        return carry

    def give_copy(b):
        rows = pl.ds(pl.multiple_of(b * VP, VP), VP)
        return remote(vland.at[:, rows, :], vland.at[:, rows, :], xs_, xr_, "lat", mate)

    def form(store, done):
        def piece(b, carry):
            piece_copy(b).wait_recv()

            def block(k, carry):
                rows = pl.ds(pl.multiple_of(b * VP + k * VR, VR), VR)
                first, second = upan[0, rows, :], upan[1, rows, :]
                for j in range(trace // LB):
                    re, im = product(first, second, wz.at[0, core], j)
                    store(j, rows, re, im)
                return carry

            lax.fori_loop(0, VP // VR, block, 0)
            done(b)
            return carry

        lax.fori_loop(0, trace // VP, piece, 0)

    def store_packed(j, rows, re, im):
        for part_no, value in enumerate((re, im)):
            high, low = split(value)
            wz[1, 1, j, rows, part_no * LB : (part_no + 1) * LB] = high
            wz[1, 1, j, rows, (2 + part_no) * LB : (3 + part_no) * LB] = low

    def store_plain(j, rows, re, im):
        vland[0, rows, j * LB : (j + 1) * LB] = re
        vland[1, rows, j * LB : (j + 1) * LB] = im

    def odd_copy(w):
        return remote(de.at[0, w], erecv.at[w], es_, er_.at[w], "slab", below)

    @pl.when(jnp.logical_and(core == 0, pair))
    def _():
        form(store_plain, lambda b: give_copy(b).start())

    def late_packs():
        panel_copy(1).wait_recv()
        pack(pan, 3, wz.at[0, 0], trace // LB)
        load_rec.wait()
        pack(rec, None, wr, rec.shape[2] // LB)

    @pl.when(core == 1)
    def _():
        @pl.when(me >= slabs // 2)
        def _():
            late_packs()

        for col in (0, 1):
            source_copy(col).wait_recv()
        lax.fori_loop(0, nch, down, 0)

        @pl.when(leaf)
        def _():
            for w in (1, 0):
                odd_copy(w).start()

        @pl.when(me < slabs // 2)
        def _():
            late_packs()

        @pl.when(pair)
        def _():
            form(store_packed, lambda b: None)
            remote(vland, vland, xs_, xr_, "lat", mate).wait_recv()
            pack(vland, None, wz.at[1, 0], trace // LB)
            for w in (1, 0):
                odd_copy(w).wait_recv()

                def two(k, carry):
                    rows = pl.ds(pl.multiple_of(k * VR, VR), VR)
                    turn(erecv.at[w], de.at[1, w], rows, wz.at[0, w], de.at[0, w])
                    return carry

                lax.fori_loop(0, shots // VR, two, 0)

        @pl.when(me < slabs - 1)
        def _():
            lax.fori_loop(0, nch, up, 0)

    load_ff.wait()

    def arrive(h):
        rows = pl.ds(half * h, half)

        @pl.when(core == 0)
        def _():
            back_copy(rows, h).wait_recv()
            first_cells(rows, 1, h, mate).wait_recv()

        @pl.when(jnp.logical_and(core == 0, lat > 0))
        def _():
            last_cells(rows, 1, h, after).wait_recv()

        @pl.when(jnp.logical_and(core == 1, lat < lats - 1))
        def _():
            first_cells(rows, 0, h, before2).wait_recv()

    def place(h, value, first_col):
        width = value.shape[-1]
        for part_no in (0, 1):
            high, low = split(value[part_no])
            xr[h, part_no * half : (part_no + 1) * half, first_col : first_col + width] = high
            xr[h, (2 + part_no) * half : (3 + part_no) * half, first_col : first_col + width] = low

    neb = gbuf.shape[0]

    depth = xr.shape[-1]

    def put_all(h, rim):
        rows = pl.ds(half * h, half)
        if rim:
            place(h, rext[:, rows, :], LB + trace)
        else:
            place(h, ubuf[core, :, rows, :], LB)
            place(h, lext[:, rows, :], 0)

    def recover(h):
        put_all(h, False)
        put_all(h, True)
        rows = pl.ds(half * h, half)

        def block(j, carry):
            cols = pl.ds(pl.multiple_of(j * LB, LB), LB)
            prod = jnp.dot(xr[h], wr[j, :, : 2 * LB], preferred_element_type=F32)
            prod = prod[: 2 * half] + prod[2 * half :]
            prod = prod + jnp.dot(xr[h, : 2 * half, :], wr[j, :, 2 * LB :], preferred_element_type=F32)
            re = prod[:half, :LB] - prod[half:, LB:]
            im = prod[:half, LB:] + prod[half:, :LB]
            row = jnp.sum(ff[0, rows, cols] * re + ff[1, rows, cols] * im, axis=0, keepdims=True)
            if h == 0:
                gbuf[pl.ds(j, 1), :] = row
            else:
                gbuf[pl.ds(j, 1), :] = gbuf[pl.ds(j, 1), :] + row
            return carry

        lax.fori_loop(0, neb, block, 0)

    leave = pltpu.make_async_copy(ubuf.at[core], u_hbm, load_sem.at[6])

    @pl.when(core == 0)
    def _():
        arrive(0)
        recover(0)
        arrive(1)
        leave.start()
        recover(1)

    @pl.when(core == 1)
    def _():
        leave.start()
        for h in (0, 1):
            put_all(h, False)
        for h in (0, 1):
            arrive(h)
            put_all(h, True)

        def block(j, carry):
            cols = pl.ds(pl.multiple_of(j * LB, LB), LB)
            prod = jnp.dot(xr[...].reshape(4 * shots, depth), wr[j], preferred_element_type=F32)
            prod = prod[:, : 2 * LB] + prod[:, 2 * LB :]
            row = jnp.zeros((1, LB), F32)
            for h in (0, 1):
                rows = pl.ds(half * h, half)
                part_sum = prod[2 * shots * h : 2 * shots * h + shots] + prod[2 * shots * h + shots : 2 * shots * (h + 1)]
                re = part_sum[:half, :LB] - part_sum[half:, LB:]
                im = part_sum[:half, LB:] + part_sum[half:, :LB]
                row = row + jnp.sum(ff[0, rows, cols] * re + ff[1, rows, cols] * im, axis=0, keepdims=True)
            gbuf[pl.ds(j, 1), :] = row
            return carry

        lax.fori_loop(0, neb, block, 0)

    grads = gbuf[...] * (shots ** (-0.5))
    lanes = lax.broadcasted_iota(jnp.int32, gsend.shape[1:], 0)
    placed = []
    for b in range(neb):
        row = jnp.broadcast_to(grads[b : b + 1, :], gsend.shape[1:])
        placed.append(jnp.where(lanes == slot_sm[b], row, 0.0))
    for s in range(slabs):
        total = jnp.zeros(gsend.shape[1:], F32)
        for b in range(neb):
            total = total + placed[b] * jnp.where(own_sm[b] == s, 1.0, 0.0).astype(F32)
        gsend[s] = total

    def grad_copy(to, sender):
        return remote(gsend.at[to], grecv.at[sender], gs_, gr_, "slab", to)

    def grad_send(k, carry):
        grad_copy(lax.rem(me + k, slabs), me).start()
        return carry

    lax.fori_loop(1, slabs, grad_send, 0)
    grecv[me] = gsend[me]

    def sent(ref, sem, axis="slab", where=me):
        remote(ref, ref, sem, sem, axis, where).wait_send()

    @pl.when(leaf)
    def _():
        sent(upan, vs_)

    @pl.when(jnp.logical_and(core == 0, pair))
    def _():
        sent(vland, xs_)

    sent(h1, h1s)
    sent(f1, f1s)
    sent(h2, h2s)
    sent(f2, f2s)

    @pl.when(core == 1)
    def _():
        @pl.when(me < slabs - 1)
        def _():
            sent(de.at[0], ds_)

        @pl.when(has_chain)
        def _():
            sent(ubuf, us_)

        @pl.when(has_leaf)
        def _():
            sent(ubuf, ul_)

        @pl.when(leaf)
        def _():
            sent(de.at[0], es_)

        sent(ubuf.at[0], as_)
        sent(rext, rs_)

        @pl.when(lat > 1)
        def _():
            sent(rext, r2s_)

        @pl.when(lat < lats - 1)
        def _():
            sent(lext, ls_)

    @pl.when(core == 0)
    def _():
        for k in (0, 1):
            panel_copy(k).wait_send()
            source_copy(k).wait_send()

    leave.wait()
    all_others = pl.ds(0, slabs - 1)
    remote(gsend.at[all_others], grecv.at[all_others], gs_, gr_, "slab", me).wait_recv()
    total = grecv[0]
    for k in range(1, slabs):
        total = total + grecv[k]
    model_out[...] = total
    sent(gsend.at[all_others], gs_)


def deliver(u_ref, model_ref, u_out, model_out):
    u_out[...] = u_ref[...]
    model_out[...] = model_ref[...]


def body(
    residual_blocks,
    residual_slab,
    residual_pos,
    shot_ids,
    wavelet,
    down_panel,
    up_panel,
    recovery,
    forward_field,
    element_owner,
    element_slot,
):
    slabs = 16
    nres, _, shots, width = residual_blocks.shape
    trace = down_panel.shape[-1]
    depth, nel = recovery.shape[-2:]
    neb = element_slot.shape[0]
    half = shots // 2
    nch = shots // CH
    smem = pl.BlockSpec(memory_space=pltpu.SMEM)
    vmem = pl.BlockSpec(memory_space=pltpu.VMEM)
    hbm = pl.BlockSpec(memory_space=pl.ANY)
    dma = pltpu.SemaphoreType.DMA
    ups, model = pl.pallas_call(
        kernel,
        out_shape=(
            jax.ShapeDtypeStruct((2, shots, trace), F32),
            jax.ShapeDtypeStruct((neb, width), F32),
        ),
        in_specs=[vmem] * 2 + [smem] * 4 + [hbm] * 5,
        out_specs=(hbm, vmem),
        scratch_shapes=[
            pltpu.VMEM((nres, 2, shots, width), F32),
            pltpu.VMEM((4, 2, trace, trace), F32),
            pltpu.VMEM((2, depth, nel), F32),
            pltpu.VMEM((2, shots, nel), F32),
            pltpu.VMEM((2, trace // width, trace, 4 * width), BF16),
            pltpu.VMEM((2, 2, trace // width, trace, 4 * width), BF16),
            pltpu.VMEM((nel // width, depth, 4 * width), BF16),
            pltpu.VMEM((slabs, 2, shots, trace), F32),
            pltpu.VMEM((2, RY, 2, half, trace), F32),
            pltpu.VMEM((2, RY, 2, 2, half, trace), F32),
            pltpu.VMEM((2, 2, half, trace), F32),
            pltpu.VMEM((2, 2, 2, half, trace), F32),
            pltpu.VMEM((2, 2, shots, trace), F32),
            pltpu.VMEM((2, 2, 2, shots, trace), F32),
            pltpu.VMEM((2, 2, shots, trace), F32),
            pltpu.VMEM((2, 2, shots, trace), F32),
            pltpu.VMEM((2, 2, shots, trace), F32),
            pltpu.VMEM((2, shots, width), F32),
            pltpu.VMEM((2, shots, width), F32),
            pltpu.VMEM((2, 2 * shots, depth), BF16),
            pltpu.VMEM((neb, width), F32),
            pltpu.VMEM((slabs, neb, width), F32),
            pltpu.VMEM((slabs, neb, width), F32),
            pltpu.VMEM((slabs, width), jnp.int32),
            pltpu.SMEM((slabs, width), jnp.int32),
            pltpu.VMEM((2, shots, width), F32),
            pltpu.VMEM((2, trace, trace), F32),
            pltpu.VMEM((2, trace, trace), F32),
            pltpu.VMEM((2, 2, shots, trace), F32),
            dma((7,)),
            dma,
            dma((2, RY, 2)),
            dma,
            dma((2, RY, 2)),
            dma,
            dma((2, 2)),
            dma,
            dma((2, 2)),
            dma,
            dma((2, nch)),
            dma,
            dma((2, nch)),
            dma,
            dma((2,)),
            dma,
            dma,
            dma((2,)),
            dma,
            dma((2,)),
            dma,
            dma,
            dma((2,)),
            dma((2,)),
            dma((2,)),
            dma((2,)),
            dma,
            dma,
            dma((trace // VP,)),
            dma,
            dma,
            dma,
            dma((2,)),
        ],
        compiler_params=pltpu.CompilerParams(
            collective_id=0, has_side_effects=True, vmem_limit_bytes=60 * 1024 * 1024
        ),
    )(
        residual_slab.reshape(1, -1),
        residual_pos.reshape(1, -1),
        element_owner.reshape(-1),
        element_slot,
        shot_ids,
        wavelet.T,
        residual_blocks,
        down_panel[0, 0],
        up_panel[0, 0],
        recovery[0, 0],
        forward_field[0, 0],
    )
    ups, model = pl.pallas_call(
        deliver,
        out_shape=(
            jax.ShapeDtypeStruct((2, shots, trace), F32),
            jax.ShapeDtypeStruct((neb, width), F32),
        ),
        in_specs=[vmem, vmem],
        out_specs=(vmem, vmem),
    )(ups, model)
    return (ups[None, None], model[None, None])


def solution(mesh):
    placed = (
        P(("slab", "lat"), None, None, None),
        P(("slab", "lat"), None),
        P(("slab", "lat")),
        P(),
        P(),
        P("slab", "lat", None, None, None),
        P("slab", "lat", None, None, None),
        P("slab", "lat", None, None, None),
        P("slab", "lat", None, None, None),
        P(("slab", "lat"), None),
        P(("slab", "lat")),
    )
    return jax.shard_map(
        body,
        mesh=mesh,
        in_specs=placed,
        out_specs=(P("slab", "lat", None, None, None), P("slab", "lat", None, None)),
        check_vma=False,
    )
```

```python
import functools

import jax
import jax.numpy as jnp
from jax import lax
from jax.experimental import pallas as pl
from jax.experimental.pallas import tpu as pltpu
from jax.sharding import PartitionSpec as P

MESH = pl.DeviceIdType.MESH
F32 = jnp.float32
BF16 = jnp.bfloat16
LB = 128
RY = 4
CAP = 4
CH = 8
VR = 32
VP = 64


def split(value):
    high = value.astype(BF16)
    low = (value - high.astype(F32)).astype(BF16)
    return high, low


def remote(src, dst, send, recv, axis, where):
    return pltpu.make_async_remote_copy(
        src_ref=src,
        dst_ref=dst,
        send_sem=send,
        recv_sem=recv,
        device_id={axis: where},
        device_id_type=MESH,
    )


def kernel(
    slab_v,
    pos_v,
    own_sm,
    slot_sm,
    shot_sm,
    wav_sm,
    res_hbm,
    down_hbm,
    up_hbm,
    rec_hbm,
    ff_hbm,
    u_hbm,
    model_out,
    res,
    pan,
    rec,
    ff,
    wd,
    wz,
    wr,
    part,
    h1,
    f1,
    h2,
    f2,
    src,
    de,
    ubuf,
    drecv,
    urecv,
    lext,
    rext,
    xr,
    gbuf,
    gsend,
    grecv,
    tab_v,
    tab_sm,
    wbuf,
    upan,
    vland,
    erecv,
    load_sem,
    h1s,
    h1r,
    f1s,
    f1r,
    h2s,
    h2r,
    f2s,
    f2r,
    ds_,
    dr_,
    us_,
    ur_,
    ls_,
    lr_,
    rs_,
    r2s_,
    rr_,
    as_,
    ar_,
    gs_,
    gr_,
    ps_,
    pr_,
    ss_,
    sr_,
    ul_,
    vs_,
    vr_,
    xs_,
    xr_,
    es_,
    er_,
):
    slabs = 16
    lats = 8
    shots, trace = src.shape[2], src.shape[3]
    half = shots // 2
    places = trace // LB
    nres = res.shape[0]
    nch = shots // CH
    me = lax.axis_index("slab")
    lat = lax.axis_index("lat")
    y = lax.rem(me, RY)
    z = lax.div(me, RY)

    core = lax.rem(lat, 2)
    mate = lat + 1 - 2 * core
    top = slabs - RY
    even = lax.rem(me, 2) == 0
    pair = jnp.logical_and(even, me < top)
    leaf = jnp.logical_and(lax.rem(me, 2) == 1, me < top)
    which = jnp.where(pair, 1, 0)
    below = lax.rem(me + slabs - 1, slabs)
    load_res = pltpu.make_async_copy(res_hbm, res, load_sem.at[0])
    load_down = pltpu.make_async_copy(down_hbm, pan.at[0], load_sem.at[1])
    load_up = pltpu.make_async_copy(up_hbm, pan.at[1], load_sem.at[2])
    load_rec = pltpu.make_async_copy(rec_hbm, rec, load_sem.at[3])
    load_ff = pltpu.make_async_copy(ff_hbm, ff, load_sem.at[4])
    load_res.start()

    @pl.when(core == 1)
    def _():
        load_down.start()

    @pl.when(jnp.logical_or(core == 1, pair))
    def _():
        load_up.start()

    load_rec.start()
    load_ff.start()

    barrier = pltpu.get_barrier_semaphore()

    for step in (1, RY - 1):
        for other in (z * RY + lax.rem(y + step, RY), lax.rem(z + step, RY) * RY + y):
            pl.semaphore_signal(barrier, inc=1, device_id={"slab": other}, device_id_type=MESH)

    def meet(step, present):
        @pl.when(present)
        def _():
            pl.semaphore_signal(barrier, inc=1, device_id={"lat": lat + step}, device_id_type=MESH)

    meet(-1, lat > 0)
    meet(1, lat < lats - 1)
    meet(-2, jnp.logical_and(core == 1, lat > 1))
    meet(2, jnp.logical_and(core == 1, lat < lats - 1))

    rows_no = lax.broadcasted_iota(jnp.int32, (1, nres), 1)
    match = slab_v[...] == lax.broadcasted_iota(jnp.int32, (slabs, nres), 0)
    hits = jnp.where(match, 1.0, 0.0).astype(F32)
    before = lax.broadcasted_iota(jnp.int32, (nres, nres), 0) < lax.broadcasted_iota(jnp.int32, (nres, nres), 1)
    rank = jnp.dot(hits.astype(BF16), jnp.where(before, 1.0, 0.0).astype(BF16), preferred_element_type=F32)
    code = (rows_no * 8 + pos_v[...]).astype(F32)
    found = jnp.sum(hits, axis=1, keepdims=True)
    lane = lax.broadcasted_iota(jnp.int32, tab_v.shape, 1)
    table = jnp.zeros(tab_v.shape, F32)
    for c in range(CAP):
        value = jnp.sum(jnp.where(rank == c, hits * code, 0.0), axis=1, keepdims=True)
        value = jnp.where(found > c, value, 7.0)
        table = table + jnp.where(lane == c, value, 0.0)
    tab_v[...] = table.astype(jnp.int32)
    load_tab = pltpu.make_async_copy(tab_v, tab_sm, load_sem.at[5])
    load_tab.start()

    def weight_row(j, carry):
        for part_no in (0, 1):
            wbuf[part_no, pl.ds(j, 1), :] = jnp.full((1, LB), wav_sm[part_no, shot_sm[j]], F32)
        return carry

    lax.fori_loop(0, shots, weight_row, 0, unroll=8)
    load_tab.wait()

    def ring(col):
        return y if col == 0 else z

    def cross(col):
        return z if col == 0 else y

    def slab_at(col, t, i):
        return i * RY + t if col == 0 else t * RY + i

    def order(col, k):
        off = jnp.where(k < 2, 2 - k, 3 * (3 - k))
        return lax.rem(cross(col) + off, RY)

    def build(col, s):
        rows = pl.ds(half * col, half)
        codes = [tab_sm[s, c] for c in range(CAP)]
        blocks = [res[lax.bitwise_and(lax.shift_right_logical(code, 3), nres - 1), :, rows, :] for code in codes]
        spots = [lax.bitwise_and(code, 7) for code in codes]
        for p in range(places):
            total = blocks[0] * jnp.where(spots[0] == p, 1.0, 0.0).astype(F32)
            for c in range(1, CAP):
                total = total + blocks[c] * jnp.where(spots[c] == p, 1.0, 0.0).astype(F32)
            part[s, :, rows, p * LB : (p + 1) * LB] = total

    def half_copy(stage, col, i, way, s):
        rows = pl.ds(half * col, half)
        a, b = ring(col), cross(col)
        if stage == 1:
            to = lax.rem(a + (RY - 1 if way == 0 else 1), RY)
            where = slab_at(col, to, b)
            return remote(
                part.at[s, way, rows, :], h1.at[col, i, way], h1s, h1r.at[col, i, way], "slab", where
            )
        to = lax.rem(b + (RY - 1 if way == 0 else 1), RY)
        where = slab_at(col, a, to)
        return remote(part.at[s, way, rows, :], h2.at[col, way], h2s, h2r.at[col, way], "slab", where)

    def full_copy(stage, col, i, way, s):
        rows = pl.ds(half * col, half)
        a, b = ring(col), cross(col)
        if stage == 1:
            to = lax.rem(a + (RY - 1 if way == 0 else 1), RY)
            where = slab_at(col, to, b)
            return remote(
                part.at[s, :, rows, :], f1.at[col, i, way], f1s, f1r.at[col, i, way], "slab", where
            )
        to = lax.rem(b + (RY - 1 if way == 0 else 1), RY)
        where = slab_at(col, a, to)
        return remote(part.at[s, :, rows, :], f2.at[col, way], f2s, f2r.at[col, way], "slab", where)

    load_res.wait()

    def first(k, carry):
        for col in (0, 1):
            i = order(col, k)
            s = slab_at(col, lax.rem(ring(col) + 2, RY), i)
            build(col, s)
        return carry

    first(0, 0)
    peers = 4 + (lat > 0).astype(jnp.int32) + (lat < lats - 1).astype(jnp.int32)
    peers = peers + core * ((lat > 1).astype(jnp.int32) + (lat < lats - 1).astype(jnp.int32))
    pl.semaphore_wait(barrier, peers)

    def panel_copy(which):
        ref = down_hbm if which == 0 else up_hbm
        return remote(ref, pan.at[2 + which], ps_.at[which], pr_.at[which], "lat", mate)

    @pl.when(core == 0)
    def _():
        panel_copy(0).start()

    def first_send(k, carry):
        for col in (0, 1):
            i = order(col, k)
            s = slab_at(col, lax.rem(ring(col) + 2, RY), i)
            for way in (0, 1):
                half_copy(1, col, i, way, s).start()
        return carry

    first_send(0, 0)

    def first_rest(k, carry):
        first(k, carry)
        return first_send(k, carry)

    lax.fori_loop(1, RY, first_rest, 0)

    def middle(k, carry):
        for col in (0, 1):
            i = order(col, k)
            for step in (RY - 1, 1, 0):
                build(col, slab_at(col, lax.rem(ring(col) + step, RY), i))
        return carry

    lax.fori_loop(0, RY, middle, 0)

    def second(k, carry):
        for col in (0, 1):
            i = order(col, k)
            for way in (0, 1):
                t = lax.rem(ring(col) + (RY - 1 if way == 0 else 1), RY)
                s = slab_at(col, t, i)
                rows = pl.ds(half * col, half)
                half_copy(1, col, i, way, s).wait_recv()
                part[s, way, rows, :] = part[s, way, rows, :] + h1[col, i, way]
                full_copy(1, col, i, way, s).start()
        return carry

    def gather(k, carry):
        for col in (0, 1):
            i = order(col, k)
            s = slab_at(col, ring(col), i)
            rows = pl.ds(half * col, half)
            for way in (0, 1):
                full_copy(1, col, i, way, s).wait_recv()
            part[s, :, rows, :] = part[s, :, rows, :] + (f1[col, i, 0] + f1[col, i, 1])
        return carry

    lax.fori_loop(0, 2, second, 0)
    gather(0, 0)
    for col in (0, 1):
        i = lax.rem(cross(col) + 2, RY)
        s = slab_at(col, ring(col), i)
        for way in (0, 1):
            half_copy(2, col, i, way, s).start()
    lax.fori_loop(2, RY, second, 0)

    def pack(source, which, target, count):
        def col_block(j, carry):
            cols = pl.ds(pl.multiple_of(j * LB, LB), LB)
            for part_no in (0, 1):
                ref = source.at[which] if which is not None else source
                high, low = split(ref[part_no, :, cols])
                target[j, :, part_no * LB : (part_no + 1) * LB] = high
                target[j, :, (2 + part_no) * LB : (3 + part_no) * LB] = low
            return carry

        lax.fori_loop(0, count, col_block, 0)

    @pl.when(core == 1)
    def _():
        load_down.wait()
        pack(pan, 0, wd.at[1], trace // LB)

    @pl.when(core == 0)
    def _():
        panel_copy(1).start()


    lax.fori_loop(1, RY - 1, gather, 0)
    for col in (0, 1):
        rows = pl.ds(half * col, half)
        for way in (0, 1):
            i = lax.rem(cross(col) + (RY - 1 if way == 0 else 1), RY)
            s = slab_at(col, ring(col), i)
            half_copy(2, col, i, way, s).wait_recv()
            part[s, way, rows, :] = part[s, way, rows, :] + h2[col, way]
            full_copy(2, col, i, way, s).start()
    gather(RY - 1, 0)

    def piece_copy(b):
        rows = pl.ds(pl.multiple_of(b * VP, VP), VP)
        return remote(up_hbm.at[:, rows, :], upan.at[:, rows, :], vs_, vr_.at[b], "slab", below)

    @pl.when(leaf)
    def _():
        for b in range(trace // VP):
            piece_copy(b).start()

    @pl.when(core == 1)
    def _():
        panel_copy(0).wait_recv()
        pack(pan, 2, wd.at[0], trace // LB)
        load_up.wait()
        pack(pan, 1, wz.at[0, 1], trace // LB)

    @pl.when(core == 0)
    def _():
        load_rec.wait()
        pack(rec, None, wr, rec.shape[2] // LB)

        @pl.when(pair)
        def _():
            load_up.wait()
            pack(pan, 1, wz.at[0, 0], trace // LB)

    @pl.when(lat == 0)
    def _():
        lext[...] = jnp.zeros_like(lext)

    @pl.when(lat == lats - 1)
    def _():
        rext[...] = jnp.zeros_like(rext)

    def source_copy(col):
        rows = pl.ds(half * col, half)
        return remote(src.at[0, :, rows, :], src.at[0, :, rows, :], ss_.at[col], sr_.at[col], "lat", mate)

    for col in (0, 1):
        rows = pl.ds(half * col, half)
        for way in (0, 1):
            full_copy(2, col, 0, way, me).wait_recv()
        total = part[me, :, rows, :] + (f2[col, 0] + f2[col, 1])
        w_re = jnp.tile(wbuf[0, rows, :], (1, places))
        w_im = jnp.tile(wbuf[1, rows, :], (1, places))
        src[core, 0, rows, :] = w_re * total[0] - w_im * total[1]
        src[core, 1, rows, :] = w_re * total[1] + w_im * total[0]

        @pl.when(core == 0)
        def _():
            source_copy(col).start()

    def product(first, second, weight, j):
        count = first.shape[0]
        high, low = split(jnp.concatenate([first, second], axis=0))
        x = jnp.concatenate([high, low], axis=0)
        prod = jnp.dot(x, weight[j], preferred_element_type=F32)
        prod = prod[: 2 * count] + prod[2 * count :]
        prod = prod[:, : 2 * LB] + prod[:, 2 * LB :]
        return prod[:count, :LB] - prod[count:, LB:], prod[:count, LB:] + prod[count:, :LB]

    def turn(arrived, target, rows, weight, extra):
        first, second = arrived[0, rows, :], arrived[1, rows, :]
        for j in range(trace // LB):
            cols = slice(j * LB, (j + 1) * LB)
            re, im = product(first, second, weight, j)
            target[0, rows, cols] = re + extra[0, rows, cols]
            target[1, rows, cols] = im + extra[1, rows, cols]

    def rows_of(c):
        return pl.ds(pl.multiple_of(c * CH, CH), CH)

    def down_copy(c, w):
        rows = rows_of(c)
        return remote(
            de.at[0, w, :, rows, :], drecv.at[w, :, rows, :], ds_, dr_.at[w, c], "slab", lax.rem(me + 1, slabs)
        )

    has_chain = jnp.logical_or(me > top, jnp.logical_and(even, me > 0))
    has_leaf = jnp.logical_and(even, jnp.logical_and(me > 0, me <= top))

    def up_copy(c, w, to_leaf=False):
        rows = rows_of(c)
        step = jnp.where(me > top, 1, 2)
        to = below if to_leaf else lax.rem(me + slabs - step, slabs)
        send = ul_ if to_leaf else us_
        return remote(ubuf.at[w, :, rows, :], urecv.at[w, :, rows, :], send, ur_.at[w, c], "slab", to)

    def last_cells(rows, w, h, to):
        return remote(
            ubuf.at[w, :, rows, pl.ds(trace - LB, LB)], lext.at[:, rows, :], ls_, lr_.at[h], "lat", to
        )

    def first_cells(rows, w, h, to):
        send = rs_ if w == 1 else r2s_
        return remote(ubuf.at[w, :, rows, pl.ds(0, LB)], rext.at[:, rows, :], send, rr_.at[h], "lat", to)

    def back_copy(rows, h):
        return remote(ubuf.at[0, :, rows, :], ubuf.at[0, :, rows, :], as_, ar_.at[h], "lat", mate)

    after = lax.rem(lat + 1, lats)
    before2 = lax.rem(lat + lats - 2, lats)

    def finish(c, w):
        rows = rows_of(c)
        h = lax.div(c, nch // 2)

        @pl.when(has_chain)
        def _():
            up_copy(c, w).start()

        @pl.when(has_leaf)
        def _():
            up_copy(c, w, True).start()

        if w == 0:
            back_copy(rows, h).start()

            @pl.when(lat > 1)
            def _():
                first_cells(rows, 0, h, before2).start()

            lext[:, rows, :] = ubuf[0, :, rows, trace - LB :]
        else:
            first_cells(rows, 1, h, mate).start()

            @pl.when(lat < lats - 1)
            def _():
                last_cells(rows, 1, h, after).start()

    def down(c, carry):
        rows = rows_of(c)
        for w in (0, 1):

            @pl.when(me == 0)
            def _():
                de[0, w, :, rows, :] = src[w, :, rows, :]

            @pl.when(me > 0)
            def _():
                down_copy(c, w).wait_recv()
                turn(drecv.at[w], de.at[0, w], rows, wd.at[w], src.at[w])

            @pl.when(me < slabs - 1)
            def _():
                down_copy(c, w).start()

            @pl.when(me == slabs - 1)
            def _():
                ubuf[w, :, rows, :] = de[0, w, :, rows, :]
                finish(c, w)

        return carry

    def up(c, carry):
        rows = rows_of(c)
        for w in (0, 1):
            up_copy(c, w).wait_recv()
            turn(urecv.at[w], ubuf.at[w], rows, wz.at[which, w], de.at[which, w])
            finish(c, w)
        return carry

    def give_copy(b):
        rows = pl.ds(pl.multiple_of(b * VP, VP), VP)
        return remote(vland.at[:, rows, :], vland.at[:, rows, :], xs_, xr_, "lat", mate)

    def form(store, done, start, stop):
        def piece(b, carry):
            piece_copy(b).wait_recv()

            def block(k, carry):
                rows = pl.ds(pl.multiple_of(b * VP + k * VR, VR), VR)
                first, second = upan[0, rows, :], upan[1, rows, :]
                for j in range(trace // LB):
                    re, im = product(first, second, wz.at[0, core], j)
                    store(j, rows, re, im)
                return carry

            lax.fori_loop(0, VP // VR, block, 0)
            done(b)
            return carry

        lax.fori_loop(start, stop, piece, 0)

    def store_packed(j, rows, re, im):
        for part_no, value in enumerate((re, im)):
            high, low = split(value)
            wz[1, 1, j, rows, part_no * LB : (part_no + 1) * LB] = high
            wz[1, 1, j, rows, (2 + part_no) * LB : (3 + part_no) * LB] = low

    def store_plain(j, rows, re, im):
        vland[0, rows, j * LB : (j + 1) * LB] = re
        vland[1, rows, j * LB : (j + 1) * LB] = im

    def odd_copy(w):
        return remote(de.at[0, w], erecv.at[w], es_, er_.at[w], "slab", below)

    @pl.when(jnp.logical_and(core == 0, pair))
    def _():
        form(store_plain, lambda b: give_copy(b).start(), 0, trace // VP)

    def late_packs():
        panel_copy(1).wait_recv()
        pack(pan, 3, wz.at[0, 0], trace // LB)
        load_rec.wait()
        pack(rec, None, wr, rec.shape[2] // LB)

    @pl.when(core == 1)
    def _():
        @pl.when(me >= slabs // 2)
        def _():
            late_packs()

        for col in (0, 1):
            source_copy(col).wait_recv()
        early = jnp.where(jnp.logical_and(pair, me >= slabs // 2), trace // VP // 2, 0)

        @pl.when(pair)
        def _():
            form(store_packed, lambda b: None, 0, early)

        lax.fori_loop(0, nch, down, 0)

        @pl.when(leaf)
        def _():
            for w in (1, 0):
                odd_copy(w).start()

        @pl.when(me < slabs // 2)
        def _():
            late_packs()

        @pl.when(pair)
        def _():
            form(store_packed, lambda b: None, early, trace // VP)
            remote(vland, vland, xs_, xr_, "lat", mate).wait_recv()
            pack(vland, None, wz.at[1, 0], trace // LB)
            for w in (1, 0):
                odd_copy(w).wait_recv()

                def two(k, carry):
                    rows = pl.ds(pl.multiple_of(k * VR, VR), VR)
                    turn(erecv.at[w], de.at[1, w], rows, wz.at[0, w], de.at[0, w])
                    return carry

                lax.fori_loop(0, shots // VR, two, 0)

        @pl.when(me < slabs - 1)
        def _():
            lax.fori_loop(0, nch, up, 0)

    load_ff.wait()

    def arrive(h):
        rows = pl.ds(half * h, half)

        @pl.when(core == 0)
        def _():
            back_copy(rows, h).wait_recv()
            first_cells(rows, 1, h, mate).wait_recv()

        @pl.when(jnp.logical_and(core == 0, lat > 0))
        def _():
            last_cells(rows, 1, h, after).wait_recv()

        @pl.when(jnp.logical_and(core == 1, lat < lats - 1))
        def _():
            first_cells(rows, 0, h, before2).wait_recv()

    def place(h, value, first_col):
        width = value.shape[-1]
        for part_no in (0, 1):
            high, low = split(value[part_no])
            xr[h, part_no * half : (part_no + 1) * half, first_col : first_col + width] = high
            xr[h, (2 + part_no) * half : (3 + part_no) * half, first_col : first_col + width] = low

    neb = gbuf.shape[0]

    depth = xr.shape[-1]

    def put_all(h, rim):
        rows = pl.ds(half * h, half)
        if rim:
            place(h, rext[:, rows, :], LB + trace)
        else:
            place(h, ubuf[core, :, rows, :], LB)
            place(h, lext[:, rows, :], 0)

    def recover(h):
        put_all(h, False)
        put_all(h, True)
        rows = pl.ds(half * h, half)

        def block(j, carry):
            cols = pl.ds(pl.multiple_of(j * LB, LB), LB)
            prod = jnp.dot(xr[h], wr[j, :, : 2 * LB], preferred_element_type=F32)
            prod = prod[: 2 * half] + prod[2 * half :]
            prod = prod + jnp.dot(xr[h, : 2 * half, :], wr[j, :, 2 * LB :], preferred_element_type=F32)
            re = prod[:half, :LB] - prod[half:, LB:]
            im = prod[:half, LB:] + prod[half:, :LB]
            row = jnp.sum(ff[0, rows, cols] * re + ff[1, rows, cols] * im, axis=0, keepdims=True)
            if h == 0:
                gbuf[pl.ds(j, 1), :] = row
            else:
                gbuf[pl.ds(j, 1), :] = gbuf[pl.ds(j, 1), :] + row
            return carry

        lax.fori_loop(0, neb, block, 0)

    leave = pltpu.make_async_copy(ubuf.at[core], u_hbm, load_sem.at[6])

    @pl.when(core == 0)
    def _():
        arrive(0)
        recover(0)
        arrive(1)
        leave.start()
        recover(1)

    @pl.when(core == 1)
    def _():
        leave.start()
        for h in (0, 1):
            put_all(h, False)
        for h in (0, 1):
            arrive(h)
            put_all(h, True)

        def block(j, carry):
            cols = pl.ds(pl.multiple_of(j * LB, LB), LB)
            prod = jnp.dot(xr[...].reshape(4 * shots, depth), wr[j], preferred_element_type=F32)
            prod = prod[:, : 2 * LB] + prod[:, 2 * LB :]
            row = jnp.zeros((1, LB), F32)
            for h in (0, 1):
                rows = pl.ds(half * h, half)
                part_sum = prod[2 * shots * h : 2 * shots * h + shots] + prod[2 * shots * h + shots : 2 * shots * (h + 1)]
                re = part_sum[:half, :LB] - part_sum[half:, LB:]
                im = part_sum[:half, LB:] + part_sum[half:, :LB]
                row = row + jnp.sum(ff[0, rows, cols] * re + ff[1, rows, cols] * im, axis=0, keepdims=True)
            gbuf[pl.ds(j, 1), :] = row
            return carry

        lax.fori_loop(0, neb, block, 0)

    grads = gbuf[...] * (shots ** (-0.5))
    lanes = lax.broadcasted_iota(jnp.int32, gsend.shape[1:], 0)
    placed = []
    for b in range(neb):
        row = jnp.broadcast_to(grads[b : b + 1, :], gsend.shape[1:])
        placed.append(jnp.where(lanes == slot_sm[b], row, 0.0))
    for s in range(slabs):
        total = jnp.zeros(gsend.shape[1:], F32)
        for b in range(neb):
            total = total + placed[b] * jnp.where(own_sm[b] == s, 1.0, 0.0).astype(F32)
        gsend[s] = total

    def grad_copy(to, sender):
        return remote(gsend.at[to], grecv.at[sender], gs_, gr_, "slab", to)

    def grad_send(k, carry):
        grad_copy(lax.rem(me + k, slabs), me).start()
        return carry

    lax.fori_loop(1, slabs, grad_send, 0)
    grecv[me] = gsend[me]

    def sent(ref, sem, axis="slab", where=me):
        remote(ref, ref, sem, sem, axis, where).wait_send()

    @pl.when(leaf)
    def _():
        sent(upan, vs_)

    @pl.when(jnp.logical_and(core == 0, pair))
    def _():
        sent(vland, xs_)

    sent(h1, h1s)
    sent(f1, f1s)
    sent(h2, h2s)
    sent(f2, f2s)

    @pl.when(core == 1)
    def _():
        @pl.when(me < slabs - 1)
        def _():
            sent(de.at[0], ds_)

        @pl.when(has_chain)
        def _():
            sent(ubuf, us_)

        @pl.when(has_leaf)
        def _():
            sent(ubuf, ul_)

        @pl.when(leaf)
        def _():
            sent(de.at[0], es_)

        sent(ubuf.at[0], as_)
        sent(rext, rs_)

        @pl.when(lat > 1)
        def _():
            sent(rext, r2s_)

        @pl.when(lat < lats - 1)
        def _():
            sent(lext, ls_)

    @pl.when(core == 0)
    def _():
        for k in (0, 1):
            panel_copy(k).wait_send()
            source_copy(k).wait_send()

    leave.wait()
    all_others = pl.ds(0, slabs - 1)
    remote(gsend.at[all_others], grecv.at[all_others], gs_, gr_, "slab", me).wait_recv()
    total = grecv[0]
    for k in range(1, slabs):
        total = total + grecv[k]
    model_out[...] = total
    sent(gsend.at[all_others], gs_)


def deliver(u_ref, model_ref, u_out, model_out):
    u_out[...] = u_ref[...]
    model_out[...] = model_ref[...]


def body(
    residual_blocks,
    residual_slab,
    residual_pos,
    shot_ids,
    wavelet,
    down_panel,
    up_panel,
    recovery,
    forward_field,
    element_owner,
    element_slot,
):
    slabs = 16
    nres, _, shots, width = residual_blocks.shape
    trace = down_panel.shape[-1]
    depth, nel = recovery.shape[-2:]
    neb = element_slot.shape[0]
    half = shots // 2
    nch = shots // CH
    smem = pl.BlockSpec(memory_space=pltpu.SMEM)
    vmem = pl.BlockSpec(memory_space=pltpu.VMEM)
    hbm = pl.BlockSpec(memory_space=pl.ANY)
    dma = pltpu.SemaphoreType.DMA
    ups, model = pl.pallas_call(
        kernel,
        out_shape=(
            jax.ShapeDtypeStruct((2, shots, trace), F32),
            jax.ShapeDtypeStruct((neb, width), F32),
        ),
        in_specs=[vmem] * 2 + [smem] * 4 + [hbm] * 5,
        out_specs=(hbm, vmem),
        scratch_shapes=[
            pltpu.VMEM((nres, 2, shots, width), F32),
            pltpu.VMEM((4, 2, trace, trace), F32),
            pltpu.VMEM((2, depth, nel), F32),
            pltpu.VMEM((2, shots, nel), F32),
            pltpu.VMEM((2, trace // width, trace, 4 * width), BF16),
            pltpu.VMEM((2, 2, trace // width, trace, 4 * width), BF16),
            pltpu.VMEM((nel // width, depth, 4 * width), BF16),
            pltpu.VMEM((slabs, 2, shots, trace), F32),
            pltpu.VMEM((2, RY, 2, half, trace), F32),
            pltpu.VMEM((2, RY, 2, 2, half, trace), F32),
            pltpu.VMEM((2, 2, half, trace), F32),
            pltpu.VMEM((2, 2, 2, half, trace), F32),
            pltpu.VMEM((2, 2, shots, trace), F32),
            pltpu.VMEM((2, 2, 2, shots, trace), F32),
            pltpu.VMEM((2, 2, shots, trace), F32),
            pltpu.VMEM((2, 2, shots, trace), F32),
            pltpu.VMEM((2, 2, shots, trace), F32),
            pltpu.VMEM((2, shots, width), F32),
            pltpu.VMEM((2, shots, width), F32),
            pltpu.VMEM((2, 2 * shots, depth), BF16),
            pltpu.VMEM((neb, width), F32),
            pltpu.VMEM((slabs, neb, width), F32),
            pltpu.VMEM((slabs, neb, width), F32),
            pltpu.VMEM((slabs, width), jnp.int32),
            pltpu.SMEM((slabs, width), jnp.int32),
            pltpu.VMEM((2, shots, width), F32),
            pltpu.VMEM((2, trace, trace), F32),
            pltpu.VMEM((2, trace, trace), F32),
            pltpu.VMEM((2, 2, shots, trace), F32),
            dma((7,)),
            dma,
            dma((2, RY, 2)),
            dma,
            dma((2, RY, 2)),
            dma,
            dma((2, 2)),
            dma,
            dma((2, 2)),
            dma,
            dma((2, nch)),
            dma,
            dma((2, nch)),
            dma,
            dma((2,)),
            dma,
            dma,
            dma((2,)),
            dma,
            dma((2,)),
            dma,
            dma,
            dma((2,)),
            dma((2,)),
            dma((2,)),
            dma((2,)),
            dma,
            dma,
            dma((trace // VP,)),
            dma,
            dma,
            dma,
            dma((2,)),
        ],
        compiler_params=pltpu.CompilerParams(
            collective_id=0, has_side_effects=True, vmem_limit_bytes=60 * 1024 * 1024
        ),
    )(
        residual_slab.reshape(1, -1),
        residual_pos.reshape(1, -1),
        element_owner.reshape(-1),
        element_slot,
        shot_ids,
        wavelet.T,
        residual_blocks,
        down_panel[0, 0],
        up_panel[0, 0],
        recovery[0, 0],
        forward_field[0, 0],
    )
    ups, model = pl.pallas_call(
        deliver,
        out_shape=(
            jax.ShapeDtypeStruct((2, shots, trace), F32),
            jax.ShapeDtypeStruct((neb, width), F32),
        ),
        in_specs=[vmem, vmem],
        out_specs=(vmem, vmem),
    )(ups, model)
    return (ups[None, None], model[None, None])


def solution(mesh):
    placed = (
        P(("slab", "lat"), None, None, None),
        P(("slab", "lat"), None),
        P(("slab", "lat")),
        P(),
        P(),
        P("slab", "lat", None, None, None),
        P("slab", "lat", None, None, None),
        P("slab", "lat", None, None, None),
        P("slab", "lat", None, None, None),
        P(("slab", "lat"), None),
        P(("slab", "lat")),
    )
    return jax.shard_map(
        body,
        mesh=mesh,
        in_specs=placed,
        out_specs=(P("slab", "lat", None, None, None), P("slab", "lat", None, None)),
        check_vma=False,
    )
```

```python
import functools

import jax
import jax.numpy as jnp
from jax import lax
from jax.experimental import pallas as pl
from jax.experimental.pallas import tpu as pltpu
from jax.sharding import PartitionSpec as P

MESH = pl.DeviceIdType.MESH
F32 = jnp.float32
BF16 = jnp.bfloat16
LB = 128
RY = 4
CAP = 4
CH = 8
VR = 32
VP = 64


def split(value):
    high = value.astype(BF16)
    low = (value - high.astype(F32)).astype(BF16)
    return high, low


def remote(src, dst, send, recv, axis, where):
    return pltpu.make_async_remote_copy(
        src_ref=src,
        dst_ref=dst,
        send_sem=send,
        recv_sem=recv,
        device_id={axis: where},
        device_id_type=MESH,
    )


def kernel(
    slab_v,
    pos_v,
    own_sm,
    slot_sm,
    shot_sm,
    wav_sm,
    res_hbm,
    down_hbm,
    up_hbm,
    rec_hbm,
    ff_hbm,
    u_hbm,
    model_out,
    res,
    pan,
    rec,
    ff,
    wd,
    wz,
    wr,
    part,
    h1,
    f1,
    h2,
    f2,
    src,
    de,
    ubuf,
    drecv,
    urecv,
    lext,
    rext,
    xr,
    gbuf,
    gsend,
    grecv,
    tab_v,
    tab_sm,
    wbuf,
    upan,
    vland,
    erecv,
    load_sem,
    h1s,
    h1r,
    f1s,
    f1r,
    h2s,
    h2r,
    f2s,
    f2r,
    ds_,
    dr_,
    us_,
    ur_,
    ls_,
    lr_,
    rs_,
    r2s_,
    rr_,
    as_,
    ar_,
    gs_,
    gr_,
    ps_,
    pr_,
    ss_,
    sr_,
    ul_,
    vs_,
    vr_,
    xs_,
    xr_,
    es_,
    er_,
):
    slabs = 16
    lats = 8
    shots, trace = src.shape[2], src.shape[3]
    half = shots // 2
    places = trace // LB
    nres = res.shape[0]
    nch = shots // CH
    me = lax.axis_index("slab")
    lat = lax.axis_index("lat")
    y = lax.rem(me, RY)
    z = lax.div(me, RY)

    core = lax.rem(lat, 2)
    mate = lat + 1 - 2 * core
    top = slabs - RY
    even = lax.rem(me, 2) == 0
    pair = jnp.logical_and(even, me < top)
    leaf = jnp.logical_and(lax.rem(me, 2) == 1, me < top)
    which = jnp.where(pair, 1, 0)
    below = lax.rem(me + slabs - 1, slabs)
    load_res = pltpu.make_async_copy(res_hbm, res, load_sem.at[0])
    load_down = pltpu.make_async_copy(down_hbm, pan.at[0], load_sem.at[1])
    load_up = pltpu.make_async_copy(up_hbm, pan.at[1], load_sem.at[2])
    load_rec = pltpu.make_async_copy(rec_hbm, rec, load_sem.at[3])
    load_ff = pltpu.make_async_copy(ff_hbm, ff, load_sem.at[4])
    load_res.start()

    @pl.when(core == 1)
    def _():
        load_down.start()

    @pl.when(jnp.logical_or(core == 1, pair))
    def _():
        load_up.start()

    load_rec.start()
    load_ff.start()

    barrier = pltpu.get_barrier_semaphore()

    for step in (1, RY - 1):
        for other in (z * RY + lax.rem(y + step, RY), lax.rem(z + step, RY) * RY + y):
            pl.semaphore_signal(barrier, inc=1, device_id={"slab": other}, device_id_type=MESH)

    def meet(step, present):
        @pl.when(present)
        def _():
            pl.semaphore_signal(barrier, inc=1, device_id={"lat": lat + step}, device_id_type=MESH)

    meet(-1, lat > 0)
    meet(1, lat < lats - 1)
    meet(-2, jnp.logical_and(core == 1, lat > 1))
    meet(2, jnp.logical_and(core == 1, lat < lats - 1))

    rows_no = lax.broadcasted_iota(jnp.int32, (1, nres), 1)
    match = slab_v[...] == lax.broadcasted_iota(jnp.int32, (slabs, nres), 0)
    hits = jnp.where(match, 1.0, 0.0).astype(F32)
    before = lax.broadcasted_iota(jnp.int32, (nres, nres), 0) < lax.broadcasted_iota(jnp.int32, (nres, nres), 1)
    rank = jnp.dot(hits.astype(BF16), jnp.where(before, 1.0, 0.0).astype(BF16), preferred_element_type=F32)
    code = (rows_no * 8 + pos_v[...]).astype(F32)
    found = jnp.sum(hits, axis=1, keepdims=True)
    lane = lax.broadcasted_iota(jnp.int32, tab_v.shape, 1)
    table = jnp.zeros(tab_v.shape, F32)
    for c in range(CAP):
        value = jnp.sum(jnp.where(rank == c, hits * code, 0.0), axis=1, keepdims=True)
        value = jnp.where(found > c, value, 7.0)
        table = table + jnp.where(lane == c, value, 0.0)
    tab_v[...] = table.astype(jnp.int32)
    load_tab = pltpu.make_async_copy(tab_v, tab_sm, load_sem.at[5])
    load_tab.start()

    def weight_row(j, carry):
        for part_no in (0, 1):
            wbuf[part_no, pl.ds(j, 1), :] = jnp.full((1, LB), wav_sm[part_no, shot_sm[j]], F32)
        return carry

    lax.fori_loop(0, shots, weight_row, 0, unroll=8)
    load_tab.wait()

    def ring(col):
        return y if col == 0 else z

    def cross(col):
        return z if col == 0 else y

    def slab_at(col, t, i):
        return i * RY + t if col == 0 else t * RY + i

    def order(col, k):
        off = jnp.where(k < 2, 2 - k, 3 * (3 - k))
        return lax.rem(cross(col) + off, RY)

    def build(col, s):
        rows = pl.ds(half * col, half)
        codes = [tab_sm[s, c] for c in range(CAP)]
        blocks = [res[lax.bitwise_and(lax.shift_right_logical(code, 3), nres - 1), :, rows, :] for code in codes]
        spots = [lax.bitwise_and(code, 7) for code in codes]
        for p in range(places):
            total = blocks[0] * jnp.where(spots[0] == p, 1.0, 0.0).astype(F32)
            for c in range(1, CAP):
                total = total + blocks[c] * jnp.where(spots[c] == p, 1.0, 0.0).astype(F32)
            part[s, :, rows, p * LB : (p + 1) * LB] = total

    def half_copy(stage, col, i, way, s):
        rows = pl.ds(half * col, half)
        a, b = ring(col), cross(col)
        if stage == 1:
            to = lax.rem(a + (RY - 1 if way == 0 else 1), RY)
            where = slab_at(col, to, b)
            return remote(
                part.at[s, way, rows, :], h1.at[col, i, way], h1s, h1r.at[col, i, way], "slab", where
            )
        to = lax.rem(b + (RY - 1 if way == 0 else 1), RY)
        where = slab_at(col, a, to)
        return remote(part.at[s, way, rows, :], h2.at[col, way], h2s, h2r.at[col, way], "slab", where)

    def full_copy(stage, col, i, way, s):
        rows = pl.ds(half * col, half)
        a, b = ring(col), cross(col)
        if stage == 1:
            to = lax.rem(a + (RY - 1 if way == 0 else 1), RY)
            where = slab_at(col, to, b)
            return remote(
                part.at[s, :, rows, :], f1.at[col, i, way], f1s, f1r.at[col, i, way], "slab", where
            )
        to = lax.rem(b + (RY - 1 if way == 0 else 1), RY)
        where = slab_at(col, a, to)
        return remote(part.at[s, :, rows, :], f2.at[col, way], f2s, f2r.at[col, way], "slab", where)

    load_res.wait()

    def first(k, carry):
        for col in (0, 1):
            i = order(col, k)
            s = slab_at(col, lax.rem(ring(col) + 2, RY), i)
            build(col, s)
        return carry

    first(0, 0)
    peers = 4 + (lat > 0).astype(jnp.int32) + (lat < lats - 1).astype(jnp.int32)
    peers = peers + core * ((lat > 1).astype(jnp.int32) + (lat < lats - 1).astype(jnp.int32))
    pl.semaphore_wait(barrier, peers)

    def panel_copy(which):
        ref = down_hbm if which == 0 else up_hbm
        return remote(ref, pan.at[2 + which], ps_.at[which], pr_.at[which], "lat", mate)

    @pl.when(core == 0)
    def _():
        panel_copy(0).start()

    def first_send(k, carry):
        for col in (0, 1):
            i = order(col, k)
            s = slab_at(col, lax.rem(ring(col) + 2, RY), i)
            for way in (0, 1):
                half_copy(1, col, i, way, s).start()
        return carry

    first_send(0, 0)

    def first_rest(k, carry):
        first(k, carry)
        return first_send(k, carry)

    lax.fori_loop(1, RY, first_rest, 0)

    def middle(k, carry):
        for col in (0, 1):
            i = order(col, k)
            for step in (RY - 1, 1, 0):
                build(col, slab_at(col, lax.rem(ring(col) + step, RY), i))
        return carry

    lax.fori_loop(0, RY, middle, 0)

    def second(k, carry):
        for col in (0, 1):
            i = order(col, k)
            for way in (0, 1):
                t = lax.rem(ring(col) + (RY - 1 if way == 0 else 1), RY)
                s = slab_at(col, t, i)
                rows = pl.ds(half * col, half)
                half_copy(1, col, i, way, s).wait_recv()
                part[s, way, rows, :] = part[s, way, rows, :] + h1[col, i, way]
                full_copy(1, col, i, way, s).start()
        return carry

    def gather(k, carry):
        for col in (0, 1):
            i = order(col, k)
            s = slab_at(col, ring(col), i)
            rows = pl.ds(half * col, half)
            for way in (0, 1):
                full_copy(1, col, i, way, s).wait_recv()
            part[s, :, rows, :] = part[s, :, rows, :] + (f1[col, i, 0] + f1[col, i, 1])
        return carry

    lax.fori_loop(0, 2, second, 0)
    gather(0, 0)
    for col in (0, 1):
        i = lax.rem(cross(col) + 2, RY)
        s = slab_at(col, ring(col), i)
        for way in (0, 1):
            half_copy(2, col, i, way, s).start()
    lax.fori_loop(2, RY, second, 0)

    def pack(source, which, target, count):
        def col_block(j, carry):
            cols = pl.ds(pl.multiple_of(j * LB, LB), LB)
            for part_no in (0, 1):
                ref = source.at[which] if which is not None else source
                high, low = split(ref[part_no, :, cols])
                target[j, :, part_no * LB : (part_no + 1) * LB] = high
                target[j, :, (2 + part_no) * LB : (3 + part_no) * LB] = low
            return carry

        lax.fori_loop(0, count, col_block, 0)

    @pl.when(core == 1)
    def _():
        load_down.wait()
        pack(pan, 0, wd.at[1], trace // LB)

    @pl.when(core == 0)
    def _():
        panel_copy(1).start()


    lax.fori_loop(1, RY - 1, gather, 0)
    for col in (0, 1):
        rows = pl.ds(half * col, half)
        for way in (0, 1):
            i = lax.rem(cross(col) + (RY - 1 if way == 0 else 1), RY)
            s = slab_at(col, ring(col), i)
            half_copy(2, col, i, way, s).wait_recv()
            part[s, way, rows, :] = part[s, way, rows, :] + h2[col, way]
            full_copy(2, col, i, way, s).start()
    gather(RY - 1, 0)

    def piece_copy(b):
        rows = pl.ds(pl.multiple_of(b * VP, VP), VP)
        return remote(up_hbm.at[:, rows, :], upan.at[:, rows, :], vs_, vr_.at[b], "slab", below)

    @pl.when(leaf)
    def _():
        for b in range(trace // VP):
            piece_copy(b).start()

    @pl.when(core == 1)
    def _():
        panel_copy(0).wait_recv()
        pack(pan, 2, wd.at[0], trace // LB)
        load_up.wait()
        pack(pan, 1, wz.at[0, 1], trace // LB)

    @pl.when(core == 0)
    def _():
        load_rec.wait()
        pack(rec, None, wr, rec.shape[2] // LB)

        @pl.when(pair)
        def _():
            load_up.wait()
            pack(pan, 1, wz.at[0, 0], trace // LB)

    @pl.when(lat == 0)
    def _():
        lext[...] = jnp.zeros_like(lext)

    @pl.when(lat == lats - 1)
    def _():
        rext[...] = jnp.zeros_like(rext)

    def source_copy(col):
        rows = pl.ds(half * col, half)
        return remote(src.at[0, :, rows, :], src.at[0, :, rows, :], ss_.at[col], sr_.at[col], "lat", mate)

    for col in (0, 1):
        rows = pl.ds(half * col, half)
        for way in (0, 1):
            full_copy(2, col, 0, way, me).wait_recv()
        total = part[me, :, rows, :] + (f2[col, 0] + f2[col, 1])
        w_re = jnp.tile(wbuf[0, rows, :], (1, places))
        w_im = jnp.tile(wbuf[1, rows, :], (1, places))
        src[core, 0, rows, :] = w_re * total[0] - w_im * total[1]
        src[core, 1, rows, :] = w_re * total[1] + w_im * total[0]

        @pl.when(core == 0)
        def _():
            source_copy(col).start()

    def product(first, second, weight, j):
        count = first.shape[0]
        high, low = split(jnp.concatenate([first, second], axis=0))
        x = jnp.concatenate([high, low], axis=0)
        prod = jnp.dot(x, weight[j], preferred_element_type=F32)
        prod = prod[: 2 * count] + prod[2 * count :]
        prod = prod[:, : 2 * LB] + prod[:, 2 * LB :]
        return prod[:count, :LB] - prod[count:, LB:], prod[:count, LB:] + prod[count:, :LB]

    def turn(arrived, target, rows, weight, extra):
        first, second = arrived[0, rows, :], arrived[1, rows, :]
        for j in range(trace // LB):
            cols = slice(j * LB, (j + 1) * LB)
            re, im = product(first, second, weight, j)
            target[0, rows, cols] = re + extra[0, rows, cols]
            target[1, rows, cols] = im + extra[1, rows, cols]

    def rows_of(c):
        return pl.ds(pl.multiple_of(c * CH, CH), CH)

    def down_copy(c, w):
        rows = rows_of(c)
        return remote(
            de.at[0, w, :, rows, :], drecv.at[w, :, rows, :], ds_, dr_.at[w, c], "slab", lax.rem(me + 1, slabs)
        )

    has_chain = jnp.logical_or(me > top, jnp.logical_and(even, me > 0))
    has_leaf = jnp.logical_and(even, jnp.logical_and(me > 0, me <= top))

    def up_copy(c, w, to_leaf=False):
        rows = rows_of(c)
        step = jnp.where(me > top, 1, 2)
        to = below if to_leaf else lax.rem(me + slabs - step, slabs)
        send = ul_ if to_leaf else us_
        return remote(ubuf.at[w, :, rows, :], urecv.at[w, :, rows, :], send, ur_.at[w, c], "slab", to)

    def last_cells(rows, w, h, to):
        return remote(
            ubuf.at[w, :, rows, pl.ds(trace - LB, LB)], lext.at[:, rows, :], ls_, lr_.at[h], "lat", to
        )

    def first_cells(rows, w, h, to):
        send = rs_ if w == 1 else r2s_
        return remote(ubuf.at[w, :, rows, pl.ds(0, LB)], rext.at[:, rows, :], send, rr_.at[h], "lat", to)

    def back_copy(rows, h):
        return remote(ubuf.at[0, :, rows, :], ubuf.at[0, :, rows, :], as_, ar_.at[h], "lat", mate)

    after = lax.rem(lat + 1, lats)
    before2 = lax.rem(lat + lats - 2, lats)

    def finish(c, w):
        rows = rows_of(c)
        h = lax.div(c, nch // 2)

        @pl.when(has_chain)
        def _():
            up_copy(c, w).start()

        if w == 0:
            back_copy(rows, h).start()

            @pl.when(lat > 1)
            def _():
                first_cells(rows, 0, h, before2).start()

            lext[:, rows, :] = ubuf[0, :, rows, trace - LB :]
        else:
            first_cells(rows, 1, h, mate).start()

            @pl.when(lat < lats - 1)
            def _():
                last_cells(rows, 1, h, after).start()

        @pl.when(has_leaf)
        def _():
            up_copy(c, w, True).start()

    def down(c, carry):
        rows = rows_of(c)
        for w in (0, 1):

            @pl.when(me == 0)
            def _():
                de[0, w, :, rows, :] = src[w, :, rows, :]

            @pl.when(me > 0)
            def _():
                down_copy(c, w).wait_recv()
                turn(drecv.at[w], de.at[0, w], rows, wd.at[w], src.at[w])

            @pl.when(me < slabs - 1)
            def _():
                down_copy(c, w).start()

            @pl.when(me == slabs - 1)
            def _():
                ubuf[w, :, rows, :] = de[0, w, :, rows, :]
                finish(c, w)

        return carry

    def up(c, carry):
        rows = rows_of(c)
        for w in (0, 1):
            up_copy(c, w).wait_recv()
            turn(urecv.at[w], ubuf.at[w], rows, wz.at[which, w], de.at[which, w])
            finish(c, w)
        return carry

    def give_copy(b):
        rows = pl.ds(pl.multiple_of(b * VP, VP), VP)
        return remote(vland.at[:, rows, :], vland.at[:, rows, :], xs_, xr_, "lat", mate)

    def form(store, done, start, stop):
        def piece(b, carry):
            piece_copy(b).wait_recv()

            def block(k, carry):
                rows = pl.ds(pl.multiple_of(b * VP + k * VR, VR), VR)
                first, second = upan[0, rows, :], upan[1, rows, :]
                for j in range(trace // LB):
                    re, im = product(first, second, wz.at[0, core], j)
                    store(j, rows, re, im)
                return carry

            lax.fori_loop(0, VP // VR, block, 0)
            done(b)
            return carry

        lax.fori_loop(start, stop, piece, 0)

    def store_packed(j, rows, re, im):
        for part_no, value in enumerate((re, im)):
            high, low = split(value)
            wz[1, 1, j, rows, part_no * LB : (part_no + 1) * LB] = high
            wz[1, 1, j, rows, (2 + part_no) * LB : (3 + part_no) * LB] = low

    def store_plain(j, rows, re, im):
        vland[0, rows, j * LB : (j + 1) * LB] = re
        vland[1, rows, j * LB : (j + 1) * LB] = im

    def odd_copy(w):
        return remote(de.at[0, w], erecv.at[w], es_, er_.at[w], "slab", below)

    @pl.when(jnp.logical_and(core == 0, pair))
    def _():
        form(store_plain, lambda b: give_copy(b).start(), 0, trace // VP)

    def late_packs():
        panel_copy(1).wait_recv()
        pack(pan, 3, wz.at[0, 0], trace // LB)
        load_rec.wait()
        pack(rec, None, wr, rec.shape[2] // LB)

    @pl.when(core == 1)
    def _():
        @pl.when(me >= slabs // 2)
        def _():
            late_packs()

        for col in (0, 1):
            source_copy(col).wait_recv()
        early = jnp.where(jnp.logical_and(pair, me >= slabs // 2), trace // VP // 2, 0)

        @pl.when(pair)
        def _():
            form(store_packed, lambda b: None, 0, early)

        lax.fori_loop(0, nch, down, 0)

        @pl.when(leaf)
        def _():
            for w in (1, 0):
                odd_copy(w).start()

        @pl.when(me < slabs // 2)
        def _():
            late_packs()

        @pl.when(pair)
        def _():
            form(store_packed, lambda b: None, early, trace // VP)
            remote(vland, vland, xs_, xr_, "lat", mate).wait_recv()
            pack(vland, None, wz.at[1, 0], trace // LB)
            for w in (1, 0):
                odd_copy(w).wait_recv()

                def two(k, carry):
                    rows = pl.ds(pl.multiple_of(k * VR, VR), VR)
                    turn(erecv.at[w], de.at[1, w], rows, wz.at[0, w], de.at[0, w])
                    return carry

                lax.fori_loop(0, shots // VR, two, 0)

        @pl.when(me < slabs - 1)
        def _():
            lax.fori_loop(0, nch, up, 0)

    load_ff.wait()

    def arrive(h):
        rows = pl.ds(half * h, half)

        @pl.when(core == 0)
        def _():
            back_copy(rows, h).wait_recv()
            first_cells(rows, 1, h, mate).wait_recv()

        @pl.when(jnp.logical_and(core == 0, lat > 0))
        def _():
            last_cells(rows, 1, h, after).wait_recv()

        @pl.when(jnp.logical_and(core == 1, lat < lats - 1))
        def _():
            first_cells(rows, 0, h, before2).wait_recv()

    def place(h, value, first_col):
        width = value.shape[-1]
        for part_no in (0, 1):
            high, low = split(value[part_no])
            xr[h, part_no * half : (part_no + 1) * half, first_col : first_col + width] = high
            xr[h, (2 + part_no) * half : (3 + part_no) * half, first_col : first_col + width] = low

    neb = gbuf.shape[0]

    depth = xr.shape[-1]

    def put_all(h, rim):
        rows = pl.ds(half * h, half)
        if rim:
            place(h, rext[:, rows, :], LB + trace)
        else:
            place(h, ubuf[core, :, rows, :], LB)
            place(h, lext[:, rows, :], 0)

    def recover(h):
        put_all(h, False)
        put_all(h, True)
        rows = pl.ds(half * h, half)

        def block(j, carry):
            cols = pl.ds(pl.multiple_of(j * LB, LB), LB)
            prod = jnp.dot(xr[h], wr[j, :, : 2 * LB], preferred_element_type=F32)
            prod = prod[: 2 * half] + prod[2 * half :]
            prod = prod + jnp.dot(xr[h, : 2 * half, :], wr[j, :, 2 * LB :], preferred_element_type=F32)
            re = prod[:half, :LB] - prod[half:, LB:]
            im = prod[:half, LB:] + prod[half:, :LB]
            row = jnp.sum(ff[0, rows, cols] * re + ff[1, rows, cols] * im, axis=0, keepdims=True)
            if h == 0:
                gbuf[pl.ds(j, 1), :] = row
            else:
                gbuf[pl.ds(j, 1), :] = gbuf[pl.ds(j, 1), :] + row
            return carry

        lax.fori_loop(0, neb, block, 0)

    leave = pltpu.make_async_copy(ubuf.at[core], u_hbm, load_sem.at[6])

    @pl.when(core == 0)
    def _():
        arrive(0)
        recover(0)
        arrive(1)
        leave.start()
        recover(1)

    @pl.when(core == 1)
    def _():
        leave.start()
        for h in (0, 1):
            put_all(h, False)
        for h in (0, 1):
            arrive(h)
            put_all(h, True)

        def block(j, carry):
            cols = pl.ds(pl.multiple_of(j * LB, LB), LB)
            prod = jnp.dot(xr[...].reshape(4 * shots, depth), wr[j], preferred_element_type=F32)
            prod = prod[:, : 2 * LB] + prod[:, 2 * LB :]
            row = jnp.zeros((1, LB), F32)
            for h in (0, 1):
                rows = pl.ds(half * h, half)
                part_sum = prod[2 * shots * h : 2 * shots * h + shots] + prod[2 * shots * h + shots : 2 * shots * (h + 1)]
                re = part_sum[:half, :LB] - part_sum[half:, LB:]
                im = part_sum[:half, LB:] + part_sum[half:, :LB]
                row = row + jnp.sum(ff[0, rows, cols] * re + ff[1, rows, cols] * im, axis=0, keepdims=True)
            gbuf[pl.ds(j, 1), :] = row
            return carry

        lax.fori_loop(0, neb, block, 0)

    grads = gbuf[...] * (shots ** (-0.5))
    lanes = lax.broadcasted_iota(jnp.int32, gsend.shape[1:], 0)
    placed = []
    for b in range(neb):
        row = jnp.broadcast_to(grads[b : b + 1, :], gsend.shape[1:])
        placed.append(jnp.where(lanes == slot_sm[b], row, 0.0))
    for s in range(slabs):
        total = jnp.zeros(gsend.shape[1:], F32)
        for b in range(neb):
            total = total + placed[b] * jnp.where(own_sm[b] == s, 1.0, 0.0).astype(F32)
        gsend[s] = total

    def grad_copy(to, sender):
        return remote(gsend.at[to], grecv.at[sender], gs_, gr_, "slab", to)

    def grad_send(k, carry):
        grad_copy(lax.rem(me + k, slabs), me).start()
        return carry

    lax.fori_loop(1, slabs, grad_send, 0)
    grecv[me] = gsend[me]

    def sent(ref, sem, axis="slab", where=me):
        remote(ref, ref, sem, sem, axis, where).wait_send()

    @pl.when(leaf)
    def _():
        sent(upan, vs_)

    @pl.when(jnp.logical_and(core == 0, pair))
    def _():
        sent(vland, xs_)

    sent(h1, h1s)
    sent(f1, f1s)
    sent(h2, h2s)
    sent(f2, f2s)

    @pl.when(core == 1)
    def _():
        @pl.when(me < slabs - 1)
        def _():
            sent(de.at[0], ds_)

        @pl.when(has_chain)
        def _():
            sent(ubuf, us_)

        @pl.when(has_leaf)
        def _():
            sent(ubuf, ul_)

        @pl.when(leaf)
        def _():
            sent(de.at[0], es_)

        sent(ubuf.at[0], as_)
        sent(rext, rs_)

        @pl.when(lat > 1)
        def _():
            sent(rext, r2s_)

        @pl.when(lat < lats - 1)
        def _():
            sent(lext, ls_)

    @pl.when(core == 0)
    def _():
        for k in (0, 1):
            panel_copy(k).wait_send()
            source_copy(k).wait_send()

    leave.wait()
    all_others = pl.ds(0, slabs - 1)
    remote(gsend.at[all_others], grecv.at[all_others], gs_, gr_, "slab", me).wait_recv()
    total = grecv[0]
    for k in range(1, slabs):
        total = total + grecv[k]
    model_out[...] = total
    sent(gsend.at[all_others], gs_)


def deliver(u_ref, model_ref, u_out, model_out):
    u_out[...] = u_ref[...]
    model_out[...] = model_ref[...]


def body(
    residual_blocks,
    residual_slab,
    residual_pos,
    shot_ids,
    wavelet,
    down_panel,
    up_panel,
    recovery,
    forward_field,
    element_owner,
    element_slot,
):
    slabs = 16
    nres, _, shots, width = residual_blocks.shape
    trace = down_panel.shape[-1]
    depth, nel = recovery.shape[-2:]
    neb = element_slot.shape[0]
    half = shots // 2
    nch = shots // CH
    smem = pl.BlockSpec(memory_space=pltpu.SMEM)
    vmem = pl.BlockSpec(memory_space=pltpu.VMEM)
    hbm = pl.BlockSpec(memory_space=pl.ANY)
    dma = pltpu.SemaphoreType.DMA
    ups, model = pl.pallas_call(
        kernel,
        out_shape=(
            jax.ShapeDtypeStruct((2, shots, trace), F32),
            jax.ShapeDtypeStruct((neb, width), F32),
        ),
        in_specs=[vmem] * 2 + [smem] * 4 + [hbm] * 5,
        out_specs=(hbm, vmem),
        scratch_shapes=[
            pltpu.VMEM((nres, 2, shots, width), F32),
            pltpu.VMEM((4, 2, trace, trace), F32),
            pltpu.VMEM((2, depth, nel), F32),
            pltpu.VMEM((2, shots, nel), F32),
            pltpu.VMEM((2, trace // width, trace, 4 * width), BF16),
            pltpu.VMEM((2, 2, trace // width, trace, 4 * width), BF16),
            pltpu.VMEM((nel // width, depth, 4 * width), BF16),
            pltpu.VMEM((slabs, 2, shots, trace), F32),
            pltpu.VMEM((2, RY, 2, half, trace), F32),
            pltpu.VMEM((2, RY, 2, 2, half, trace), F32),
            pltpu.VMEM((2, 2, half, trace), F32),
            pltpu.VMEM((2, 2, 2, half, trace), F32),
            pltpu.VMEM((2, 2, shots, trace), F32),
            pltpu.VMEM((2, 2, 2, shots, trace), F32),
            pltpu.VMEM((2, 2, shots, trace), F32),
            pltpu.VMEM((2, 2, shots, trace), F32),
            pltpu.VMEM((2, 2, shots, trace), F32),
            pltpu.VMEM((2, shots, width), F32),
            pltpu.VMEM((2, shots, width), F32),
            pltpu.VMEM((2, 2 * shots, depth), BF16),
            pltpu.VMEM((neb, width), F32),
            pltpu.VMEM((slabs, neb, width), F32),
            pltpu.VMEM((slabs, neb, width), F32),
            pltpu.VMEM((slabs, width), jnp.int32),
            pltpu.SMEM((slabs, width), jnp.int32),
            pltpu.VMEM((2, shots, width), F32),
            pltpu.VMEM((2, trace, trace), F32),
            pltpu.VMEM((2, trace, trace), F32),
            pltpu.VMEM((2, 2, shots, trace), F32),
            dma((7,)),
            dma,
            dma((2, RY, 2)),
            dma,
            dma((2, RY, 2)),
            dma,
            dma((2, 2)),
            dma,
            dma((2, 2)),
            dma,
            dma((2, nch)),
            dma,
            dma((2, nch)),
            dma,
            dma((2,)),
            dma,
            dma,
            dma((2,)),
            dma,
            dma((2,)),
            dma,
            dma,
            dma((2,)),
            dma((2,)),
            dma((2,)),
            dma((2,)),
            dma,
            dma,
            dma((trace // VP,)),
            dma,
            dma,
            dma,
            dma((2,)),
        ],
        compiler_params=pltpu.CompilerParams(
            collective_id=0, has_side_effects=True, vmem_limit_bytes=60 * 1024 * 1024
        ),
    )(
        residual_slab.reshape(1, -1),
        residual_pos.reshape(1, -1),
        element_owner.reshape(-1),
        element_slot,
        shot_ids,
        wavelet.T,
        residual_blocks,
        down_panel[0, 0],
        up_panel[0, 0],
        recovery[0, 0],
        forward_field[0, 0],
    )
    ups, model = pl.pallas_call(
        deliver,
        out_shape=(
            jax.ShapeDtypeStruct((2, shots, trace), F32),
            jax.ShapeDtypeStruct((neb, width), F32),
        ),
        in_specs=[vmem, vmem],
        out_specs=(vmem, vmem),
    )(ups, model)
    return (ups[None, None], model[None, None])


def solution(mesh):
    placed = (
        P(("slab", "lat"), None, None, None),
        P(("slab", "lat"), None),
        P(("slab", "lat")),
        P(),
        P(),
        P("slab", "lat", None, None, None),
        P("slab", "lat", None, None, None),
        P("slab", "lat", None, None, None),
        P("slab", "lat", None, None, None),
        P(("slab", "lat"), None),
        P(("slab", "lat")),
    )
    return jax.shard_map(
        body,
        mesh=mesh,
        in_specs=placed,
        out_specs=(P("slab", "lat", None, None, None), P("slab", "lat", None, None)),
        check_vma=False,
    )
```
